256 devices in a mesh: seq: 8 (over x, core), expert: 32 (over z, y).
Axes of the slice: x: 4, y: 4, z: 8, core: 2. Of those that a mesh axis runs over, the one named last changes fastest.
Arguments:
- queries: bfloat16 [2, 2048, 8192], P(None, 'seq', 'expert'), may hold values from -6 to 6
- key_rows: bfloat16 [2, 2048, 8192], P(None, 'seq', 'expert'), may hold values from -6 to 6
- value_rows: bfloat16 [2, 2048, 8192], P(None, 'seq', 'expert'), may hold values from -6 to 6
- decay_rate: float32 [64], P('expert'), as said below
- norm_gain: float32 [8192], P('expert'), may hold values from 0.1 to 1.9
- attn_probe: bfloat16 [2, 2048, 8192], P(None, 'seq', 'expert'), may hold values from -6 to 6
- hidden_in: bfloat16 [2, 2048, 6144], P(None, ('seq', 'expert')), may hold values from -6 to 6
- moe_probe: bfloat16 [2, 2048, 6144], P(None, ('seq', 'expert')), may hold values from -6 to 6
- router_weight: bfloat16 [6144, 4], replicated, may hold values from -0.078125 to 0.078125
- routes: int32 [2, 2048, 2], P(None, ('seq', 'expert')), may hold values from 0 to 3, all different within a row; in each aligned block of 8 rows (0 to 7, 8 to 15, ..., all dimensions but the last counted through in order) at most 5 rows name the same one
- gate_weight: bfloat16 [32, 6144, 576], P('expert', 'seq'), may hold values from -0.078125 to 0.078125
- up_weight: bfloat16 [32, 6144, 576], P('expert', 'seq'), may hold values from -0.078125 to 0.078125
- down_weight: bfloat16 [32, 6144, 576], P('expert', 'seq'), may hold values from -0.09375 to 0.09375
- rollout_logprob: float32 [2, 2048], P(None, 'seq'), may hold values from -1 to 0
- trainer_logprob: float32 [2, 2048], P(None, 'seq'), may hold values from -1 to 0
- advantage: float32 [2, 2048], P(None, 'seq'), may hold values from -4 to 4
- clip_low: float32 [1], replicated, may hold values from 0.4 to 0.95
- clip_high: float32 [1], replicated, may hold values from 1.05 to 2.5
Outputs:
- objective: float32 [2, 2048], P(None, 'seq')
- grad_queries: bfloat16 [2, 2048, 8192], P(None, 'seq', 'expert')
- grad_keys: bfloat16 [2, 2048, 8192], P(None, 'seq', 'expert')
- grad_values: bfloat16 [2, 2048, 8192], P(None, 'seq', 'expert')
- grad_hidden: bfloat16 [2, 2048, 6144], P(None, ('seq', 'expert'))
The draws below stay inside these ranges and needn't reach their ends.
Inputs may be any that keep to these rules, and one draw needn't show every extreme that they name: `routes`: in each rollout, the 8 positions that one device holds in the expert block name no expert more than 5 times; the 2 experts of a token differ. `decay_rate`: positive rates.
All inputs are finite; a program needn't handle non-finite values.
Results may differ from the reference program's by a relative error of at most 0.0045.
The reference program's roundings to bfloat16 on the way count: a program that leaves them out, or rounds other values in their place, can miss the bound.
Values may be sent and summed in bfloat16 or wider, within the bound.
A program may use at most 128 MiB of HBM per device.

```python
import math
import jax
import jax.numpy as jnp
import numpy as np
from jax import lax

D = 6144
HD = 128
TOP = 2
EXP_WIN = 4
FF_WIN = 4608
ROLL = 2
HEADS = 64
LEN = 2048
POS_DEV = 8
MOST = 5
SLICES = 8
FF_DEV = 576
N_SEQ = 8
N_EXPERT = 32


def draw_decay_rate(key, part):
    pick_key, slow_key, fast_key = jax.random.split(key, 3)
    share = 0.5
    slow = jax.random.uniform(pick_key, (HEADS,), jnp.float32) < share
    slow_rate = jnp.exp(jax.random.uniform(slow_key, (HEADS,), jnp.float32, minval=jnp.log(0.1), maxval=0.0)) * (jnp.log(10.0) / LEN)
    fast_rate = jax.random.uniform(fast_key, (HEADS,), jnp.float32, minval=1.0 / 50.0, maxval=1.0 / 30.0)
    return jnp.where(slow, slow_rate, fast_rate).astype(jnp.float32)


def block_levels(key, dims, shards, least, largest):
    factor_of, own = 1.0, jax.random.fold_in(key, 6)
    for dim, shards_of in shards:
        steps = jnp.exp(jax.random.uniform(jax.random.fold_in(own, dim), (shards_of,), jnp.float32, least / len(shards), largest / len(shards)))
        factor_of = factor_of * jnp.repeat(steps, dims[dim] // shards_of).reshape([-1 if axis == dim else 1 for axis in range(len(dims))])
    return factor_of


def shared_out(own_key, own, number, rows, count, top, bound, skew):
    ranking = jax.random.permutation(own_key, count)
    packed, usual = shares(count, rows * top, bound, skew, True), shares(count, rows * top, bound, skew, False)
    places = jnp.arange(count)

    def named(tallies, offset_by):
        used = int((tallies > 0).sum())
        fixed = max(1, used // 4)
        shifted = fixed + (places - fixed + offset_by * (used - fixed)) % max(1, count - fixed)
        return jnp.zeros((count,), jnp.int32).at[ranking[jnp.where(places < fixed, places, shifted)]].set(jnp.asarray(tallies, jnp.int32))

    tallies = jnp.where(number % 4 == 0, named(packed, number // 4), named(usual, number - number // 4 - 1))
    mixed = jax.random.permutation(jax.random.fold_in(own, 3), count)
    giver, receiver = mixed[0:count // 2 * 2:2], mixed[1:count // 2 * 2:2]
    slack = jnp.minimum(tallies[giver] - 1, bound - tallies[receiver]) // 2
    slack = jnp.where((giver == ranking[0]) | (receiver == ranking[0]) | (tallies[receiver] == 0), 0, jnp.maximum(slack, 0))
    shifted = jax.random.randint(jax.random.fold_in(own, 4), (count // 2,), 0, 1 << 20) % (slack + 1)
    tallies = tallies.at[giver].add(-shifted).at[receiver].add(shifted)
    labels = jnp.searchsorted(jnp.cumsum(tallies), jnp.arange(rows * top), side="right").astype(jnp.int32)
    grid = labels.reshape(top, rows).T
    grid = grid[jax.random.permutation(jax.random.fold_in(own, 1), rows)]
    offset_by = jax.random.randint(jax.random.fold_in(own, 2), (rows, 1), 0, top)
    return jnp.take_along_axis(grid, (jnp.arange(top)[None, :] + offset_by) % top, axis=1)


def shares(count, total, bound, skew, full):
    portions = [(1 << 20) // math.isqrt(rank ** skew) + 1 for rank in range(1, count + 1)]
    largest = bound if full else min(bound, max(-(-total // count), total * portions[0] // sum(portions)))
    least = 1 if total - largest >= count - 1 else 0
    counts, rest = [largest] + [least] * (count - 1), total - largest - least * (count - 1)
    while rest > 0:
        movable = [i for i in range(1, count) if counts[i] < largest] or [i for i in range(1, count) if counts[i] < bound]
        pool, remaining = sum([portions[i] for i in movable]), rest
        for i in movable:
            extra = min(bound - counts[i], max(1, remaining * portions[i] // pool), rest)
            counts[i] = counts[i] + extra
            rest = rest - extra
    return np.array(counts)


def bell_draw(stream_key, dims, spread, reach, cuts=(), kind=jnp.bfloat16):
    drawn = jax.random.normal(stream_key, dims, jnp.float32) * spread
    if len(cuts) > 0:
        drawn = block_levels(stream_key, dims, cuts, -0.22, 0.18) * drawn
    return jnp.clip(drawn, min=-reach, max=reach).astype(kind)


def setup_inputs(seed: int = 0) -> dict:
    arg_keys = jax.random.split(jax.random.key(seed), 19)
    queries = bell_draw(arg_keys[0], (ROLL, LEN, HEADS * HD), 1.0, 6.0, ((1, 8), (2, 32)))
    key_rows = bell_draw(arg_keys[1], (ROLL, LEN, HEADS * HD), 1.0, 6.0, ((1, 8), (2, 32)))
    value_rows = bell_draw(arg_keys[2], (ROLL, LEN, HEADS * HD), 1.0, 6.0, ((1, 8), (2, 32)))
    decay_rate = draw_decay_rate(jax.random.fold_in(arg_keys[18], 71), 0)
    norm_gain = jnp.clip(1.0 + 0.18 * jax.random.normal(arg_keys[4], (HEADS * HD,), jnp.float32), 0.1, 1.9)
    attn_probe = bell_draw(arg_keys[5], (ROLL, LEN, HEADS * HD), 1.0, 6.0, ((1, 8), (2, 32)))
    hidden_in = bell_draw(arg_keys[6], (ROLL, LEN, D), 1.0, 6.0, ((1, 256),))
    moe_probe = bell_draw(arg_keys[7], (ROLL, LEN, D), 1.0, 6.0, ((1, 256),))
    router_weight = bell_draw(arg_keys[8], (D, EXP_WIN), D ** -0.5, 0.078125)
    routes_keys = jax.random.split(jax.random.fold_in(arg_keys[9], 1), ROLL * LEN // POS_DEV)
    routes_turns = jax.random.permutation(jax.random.fold_in(arg_keys[9], 3), ROLL * LEN // POS_DEV)
    routes = jax.vmap(lambda own, number: shared_out(jax.random.fold_in(arg_keys[9], 2), own, number, POS_DEV, EXP_WIN, TOP, MOST, 2))(routes_keys, routes_turns).reshape((ROLL, LEN, TOP))
    gate_weight = bell_draw(arg_keys[10], (EXP_WIN * SLICES, D, FF_DEV), D ** -0.5, 0.078125, ((0, 32), (1, 8)))
    up_weight = bell_draw(arg_keys[11], (EXP_WIN * SLICES, D, FF_DEV), D ** -0.5, 0.078125, ((0, 32), (1, 8)))
    down_weight = bell_draw(arg_keys[12], (EXP_WIN * SLICES, D, FF_DEV), FF_WIN ** -0.5, 0.09375, ((0, 32), (1, 8)))
    rollout_logprob = jnp.clip(-1.0 + 1.0 * jax.random.uniform(arg_keys[13], (ROLL, LEN), jnp.float32) ** block_levels(arg_keys[13], (ROLL, LEN), ((1, 8),), -0.2, 0.2), -1.0, 0.0)
    trainer_logprob = jnp.clip(-1.0 + 1.0 * jax.random.uniform(arg_keys[14], (ROLL, LEN), jnp.float32) ** block_levels(arg_keys[14], (ROLL, LEN), ((1, 8),), -0.2, 0.2), -1.0, 0.0)
    advantage = bell_draw(arg_keys[15], (ROLL, LEN), 1.0, 4.0, ((1, 8),), jnp.float32)
    clip_low = jnp.clip(jax.random.uniform(arg_keys[16], (1,), jnp.float32, 0.4, 0.95), 0.4, 0.95)
    clip_high = jnp.clip(jax.random.uniform(arg_keys[17], (1,), jnp.float32, 1.05, 2.5), 1.05, 2.5)
    return {"queries": queries, "key_rows": key_rows, "value_rows": value_rows, "decay_rate": decay_rate, "norm_gain": norm_gain, "attn_probe": attn_probe, "hidden_in": hidden_in, "moe_probe": moe_probe, "router_weight": router_weight, "routes": routes, "gate_weight": gate_weight, "up_weight": up_weight, "down_weight": down_weight, "rollout_logprob": rollout_logprob, "trainer_logprob": trainer_logprob, "advantage": advantage, "clip_low": clip_low, "clip_high": clip_high}


highest = lax.Precision.HIGHEST
norm_epsilon = 1e-06

def attention_grads(queries, key_rows, value_rows, decay_rate, norm_gain, attn_probe, coeff):

    def split_heads(array):
        return jnp.transpose(array.reshape(ROLL, LEN, HEADS, HD).astype(jnp.float32), (2, 0, 1, 3))

    def one_head(inputs):
        query_head, key_head, value_head, probe_head, rate, gain = inputs
        offsets = jnp.arange(LEN, dtype=jnp.float32)
        distance = offsets[:, None] - offsets[None, :]
        mask_decay = jnp.where(distance >= 0, jnp.exp(-rate * jnp.maximum(distance, 0.0)), 0.0)
        scores = jnp.einsum('ric,rjc->rij', query_head, key_head, precision=highest) * mask_decay
        output = jnp.einsum('rij,rjc->ric', scores, value_head, precision=highest)
        inverse = lax.rsqrt(lax.optimization_barrier(jnp.mean(output * output, axis=-1, keepdims=True)) + norm_epsilon)
        scaled = gain * (coeff[:, :, None] * probe_head)
        grad_out = inverse * scaled - output * inverse ** 3 * lax.optimization_barrier(jnp.mean(scaled * output, axis=-1, keepdims=True))
        product = jnp.einsum('ric,rjc->rij', grad_out, value_head, precision=highest) * mask_decay
        grad_query = jnp.einsum('rij,rjc->ric', product, key_head, precision=highest)
        grad_key = jnp.einsum('rij,ric->rjc', product, query_head, precision=highest)
        grad_value = jnp.einsum('rij,ric->rjc', scores, grad_out, precision=highest)
        return (grad_query.astype(jnp.bfloat16), grad_key.astype(jnp.bfloat16), grad_value.astype(jnp.bfloat16))
    gains = norm_gain.reshape(HEADS, HD)
    results = lax.map(one_head, (split_heads(queries), split_heads(key_rows), split_heads(value_rows), split_heads(attn_probe), decay_rate, gains))

    def merge_heads(array):
        return jnp.transpose(array, (1, 2, 0, 3)).reshape(ROLL, LEN, HEADS * HD)
    return (merge_heads(results[0]), merge_heads(results[1]), merge_heads(results[2]))

def expert_terms(token_flat, grad_flat, member, gate_slices, up_slices, down_slices, capacity):
    order = jnp.argsort(jnp.where(member, 0, 1).astype(jnp.int32), stable=True)[:capacity].astype(jnp.int32)
    valid = member[order].astype(jnp.float32)
    tokens_sel = token_flat[order]
    grads_sel = grad_flat[order]
    model_width = token_flat.shape[1]

    def one_slice(index, totals):
        dx_total, score_total = totals
        gate_mat = gate_slices[index]
        up_mat = up_slices[index]
        down_mat = down_slices[index]
        pre_gate = jnp.dot(tokens_sel, gate_mat, preferred_element_type=jnp.float32)
        pre_up = jnp.dot(tokens_sel, up_mat, preferred_element_type=jnp.float32)
        sigmoid_gate = jax.nn.sigmoid(pre_gate)
        activated = pre_gate * sigmoid_gate
        units = activated * pre_up
        unit_grad = jnp.dot(grads_sel, down_mat, preferred_element_type=jnp.float32)
        up_grad = (unit_grad * activated).astype(jnp.bfloat16)
        gate_grad = (unit_grad * pre_up * sigmoid_gate * (1.0 + pre_gate * (1.0 - sigmoid_gate))).astype(jnp.bfloat16)
        slice_dx = jnp.dot(gate_grad, gate_mat.T, preferred_element_type=jnp.float32) + jnp.dot(up_grad, up_mat.T, preferred_element_type=jnp.float32)
        slice_dx = lax.optimization_barrier(slice_dx.astype(jnp.bfloat16)).astype(jnp.float32)
        slice_score = lax.optimization_barrier(lax.optimization_barrier(jnp.sum(units * unit_grad, axis=-1)).astype(jnp.bfloat16)).astype(jnp.float32)
        return (dx_total + slice_dx, score_total + slice_score)
    start = (jnp.zeros((capacity, model_width), jnp.float32), jnp.zeros((capacity,), jnp.float32))
    dx_total, score_total = lax.fori_loop(0, gate_slices.shape[0], one_slice, start)
    full_dx = jnp.zeros(token_flat.shape, jnp.float32).at[order].add(dx_total * valid[:, None])
    full_score = jnp.zeros((token_flat.shape[0],), jnp.float32).at[order].add(score_total * valid)
    return (full_dx, full_score)

def reference(queries, key_rows, value_rows, decay_rate, norm_gain, attn_probe, hidden_in, moe_probe, router_weight, routes, gate_weight, up_weight, down_weight, rollout_logprob, trainer_logprob, advantage, clip_low, clip_high):
    importance = jnp.exp(trainer_logprob - rollout_logprob)
    clipped = jnp.minimum(jnp.maximum(importance, clip_low[0]), clip_high[0])
    coeff = -(clipped * advantage) / ROLL
    objective = coeff * trainer_logprob
    grad_queries, grad_keys, grad_values = attention_grads(queries, key_rows, value_rows, decay_rate, norm_gain, attn_probe, coeff)
    token_count = ROLL * LEN
    token_flat = hidden_in.reshape(token_count, D)
    grad_flat = (coeff[:, :, None] * moe_probe.astype(jnp.float32)).astype(jnp.bfloat16).reshape(token_count, D)
    routes_flat = routes.reshape(token_count, TOP)
    capacity = min(token_count, ROLL * N_SEQ * N_EXPERT * MOST)
    gate_all = gate_weight.reshape(EXP_WIN, SLICES, D, FF_DEV)
    up_all = up_weight.reshape(EXP_WIN, SLICES, D, FF_DEV)
    down_all = down_weight.reshape(EXP_WIN, SLICES, D, FF_DEV)

    def one_expert(inputs):
        expert_id, gate_slices, up_slices, down_slices = inputs
        member = jnp.any(routes_flat == expert_id, axis=-1)
        return expert_terms(token_flat, grad_flat, member, gate_slices, up_slices, down_slices, capacity)
    expert_ids = jnp.arange(EXP_WIN, dtype=jnp.int32)
    expert_dx, expert_score = lax.map(one_expert, (expert_ids, gate_all, up_all, down_all))
    onehot = (routes_flat[:, :, None] == expert_ids[None, None, :]).astype(jnp.float32)
    logits = jnp.dot(token_flat, router_weight, preferred_element_type=jnp.float32)
    chosen = jnp.einsum('nke,ne->nk', onehot, logits, precision=highest)
    exponent = jnp.exp(chosen)
    gates = exponent / lax.optimization_barrier(jnp.sum(exponent, axis=-1, keepdims=True))
    gate_expert = jnp.einsum('nk,nke->ne', gates, onehot, precision=highest)
    score_pick = jnp.einsum('nke,en->nk', onehot, expert_score, precision=highest)
    score_mean = lax.optimization_barrier(jnp.sum(gates * score_pick, axis=-1, keepdims=True))
    logit_grad = gates * (score_pick - score_mean)
    logit_expert = jnp.einsum('nk,nke->ne', logit_grad, onehot, precision=highest)
    grad_hidden = jnp.einsum('ne,end->nd', gate_expert, expert_dx, precision=highest)
    grad_hidden = grad_hidden + jnp.einsum('ne,de->nd', logit_expert, router_weight.astype(jnp.float32), precision=highest)
    grad_hidden = grad_hidden.astype(jnp.bfloat16).reshape(ROLL, LEN, D)
    return (objective, grad_queries, grad_keys, grad_values, grad_hidden)
```

```python
import jax
import jax.numpy as jnp
from jax import lax
from jax.experimental import pallas as pl
from jax.experimental.pallas import tpu as pltpu
from jax.sharding import Mesh, PartitionSpec as P

highest = lax.Precision.HIGHEST
norm_epsilon = 1e-06
MESH = pl.DeviceIdType.MESH
AXES_SEQ = ("x", "c")
AXES_EXPERT = ("z", "y")

D = 6144
W_ROWS = 768
H_MAIN = 512
H_TAIL = 64
N_IN = 1152
N_ALL = 1792
TOK = 16
CAP = 80
HALF = 3072
D_EXT = D + 128


def expert_kernel(
    tok, grd, info, wall, out,
    wbuf, zx, zg, zi, xa, ga, pre, ugr, ggu, dxs, yha, yhb, yfp, yfm, cz, zr, zl, psel,
    ssem, rsem, lsem,
):
    x, c, z, y = (lax.axis_index(a) for a in ("x", "c", "z", "y"))
    xp, xm = (x + 1) % 4, (x + 3) % 4
    yp, ym, y2 = (y + 1) % 4, (y + 3) % 4, (y + 2) % 4
    zp, zm = (z + 1) % 8, (z + 7) % 8
    right = {"x": {"x": xp}, "y": {"y": yp}, "z": {"z": zp}}
    left = {"x": {"x": xm}, "y": {"y": ym}, "z": {"z": zm}}
    sib = {"c": 1 - c}
    me = 2 * x + c
    started = []

    def send(src, dst, dev):
        at = len(started)
        copy = pltpu.make_async_remote_copy(
            src_ref=src, dst_ref=dst, send_sem=ssem.at[at], recv_sem=rsem.at[at],
            device_id=dev, device_id_type=MESH,
        )
        copy.start()
        started.append(copy)
        return copy

    barrier = pltpu.get_barrier_semaphore()
    peers = [right[a] for a in "xyz"] + [left[a] for a in "xyz"] + [sib]
    for peer in peers:
        pl.semaphore_signal(barrier, inc=1, device_id=peer, device_id_type=MESH)
    pl.semaphore_wait(barrier, len(peers))

    half_a, half_b = pl.ds(0, W_ROWS // 2), pl.ds(W_ROWS // 2, W_ROWS // 2)
    wra = send(wall.at[half_a], wbuf.at[me, half_a], right["x"])
    wlb = send(wall.at[half_b], wbuf.at[me, half_b], left["x"])
    zxr = [send(tok, zx.at[z], right["z"])]
    zxl = [send(tok, zx.at[z], left["z"])]
    zir = [send(info, zi.at[z], right["z"])]
    zil = [send(info, zi.at[z], left["z"])]
    wrb = send(wall.at[half_b], wbuf.at[me, half_b], right["x"])
    wla = send(wall.at[half_a], wbuf.at[me, half_a], left["x"])
    ws = [send(wall, wbuf.at[me], sib)]
    own = pltpu.make_async_copy(wall, wbuf.at[me], lsem.at[0])
    own.start()
    zx[z] = tok[...]
    zg[z] = grd[...]
    zi[z] = info[...]
    pre[...] = jnp.zeros_like(pre)
    ugr[...] = jnp.zeros_like(ugr)

    def z_hop(h, buf, rights, lefts):
        rights[h - 1].wait_recv()
        if h < 4:
            at = (z + 8 - h) % 8
            rights.append(send(buf.at[at], buf.at[at], right["z"]))
        if h <= 3:
            lefts[h - 1].wait_recv()
            if h < 3:
                at = (z + h) % 8
                lefts.append(send(buf.at[at], buf.at[at], left["z"]))

    for h in range(1, 5):
        z_hop(h, zx, zxr, zxl)
        z_hop(h, zi, zir, zil)
    zgr = [send(grd, zg.at[z], right["z"])]
    zgl = [send(grd, zg.at[z], left["z"])]

    k = z // 2
    total = zi[0]
    for i in range(1, 8):
        total = total + zi[i]
    kind = lax.broadcasted_iota(jnp.int32, (8, 128), 0)
    slot_row = jnp.sum(jnp.where(kind == k, total, 0.0), axis=0, keepdims=True)
    gate_row = jnp.sum(jnp.where(kind == k + 4, total, 0.0), axis=0, keepdims=True)
    rows = lax.broadcasted_iota(jnp.int32, (CAP, 128), 0).astype(jnp.float32) + 1.0
    hot = (rows == jnp.broadcast_to(slot_row, (CAP, 128))).astype(jnp.float32)
    gate_slot = jnp.sum(hot * jnp.broadcast_to(gate_row, (CAP, 128)), axis=1, keepdims=True)
    psel[...] = hot.astype(jnp.bfloat16)

    def compact(buf, dst):
        @pl.loop(0, D // 512)
        def _(i):
            cols = pl.ds(pl.multiple_of(i * 512, 512), 512)
            block = buf[:, :, cols].reshape(8 * TOK, 512)
            dst[y, :, cols] = jnp.dot(
                psel[...], block, preferred_element_type=jnp.float32
            ).astype(jnp.bfloat16)

    col_a, col_b = pl.ds(0, HALF), pl.ds(HALF, HALF)

    def y_send(buf):
        ra = send(buf.at[y, :, col_a], buf.at[y, :, col_a], right["y"])
        lb = send(buf.at[y, :, col_b], buf.at[y, :, col_b], left["y"])
        rb = send(buf.at[y, :, col_b], buf.at[y, :, col_b], right["y"])
        la = send(buf.at[y, :, col_a], buf.at[y, :, col_a], left["y"])
        return ra, lb, rb, la

    def y_relay(buf, ra, lb):
        ra.wait_recv()
        fa = send(buf.at[ym, :, col_a], buf.at[ym, :, col_a], right["y"])
        lb.wait_recv()
        fb = send(buf.at[yp, :, col_b], buf.at[yp, :, col_b], left["y"])
        return fa, fb

    compact(zx, xa)
    yx = y_send(xa)
    z_hop(1, zg, zgr, zgl)
    s_xm, s_xp, s_x2 = 2 * xm + c, 2 * xp + c, 2 * ((x + 2) % 4) + c
    wra.wait_recv()
    wfa = send(wbuf.at[s_xm, half_a], wbuf.at[s_xm, half_a], right["x"])
    ws.append(send(wbuf.at[s_xm, half_a], wbuf.at[s_xm, half_a], sib))
    wlb.wait_recv()
    wfb = send(wbuf.at[s_xp, half_b], wbuf.at[s_xp, half_b], left["x"])
    ws.append(send(wbuf.at[s_xp, half_b], wbuf.at[s_xp, half_b], sib))
    z_hop(2, zg, zgr, zgl)
    z_hop(3, zg, zgr, zgl)
    yxf = y_relay(xa, yx[0], yx[1])
    z_hop(4, zg, zgr, zgl)
    compact(zg, ga)
    yg = y_send(ga)
    yx[2].wait_recv()
    yx[3].wait_recv()
    wrb.wait_recv()
    ws.append(send(wbuf.at[s_xm, half_b], wbuf.at[s_xm, half_b], sib))
    wla.wait_recv()
    ws.append(send(wbuf.at[s_xp, half_a], wbuf.at[s_xp, half_a], sib))
    yxf[0].wait_recv()
    yxf[1].wait_recv()

    def add_in(shard):
        cols = pl.ds(pl.multiple_of(shard * W_ROWS, W_ROWS), W_ROWS)
        left_op = xa[:, :, cols].reshape(4 * CAP, W_ROWS)
        for at, wide in ((0, 256), (256, 256), (512, 256), (768, 256), (1024, 128)):
            pre[:, at : at + wide] += jnp.dot(
                left_op, wbuf[shard, :, at : at + wide], preferred_element_type=jnp.float32
            )

    def add_out(shard):
        cols = pl.ds(pl.multiple_of(shard * W_ROWS, W_ROWS), W_ROWS)
        left_op = ga[:, :, cols].reshape(4 * CAP, W_ROWS)
        for at, wide in ((0, 256), (256, 256), (512, 128)):
            ugr[:, at : at + wide] += jnp.dot(
                left_op, wbuf[shard, :, N_IN + at : N_IN + at + wide],
                preferred_element_type=jnp.float32,
            )

    own.wait()
    for copy in ws:
        copy.wait_recv()
    ws_done = len(ws)

    @pl.loop(0, 6)
    def _(i):
        add_in((2 * (x + 3) + i) % 8)

    ygf = y_relay(ga, yg[0], yg[1])
    yg[2].wait_recv()
    yg[3].wait_recv()
    ygf[0].wait_recv()
    ygf[1].wait_recv()

    @pl.loop(0, 6)
    def _(i):
        add_out((2 * (x + 3) + i) % 8)

    wfa.wait_recv()
    ws.append(send(wbuf.at[s_x2, half_a], wbuf.at[s_x2, half_a], sib))
    wfb.wait_recv()
    ws.append(send(wbuf.at[s_x2, half_b], wbuf.at[s_x2, half_b], sib))
    add_in(s_x2)
    add_out(s_x2)
    for copy in ws[ws_done:]:
        copy.wait_recv()
    s_x2o = 2 * ((x + 2) % 4) + 1 - c
    add_in(s_x2o)
    add_out(s_x2o)

    lane = lax.broadcasted_iota(jnp.int32, (TOK, 128), 1)

    def grads(gate, up, unit):
        sig = jax.nn.sigmoid(gate)
        act = gate * sig
        up_grad = unit * act
        gate_grad = unit * up * sig * (1.0 + gate * (1.0 - sig))
        score = jnp.sum(act * up * unit, axis=1, keepdims=True)
        return gate_grad, up_grad, score

    @pl.loop(0, 4)
    def _(b):
        @pl.loop(0, CAP // TOK)
        def _(i):
            at = pl.multiple_of(b * CAP + i * TOK, TOK)
            r = pl.ds(at, TOK)
            gg, ug, s1 = grads(pre[r, 0:512], pre[r, 512:1024], ugr[r, 0:512])
            tail = pre[r, 1024:1152]
            ggt, ugt, s2 = grads(tail, pltpu.roll(tail, 64, 1), ugr[r, 512:640])
            ggu[r, 0:512] = gg.astype(jnp.bfloat16)
            ggu[r, 512:1024] = ug.astype(jnp.bfloat16)
            ggu[r, 1024:1152] = (ggt + pltpu.roll(ugt, 64, 1)).astype(jnp.bfloat16)
            score = jnp.where(lane == k, jnp.broadcast_to(s1 + s2, (TOK, 128)), 0.0)
            dxs[b, pl.ds(pl.multiple_of(i * TOK, TOK), TOK), D:D_EXT] = score.astype(jnp.bfloat16)

    def to_dx(shard):
        for at in (0, 256, 512):
            cols = pl.ds(pl.multiple_of(shard * W_ROWS + at, 256), 256)
            part = lax.dot_general(
                ggu[...], wbuf[shard, at : at + 256, 0:N_IN], (((1,), (1,)), ((), ())),
                preferred_element_type=jnp.float32,
            )
            dxs[:, :, cols] = part.astype(jnp.bfloat16).reshape(4, CAP, 256)

    ext_b = pl.ds(HALF, D_EXT - HALF)

    @pl.loop(0, 4)
    def _(i):
        to_dx(i)

    ha = send(dxs.at[y2, :, col_a], yha, right["y"])
    fma = send(dxs.at[ym, :, col_a], yfp.at[:, col_a], left["y"])

    @pl.loop(4, 8)
    def _(i):
        to_dx(i)

    hb = send(dxs.at[y2, :, ext_b], yhb, left["y"])
    fpb = send(dxs.at[yp, :, ext_b], yfm.at[:, ext_b], right["y"])

    def add_rows(dst, add, lo, n):
        @pl.loop(0, n // 128)
        def _(i):
            to = pl.ds(pl.multiple_of(lo + i * 128, 128), 128)
            fr = pl.ds(pl.multiple_of(i * 128, 128), 128)
            dst[:, to] = (
                dst[:, to].astype(jnp.float32) + add[:, fr].astype(jnp.float32)
            ).astype(jnp.bfloat16)

    ha.wait_recv()
    add_rows(dxs.at[yp], yha, 0, HALF)
    fpa = send(dxs.at[yp, :, col_a], yfm.at[:, col_a], right["y"])
    hb.wait_recv()
    add_rows(dxs.at[ym], yhb, HALF, D_EXT - HALF)
    fmb = send(dxs.at[ym, :, ext_b], yfp.at[:, ext_b], left["y"])
    for copy in (fma, fpb, fpa, fmb):
        copy.wait_recv()

    def spread(cols, wide, gated):
        part = dxs[y, :, cols].astype(jnp.float32) + yfp[:, cols].astype(jnp.float32)
        part = part + yfm[:, cols].astype(jnp.float32)
        if gated:
            part = part * gate_slot
        back = lax.dot_general(
            psel[...], part.astype(jnp.bfloat16), (((0,), (0,)), ((), ())),
            preferred_element_type=jnp.float32,
        )
        cz[:, :, cols] = back.astype(jnp.bfloat16).reshape(8, TOK, wide)

    @pl.loop(0, D // 512)
    def _(i):
        spread(pl.ds(pl.multiple_of(i * 512, 512), 512), 512, True)

    spread(pl.ds(D, 128), 128, False)

    parts = (col_a, ext_b)

    def z_first(dst, dev, at):
        return [send(cz.at[at, :, p], dst.at[0, :, p], dev) for p in parts]

    zrc = [z_first(zr, right["z"], (z + 4) % 8)]
    zlc = [z_first(zl, left["z"], (z + 5) % 8)]
    for h in range(1, 4):
        nr, nl = [], []
        for n, p in enumerate(parts):
            at = (z + 4 - h) % 8
            zrc[h - 1][n].wait_recv()
            cz[at, :, p] = (
                cz[at, :, p].astype(jnp.float32) + zr[h - 1, :, p].astype(jnp.float32)
            ).astype(jnp.bfloat16)
            nr.append(send(cz.at[at, :, p], zr.at[h, :, p], right["z"]))
            if h < 3:
                at = (z + 5 + h) % 8
                zlc[h - 1][n].wait_recv()
                cz[at, :, p] = (
                    cz[at, :, p].astype(jnp.float32) + zl[h - 1, :, p].astype(jnp.float32)
                ).astype(jnp.bfloat16)
                nl.append(send(cz.at[at, :, p], zl.at[h, :, p], left["z"]))
        zrc.append(nr)
        zlc.append(nl)
    for n, p in enumerate(parts):
        zlc[2][n].wait_recv()
        zrc[3][n].wait_recv()
        out[:, p] = (
            cz[z, :, p].astype(jnp.float32)
            + zr[3, :, p].astype(jnp.float32)
            + zl[2, :, p].astype(jnp.float32)
        )
    for copy in started:
        copy.wait_send()


def expert_block(tok, grd, info, wall):
    bf16, f32 = jnp.bfloat16, jnp.float32
    vmem = pl.BlockSpec(memory_space=pltpu.VMEM)
    n_copies = 66
    return pl.pallas_call(
        expert_kernel,
        out_shape=jax.ShapeDtypeStruct((TOK, D_EXT), f32),
        in_specs=[vmem, vmem, vmem, pl.BlockSpec(memory_space=pl.ANY)],
        out_specs=vmem,
        scratch_shapes=[
            pltpu.VMEM((8, W_ROWS, N_ALL), bf16),
            pltpu.VMEM((8, TOK, D), bf16),
            pltpu.VMEM((8, TOK, D), bf16),
            pltpu.VMEM((8, 8, 128), f32),
            pltpu.VMEM((4, CAP, D), bf16),
            pltpu.VMEM((4, CAP, D), bf16),
            pltpu.VMEM((4 * CAP, N_IN), f32),
            pltpu.VMEM((4 * CAP, N_ALL - N_IN), f32),
            pltpu.VMEM((4 * CAP, N_IN), bf16),
            pltpu.VMEM((4, CAP, D_EXT), bf16),
            pltpu.VMEM((CAP, HALF), bf16),
            pltpu.VMEM((CAP, D_EXT - HALF), bf16),
            pltpu.VMEM((CAP, D_EXT), bf16),
            pltpu.VMEM((CAP, D_EXT), bf16),
            pltpu.VMEM((8, TOK, D_EXT), bf16),
            pltpu.VMEM((4, TOK, D_EXT), bf16),
            pltpu.VMEM((3, TOK, D_EXT), bf16),
            pltpu.VMEM((CAP, 128), bf16),
            pltpu.SemaphoreType.DMA((n_copies,)),
            pltpu.SemaphoreType.DMA((n_copies,)),
            pltpu.SemaphoreType.DMA((1,)),
        ],
        compiler_params=pltpu.CompilerParams(
            collective_id=0, has_side_effects=True, vmem_limit_bytes=64 * 1024 * 1024 - 65536
        ),
        cost_estimate=pl.CostEstimate(
            flops=12 * 10**9, bytes_accessed=40 * 10**6, transcendentals=200000
        ),
        name="expert_block",
    )(tok, grd, info, wall)


def entering(x, axis, combine, identity, reverse):
    length, here = (8, 2 * lax.axis_index("x") + lax.axis_index("c"))
    everything = jax.tree.map(lambda part: lax.all_gather(part, axis), x)
    start = jax.tree.map(
        lambda part, zero: jnp.broadcast_to(jnp.asarray(zero, part.dtype), part.shape), x, identity
    )

    def lap(k, before):
        at = length - 1 - k if reverse else k
        reached = at > here if reverse else at < here
        new = combine(before, jax.tree.map(lambda part: part[at], everything))
        return jax.tree.map(lambda a, b: jnp.where(reached, a, b), new, before)

    return lax.fori_loop(0, length, lap, start)


def carry_combine(earlier, later):
    return (earlier[0] * later[0], later[0] * earlier[1] + later[1])


def earlier_state(summary, block_decay):
    identity = (jnp.ones_like(block_decay), jnp.zeros_like(summary))
    result = entering((block_decay, summary), AXES_SEQ, carry_combine, identity, False)
    return result[1]


def later_state(summary, block_decay):
    identity = (jnp.ones_like(block_decay), jnp.zeros_like(summary))
    result = entering((block_decay, summary), AXES_SEQ, carry_combine, identity, True)
    return result[1]


def on_device(
    queries,
    key_rows,
    value_rows,
    decay_rate,
    norm_gain,
    attn_probe,
    hidden_in,
    moe_probe,
    router_weight,
    routes,
    gate_weight,
    up_weight,
    down_weight,
    rollout_logprob,
    trainer_logprob,
    advantage,
    clip_low,
    clip_high,
):
    rollouts, block_size, feature_width = queries.shape
    head_count = decay_rate.shape[0]
    head_size = feature_width // head_count
    importance = jnp.exp(trainer_logprob - rollout_logprob)
    clipped = jnp.minimum(jnp.maximum(importance, clip_low[0]), clip_high[0])
    coeff = -(clipped * advantage) / rollouts
    objective = coeff * trainer_logprob
    shape_four = (rollouts, block_size, head_count, head_size)
    query_full = queries.reshape(shape_four).astype(jnp.float32)
    key_full = key_rows.reshape(shape_four).astype(jnp.float32)
    value_full = value_rows.reshape(shape_four).astype(jnp.float32)
    probe_full = attn_probe.reshape(shape_four).astype(jnp.float32)
    gain_full = norm_gain.reshape(head_count, head_size)
    offsets = jnp.arange(block_size, dtype=jnp.float32)
    rate_row = decay_rate[None, :]
    distance = offsets[:, None] - offsets[None, :]
    within = jnp.where(
        (distance >= 0)[None],
        jnp.exp(-decay_rate[:, None, None] * jnp.maximum(distance, 0.0)[None]),
        0.0,
    )
    lead_decay = jnp.exp(-rate_row * (offsets[:, None] + 1.0))[None, :, :, None]
    key_tail = jnp.exp(-rate_row * (block_size - 1.0 - offsets[:, None]))[None, :, :, None]
    query_tail = jnp.exp(-rate_row * offsets[:, None])[None, :, :, None]
    grad_tail = jnp.exp(-rate_row * (block_size - offsets[:, None]))[None, :, :, None]
    block_decay = jnp.exp(-decay_rate * block_size).reshape(1, head_count, 1, 1)
    forward_summary = jnp.einsum(
        "rjhk,rjhv->rhkv", key_full * key_tail, value_full, precision=highest
    )
    state_before = earlier_state(forward_summary, block_decay)
    scores = jnp.einsum("rihc,rjhc->rhij", query_full, key_full, precision=highest) * within[None]
    output = jnp.einsum("rhij,rjhv->rihv", scores, value_full, precision=highest)
    output = output + lead_decay * jnp.einsum(
        "rihk,rhkv->rihv", query_full, state_before, precision=highest
    )
    inverse = lax.rsqrt(jnp.mean(output * output, axis=-1, keepdims=True) + norm_epsilon)
    scaled = gain_full[None, None] * (coeff[:, :, None, None] * probe_full)
    grad_out = inverse * scaled - output * inverse**3 * jnp.mean(
        scaled * output, axis=-1, keepdims=True
    )
    backward_summary = jnp.einsum(
        "rihk,rihv->rhkv", query_full * query_tail, grad_out, precision=highest
    )
    state_after = later_state(backward_summary, block_decay)
    product = jnp.einsum("rihv,rjhv->rhij", grad_out, value_full, precision=highest) * within[None]
    grad_query = jnp.einsum("rhij,rjhk->rihk", product, key_full, precision=highest)
    grad_query = grad_query + lead_decay * jnp.einsum(
        "rihv,rhkv->rihk", grad_out, state_before, precision=highest
    )
    grad_key = jnp.einsum("rhij,rihk->rjhk", product, query_full, precision=highest)
    grad_key = grad_key + grad_tail * jnp.einsum(
        "rjhv,rhkv->rjhk", value_full, state_after, precision=highest
    )
    grad_value = jnp.einsum("rhij,rihv->rjhv", scores, grad_out, precision=highest)
    grad_value = grad_value + grad_tail * jnp.einsum(
        "rjhk,rhkv->rjhv", key_full, state_after, precision=highest
    )
    out_shape = (rollouts, block_size, feature_width)
    grad_queries = grad_query.reshape(out_shape).astype(jnp.bfloat16)
    grad_keys = grad_key.reshape(out_shape).astype(jnp.bfloat16)
    grad_values = grad_value.reshape(out_shape).astype(jnp.bfloat16)
    positions, model_width = hidden_in.shape[1:]
    experts = router_weight.shape[1]
    z_index = lax.axis_index("z")
    local_coeff = lax.dynamic_slice_in_dim(
        coeff, (4 * z_index + lax.axis_index("y")) * positions, positions, 1
    )
    grad_rows = (local_coeff[:, :, None] * moe_probe.astype(jnp.float32)).astype(jnp.bfloat16)
    onehot = (routes[..., None] == jnp.arange(experts, dtype=jnp.int32)).astype(jnp.float32)
    member = onehot.sum(axis=2)
    rank = jnp.cumsum(member, axis=1) - member
    slot = rank + 5.0 * jnp.arange(rollouts, dtype=jnp.float32)[:, None, None]
    slot = jnp.where(member > 0, slot + 1.0 + (10 * z_index).astype(jnp.float32), 0.0)
    logits = jnp.einsum("rpd,de->rpe", hidden_in, router_weight, preferred_element_type=jnp.float32)
    chosen = jnp.einsum("rpke,rpe->rpk", onehot, logits, precision=highest)
    exponent = jnp.exp(chosen)
    gates = exponent / jnp.sum(exponent, axis=-1, keepdims=True)
    gate_expert = jnp.einsum("rpk,rpke->rpe", gates, onehot, precision=highest)
    both = jnp.concatenate([slot, gate_expert], axis=2).reshape(TOK, 2 * experts).T
    info = lax.dynamic_update_slice(
        jnp.zeros((2 * experts, 128), jnp.float32), both, (0, TOK * z_index)
    )
    gate, up, down = gate_weight[0], up_weight[0], down_weight[0]
    wall = jnp.concatenate(
        [
            gate[:, :H_MAIN], up[:, :H_MAIN], gate[:, H_MAIN:], up[:, H_MAIN:],
            down, jnp.zeros((W_ROWS, H_TAIL), jnp.bfloat16),
        ],
        axis=1,
    )
    summed = expert_block(
        hidden_in.reshape(TOK, model_width), grad_rows.reshape(TOK, model_width), info, wall
    )
    row_score = summed[:, model_width : model_width + experts].reshape(rollouts, positions, experts)
    score_pick = jnp.einsum("rpke,rpe->rpk", onehot, row_score, precision=highest)
    score_mean = jnp.sum(gates * score_pick, axis=-1, keepdims=True)
    logit_grad = gates * (score_pick - score_mean)
    logit_expert = jnp.einsum("rpk,rpke->rpe", logit_grad, onehot, precision=highest)
    grad_hidden = summed[:, :model_width].reshape(rollouts, positions, model_width)
    grad_hidden = grad_hidden + jnp.einsum(
        "rpe,de->rpd", logit_expert, router_weight.astype(jnp.float32), precision=highest
    )
    return (objective, grad_queries, grad_keys, grad_values, grad_hidden.astype(jnp.bfloat16))


def solution(mesh):
    grid = Mesh(mesh.devices.reshape(4, 2, 8, 4), ("x", "c", "z", "y"))
    seq, exp = AXES_SEQ, AXES_EXPERT
    rows = P(None, seq, exp)
    toks = P(None, seq + exp, None)
    wts = P(exp, seq, None)
    in_specs = (
        rows, rows, rows, P(exp), P(exp), rows, toks, toks, P(), toks, wts, wts, wts,
        P(None, seq), P(None, seq), P(None, seq), P(), P(),
    )
    out_specs = (P(None, seq), rows, rows, rows, toks)
    return jax.shard_map(
        on_device, mesh=grid, in_specs=in_specs, out_specs=out_specs, check_vma=False
    )
```

```python
import jax
import jax.numpy as jnp
from jax import lax
from jax.experimental import pallas as pl
from jax.experimental.pallas import tpu as pltpu
from jax.sharding import Mesh, PartitionSpec as P

highest = lax.Precision.HIGHEST
norm_epsilon = 1e-06
MESH = pl.DeviceIdType.MESH
AXES_SEQ = ("x", "c")
AXES_EXPERT = ("z", "y")

D = 6144
W_ROWS = 768
H_MAIN = 512
H_TAIL = 64
N_IN = 1152
N_ALL = 1792
TOK = 16
CAP = 80
HALF = 3072
BLOCK, HEAD = 256, 128
D_EXT = D + 128


def kernel(
    tok, grd, info, wall, qr, kr, vr, pr, rate, gain, coef,
    out, gq, gk, gv,
    wbuf, zx, zg, zi, xa, ga, pre, ugr, ggu, dxs, yha, yhb, yfp, yfm, cz, zr, zl, psel,
    f_own, f_sib, f_chip, b_own, b_sib, b_chip, f_far, b_far, state, dk_part, dv_part,
    ssem, rsem, lsem, xss, xrs,
):
    x, c, z, y = (lax.axis_index(a) for a in ("x", "c", "z", "y"))
    xp, xm = (x + 1) % 4, (x + 3) % 4
    yp, ym, y2 = (y + 1) % 4, (y + 3) % 4, (y + 2) % 4
    zp, zm = (z + 1) % 8, (z + 7) % 8
    right = {"x": {"x": xp}, "y": {"y": yp}, "z": {"z": zp}}
    left = {"x": {"x": xm}, "y": {"y": ym}, "z": {"z": zm}}
    sib = {"c": 1 - c}
    me = 2 * x + c
    started = []

    def send(src, dst, dev):
        at = len(started)
        copy = pltpu.make_async_remote_copy(
            src_ref=src, dst_ref=dst, send_sem=ssem.at[at], recv_sem=rsem.at[at],
            device_id=dev, device_id_type=MESH,
        )
        copy.start()
        started.append(copy)
        return copy

    barrier = pltpu.get_barrier_semaphore()
    peers = [right[a] for a in "xyz"] + [left[a] for a in "xyz"] + [sib]
    peers += [{"x": xp, "c": 1 - c}, {"x": xm, "c": 1 - c}, {"x": (x + 2) % 4}]
    peers += [{"x": (x + 2) % 4, "c": 1 - c}]
    for peer in peers:
        pl.semaphore_signal(barrier, inc=1, device_id=peer, device_id_type=MESH)
    pl.semaphore_wait(barrier, len(peers))

    half_a, half_b = pl.ds(0, W_ROWS // 2), pl.ds(W_ROWS // 2, W_ROWS // 2)
    wra = send(wall.at[half_a], wbuf.at[me, half_a], right["x"])
    wlb = send(wall.at[half_b], wbuf.at[me, half_b], left["x"])
    zxr = [send(tok, zx.at[z], right["z"])]
    zxl = [send(tok, zx.at[z], left["z"])]
    zir = [send(info, zi.at[z], right["z"])]
    zil = [send(info, zi.at[z], left["z"])]
    wrb = send(wall.at[half_b], wbuf.at[me, half_b], right["x"])
    wla = send(wall.at[half_a], wbuf.at[me, half_a], left["x"])
    ws = [send(wall, wbuf.at[me], sib)]
    own = pltpu.make_async_copy(wall, wbuf.at[me], lsem.at[0])
    own.start()
    zx[z] = tok[...]
    zg[z] = grd[...]
    zi[z] = info[...]
    pre[...] = jnp.zeros_like(pre)
    ugr[...] = jnp.zeros_like(ugr)

    f32, bf16 = jnp.float32, jnp.bfloat16
    nn, nt, tn = (((1,), (0,)), ((), ())), (((1,), (1,)), ((), ())), (((0,), (0,)), ((), ()))

    def mm(a, b, dims):
        return lax.dot_general(a, b, dims, preferred_element_type=f32)

    def parts_of(v):
        high = v.astype(bf16)
        return high, (v - high.astype(f32)).astype(bf16)

    def row_decay(h, sign, shift):
        row = lax.broadcasted_iota(jnp.int32, (BLOCK, HEAD), 0).astype(f32)
        return jnp.exp(-rate[h] * (sign * row + shift))

    def lanes(h):
        return pl.ds(pl.multiple_of(h * HEAD, HEAD), HEAD)

    def block_decay(h, blocks):
        return jnp.exp(jnp.full((HEAD, HEAD), -rate[h] * (BLOCK * blocks), f32))

    def summaries():
        @pl.loop(0, 4)
        def _(i):
            r, h = i // 2, i % 2
            v_high, v_low = parts_of(vr[r, :, lanes(h)].astype(f32) * row_decay(h, -1.0, BLOCK - 1.0))
            key = kr[r, :, lanes(h)]
            f_own[r, h] = mm(key, v_high, tn) + mm(key, v_low, tn)

    def chip_state(own_ref, sib_ref, chip_ref, near_is_own):
        for h in range(2):
            mine, other = own_ref[c, h], sib_ref[c, h]
            near = jnp.where(near_is_own, mine, other)
            far = jnp.where(near_is_own, other, mine)
            chip_ref[h] = near + block_decay(h, 1) * far

    def far_copy(chip_ref, far_ref, base, dx, cc, to):
        return pltpu.make_async_remote_copy(
            src_ref=chip_ref, dst_ref=far_ref.at[dx - 1, c],
            send_sem=xss.at[base + 2 * (dx - 1) + cc], recv_sem=xrs.at[base + 2 * (dx - 1) + c],
            device_id={"x": to, "c": cc}, device_id_type=MESH,
        )

    def far_send(chip_ref, far_ref, base, step, finish=False):
        for dx in (1, 2, 3):
            to = x + step * dx

            @pl.when(jnp.logical_and(to >= 0, to < 4))
            def _():
                for cc in (0, 1):
                    copy = far_copy(chip_ref, far_ref, base, dx, cc, to)
                    if finish:
                        copy.wait_send()
                    else:
                        copy.start()

    def far_state(chip_ref, far_ref, sib_ref, base, step, with_sib):
        for dx in (1, 2, 3):
            at = x - step * dx
            there = jnp.logical_and(at >= 0, at < 4)

            @pl.when(there)
            def _():
                for r in (0, 1):
                    pltpu.make_async_remote_copy(
                        src_ref=chip_ref, dst_ref=far_ref.at[dx - 1, r],
                        send_sem=xss.at[base + 2 * (dx - 1) + r],
                        recv_sem=xrs.at[base + 2 * (dx - 1) + r],
                        device_id={"x": (x + 1) % 4, "c": r}, device_id_type=MESH,
                    ).wait_recv()

            @pl.when(jnp.logical_not(there))
            def _():
                far_ref[dx - 1] = jnp.zeros_like(far_ref[dx - 1])

        for r in range(2):
            for h in range(2):
                two = block_decay(h, 2)
                far = far_ref[0, r, h] + two * (far_ref[1, r, h] + two * far_ref[2, r, h])
                near = sib_ref[r, h] + block_decay(h, 1) * far
                state[r, h] = jnp.where(with_sib, near, far)

    def attention_main():
        @pl.loop(0, 4)
        def _(i):
            r, h = i // 2, i % 2
            query, key, value = qr[r, :, lanes(h)], kr[r, :, lanes(h)], vr[r, :, lanes(h)]
            at_i = lax.broadcasted_iota(jnp.int32, (BLOCK, BLOCK), 0)
            at_j = lax.broadcasted_iota(jnp.int32, (BLOCK, BLOCK), 1)
            apart = jnp.maximum(at_i - at_j, 0).astype(f32)
            within = jnp.where(at_i >= at_j, jnp.exp(-rate[h] * apart), 0.0)
            s_high, s_low = parts_of(mm(query, key, nt) * within)
            t_high, t_low = parts_of(state[r, h])
            lead = row_decay(h, 1.0, 1.0)
            attn = mm(s_high, value, nn) + mm(s_low, value, nn)
            attn = attn + lead * (mm(query, t_high, nn) + mm(query, t_low, nn))
            inverse = lax.rsqrt(jnp.mean(attn * attn, axis=1, keepdims=True) + norm_epsilon)
            scaled = gain[:, lanes(h)] * (coef[r] * pr[r, :, lanes(h)].astype(f32))
            along = jnp.mean(scaled * attn, axis=1, keepdims=True)
            grad = inverse * scaled - attn * (inverse * inverse * inverse * along)
            g_high, g_low = parts_of(grad)
            d_high, d_low = parts_of(grad * row_decay(h, 1.0, 0.0))
            b_own[r, h] = mm(query, d_high, tn) + mm(query, d_low, tn)
            p_high, p_low = parts_of((mm(g_high, value, nt) + mm(g_low, value, nt)) * within)
            dq = mm(p_high, key, nn) + mm(p_low, key, nn)
            dq = dq + lead * (mm(g_high, t_high, nt) + mm(g_low, t_high, nt) + mm(g_high, t_low, nt))
            gq[r, :, lanes(h)] = dq.astype(bf16)
            dk_part[r, :, lanes(h)] = mm(p_high, query, tn) + mm(p_low, query, tn)
            dv_part[r, :, lanes(h)] = (
                mm(s_high, g_high, tn) + mm(s_low, g_high, tn) + mm(s_high, g_low, tn)
            )

    def attention_last():
        @pl.loop(0, 4)
        def _(i):
            r, h = i // 2, i % 2
            key, value = kr[r, :, lanes(h)], vr[r, :, lanes(h)]
            t_high, t_low = parts_of(state[r, h])
            tail = row_decay(h, -1.0, float(BLOCK))
            dk = dk_part[r, :, lanes(h)] + tail * (mm(value, t_high, nt) + mm(value, t_low, nt))
            dv = dv_part[r, :, lanes(h)] + tail * (mm(key, t_high, nn) + mm(key, t_low, nn))
            gk[r, :, lanes(h)] = dk.astype(bf16)
            gv[r, :, lanes(h)] = dv.astype(bf16)

    summaries()
    fs = send(f_own, f_sib, sib)

    def z_hop(h, buf, rights, lefts):
        rights[h - 1].wait_recv()
        if h < 4:
            at = (z + 8 - h) % 8
            rights.append(send(buf.at[at], buf.at[at], right["z"]))
        if h <= 3:
            lefts[h - 1].wait_recv()
            if h < 3:
                at = (z + h) % 8
                lefts.append(send(buf.at[at], buf.at[at], left["z"]))

    for h in range(1, 5):
        z_hop(h, zx, zxr, zxl)
        z_hop(h, zi, zir, zil)
    zgr = [send(grd, zg.at[z], right["z"])]
    zgl = [send(grd, zg.at[z], left["z"])]

    k = z // 2
    total = zi[0]
    for i in range(1, 8):
        total = total + zi[i]
    kind = lax.broadcasted_iota(jnp.int32, (8, 128), 0)
    slot_row = jnp.sum(jnp.where(kind == k, total, 0.0), axis=0, keepdims=True)
    gate_row = jnp.sum(jnp.where(kind == k + 4, total, 0.0), axis=0, keepdims=True)
    rows = lax.broadcasted_iota(jnp.int32, (CAP, 128), 0).astype(jnp.float32) + 1.0
    hot = (rows == jnp.broadcast_to(slot_row, (CAP, 128))).astype(jnp.float32)
    gate_slot = jnp.sum(hot * jnp.broadcast_to(gate_row, (CAP, 128)), axis=1, keepdims=True)
    psel[...] = hot.astype(jnp.bfloat16)

    def compact(buf, dst):
        @pl.loop(0, D // 512)
        def _(i):
            cols = pl.ds(pl.multiple_of(i * 512, 512), 512)
            block = buf[:, :, cols].reshape(8 * TOK, 512)
            dst[y, :, cols] = jnp.dot(
                psel[...], block, preferred_element_type=jnp.float32
            ).astype(jnp.bfloat16)

    col_a, col_b = pl.ds(0, HALF), pl.ds(HALF, HALF)

    def y_send(buf):
        ra = send(buf.at[y, :, col_a], buf.at[y, :, col_a], right["y"])
        lb = send(buf.at[y, :, col_b], buf.at[y, :, col_b], left["y"])
        rb = send(buf.at[y, :, col_b], buf.at[y, :, col_b], right["y"])
        la = send(buf.at[y, :, col_a], buf.at[y, :, col_a], left["y"])
        return ra, lb, rb, la

    def y_relay(buf, ra, lb):
        ra.wait_recv()
        fa = send(buf.at[ym, :, col_a], buf.at[ym, :, col_a], right["y"])
        lb.wait_recv()
        fb = send(buf.at[yp, :, col_b], buf.at[yp, :, col_b], left["y"])
        return fa, fb

    compact(zx, xa)
    yx = y_send(xa)
    z_hop(1, zg, zgr, zgl)
    s_xm, s_xp, s_x2 = 2 * xm + c, 2 * xp + c, 2 * ((x + 2) % 4) + c
    wra.wait_recv()
    wfa = send(wbuf.at[s_xm, half_a], wbuf.at[s_xm, half_a], right["x"])
    ws.append(send(wbuf.at[s_xm, half_a], wbuf.at[s_xm, half_a], sib))
    wlb.wait_recv()
    wfb = send(wbuf.at[s_xp, half_b], wbuf.at[s_xp, half_b], left["x"])
    ws.append(send(wbuf.at[s_xp, half_b], wbuf.at[s_xp, half_b], sib))
    fs.wait_recv()
    chip_state(f_own, f_sib, f_chip, c == 1)
    far_send(f_chip, f_far, 0, 1)
    z_hop(2, zg, zgr, zgl)
    z_hop(3, zg, zgr, zgl)
    yxf = y_relay(xa, yx[0], yx[1])
    z_hop(4, zg, zgr, zgl)
    compact(zg, ga)
    yg = y_send(ga)
    yx[2].wait_recv()
    yx[3].wait_recv()
    wrb.wait_recv()
    ws.append(send(wbuf.at[s_xm, half_b], wbuf.at[s_xm, half_b], sib))
    wla.wait_recv()
    ws.append(send(wbuf.at[s_xp, half_a], wbuf.at[s_xp, half_a], sib))
    yxf[0].wait_recv()
    yxf[1].wait_recv()

    def add_in(shard):
        cols = pl.ds(pl.multiple_of(shard * W_ROWS, W_ROWS), W_ROWS)
        left_op = xa[:, :, cols].reshape(4 * CAP, W_ROWS)
        for at, wide in ((0, 256), (256, 256), (512, 256), (768, 256), (1024, 128)):
            pre[:, at : at + wide] += jnp.dot(
                left_op, wbuf[shard, :, at : at + wide], preferred_element_type=jnp.float32
            )

    def add_out(shard):
        cols = pl.ds(pl.multiple_of(shard * W_ROWS, W_ROWS), W_ROWS)
        left_op = ga[:, :, cols].reshape(4 * CAP, W_ROWS)
        for at, wide in ((0, 256), (256, 256), (512, 128)):
            ugr[:, at : at + wide] += jnp.dot(
                left_op, wbuf[shard, :, N_IN + at : N_IN + at + wide],
                preferred_element_type=jnp.float32,
            )

    own.wait()
    for copy in ws:
        copy.wait_recv()
    ws_done = len(ws)

    @pl.loop(0, 6)
    def _(i):
        add_in((2 * (x + 3) + i) % 8)

    ygf = y_relay(ga, yg[0], yg[1])
    yg[2].wait_recv()
    yg[3].wait_recv()
    ygf[0].wait_recv()
    ygf[1].wait_recv()

    @pl.loop(0, 6)
    def _(i):
        add_out((2 * (x + 3) + i) % 8)

    wfa.wait_recv()
    ws.append(send(wbuf.at[s_x2, half_a], wbuf.at[s_x2, half_a], sib))
    wfb.wait_recv()
    ws.append(send(wbuf.at[s_x2, half_b], wbuf.at[s_x2, half_b], sib))
    add_in(s_x2)
    add_out(s_x2)
    for copy in ws[ws_done:]:
        copy.wait_recv()
    s_x2o = 2 * ((x + 2) % 4) + 1 - c
    add_in(s_x2o)
    add_out(s_x2o)

    lane = lax.broadcasted_iota(jnp.int32, (TOK, 128), 1)

    def grads(gate, up, unit):
        sig = jax.nn.sigmoid(gate)
        act = gate * sig
        up_grad = unit * act
        gate_grad = unit * up * sig * (1.0 + gate * (1.0 - sig))
        score = jnp.sum(act * up * unit, axis=1, keepdims=True)
        return gate_grad, up_grad, score

    @pl.loop(0, 4)
    def _(b):
        @pl.loop(0, CAP // TOK)
        def _(i):
            at = pl.multiple_of(b * CAP + i * TOK, TOK)
            r = pl.ds(at, TOK)
            gg, ug, s1 = grads(pre[r, 0:512], pre[r, 512:1024], ugr[r, 0:512])
            tail = pre[r, 1024:1152]
            ggt, ugt, s2 = grads(tail, pltpu.roll(tail, 64, 1), ugr[r, 512:640])
            ggu[r, 0:512] = gg.astype(jnp.bfloat16)
            ggu[r, 512:1024] = ug.astype(jnp.bfloat16)
            ggu[r, 1024:1152] = (ggt + pltpu.roll(ugt, 64, 1)).astype(jnp.bfloat16)
            score = jnp.where(lane == k, jnp.broadcast_to(s1 + s2, (TOK, 128)), 0.0)
            dxs[b, pl.ds(pl.multiple_of(i * TOK, TOK), TOK), D:D_EXT] = score.astype(jnp.bfloat16)

    def to_dx(shard):
        for at in (0, 256, 512):
            cols = pl.ds(pl.multiple_of(shard * W_ROWS + at, 256), 256)
            part = lax.dot_general(
                ggu[...], wbuf[shard, at : at + 256, 0:N_IN], (((1,), (1,)), ((), ())),
                preferred_element_type=jnp.float32,
            )
            dxs[:, :, cols] = part.astype(jnp.bfloat16).reshape(4, CAP, 256)

    ext_b = pl.ds(HALF, D_EXT - HALF)

    @pl.loop(0, 4)
    def _(i):
        to_dx(i)

    ha = send(dxs.at[y2, :, col_a], yha, right["y"])
    fma = send(dxs.at[ym, :, col_a], yfp.at[:, col_a], left["y"])

    @pl.loop(4, 8)
    def _(i):
        to_dx(i)

    hb = send(dxs.at[y2, :, ext_b], yhb, left["y"])
    fpb = send(dxs.at[yp, :, ext_b], yfm.at[:, ext_b], right["y"])

    def add_rows(dst, add, lo, n):
        @pl.loop(0, n // 128)
        def _(i):
            to = pl.ds(pl.multiple_of(lo + i * 128, 128), 128)
            fr = pl.ds(pl.multiple_of(i * 128, 128), 128)
            dst[:, to] = (
                dst[:, to].astype(jnp.float32) + add[:, fr].astype(jnp.float32)
            ).astype(jnp.bfloat16)

    ha.wait_recv()
    add_rows(dxs.at[yp], yha, 0, HALF)
    fpa = send(dxs.at[yp, :, col_a], yfm.at[:, col_a], right["y"])
    hb.wait_recv()
    add_rows(dxs.at[ym], yhb, HALF, D_EXT - HALF)
    fmb = send(dxs.at[ym, :, ext_b], yfp.at[:, ext_b], left["y"])
    far_state(f_chip, f_far, f_sib, 0, 1, c == 1)
    attention_main()
    bs = send(b_own, b_sib, sib)
    bs.wait_recv()
    chip_state(b_own, b_sib, b_chip, c == 0)
    far_send(b_chip, b_far, 6, -1)
    for copy in (fma, fpb, fpa, fmb):
        copy.wait_recv()

    def spread(cols, wide, gated):
        part = dxs[y, :, cols].astype(jnp.float32) + yfp[:, cols].astype(jnp.float32)
        part = part + yfm[:, cols].astype(jnp.float32)
        if gated:
            part = part * gate_slot
        back = lax.dot_general(
            psel[...], part.astype(jnp.bfloat16), (((0,), (0,)), ((), ())),
            preferred_element_type=jnp.float32,
        )
        cz[:, :, cols] = back.astype(jnp.bfloat16).reshape(8, TOK, wide)

    @pl.loop(0, D // 512)
    def _(i):
        spread(pl.ds(pl.multiple_of(i * 512, 512), 512), 512, True)

    spread(pl.ds(D, 128), 128, False)

    parts = (col_a, ext_b)

    def z_first(dst, dev, at):
        return [send(cz.at[at, :, p], dst.at[0, :, p], dev) for p in parts]

    zrc = [z_first(zr, right["z"], (z + 4) % 8)]
    zlc = [z_first(zl, left["z"], (z + 5) % 8)]
    far_state(b_chip, b_far, b_sib, 6, -1, c == 0)
    attention_last()
    for h in range(1, 4):
        nr, nl = [], []
        for n, p in enumerate(parts):
            at = (z + 4 - h) % 8
            zrc[h - 1][n].wait_recv()
            cz[at, :, p] = (
                cz[at, :, p].astype(jnp.float32) + zr[h - 1, :, p].astype(jnp.float32)
            ).astype(jnp.bfloat16)
            nr.append(send(cz.at[at, :, p], zr.at[h, :, p], right["z"]))
            if h < 3:
                at = (z + 5 + h) % 8
                zlc[h - 1][n].wait_recv()
                cz[at, :, p] = (
                    cz[at, :, p].astype(jnp.float32) + zl[h - 1, :, p].astype(jnp.float32)
                ).astype(jnp.bfloat16)
                nl.append(send(cz.at[at, :, p], zl.at[h, :, p], left["z"]))
        zrc.append(nr)
        zlc.append(nl)
    for n, p in enumerate(parts):
        zlc[2][n].wait_recv()
        zrc[3][n].wait_recv()
        out[:, p] = (
            cz[z, :, p].astype(jnp.float32)
            + zr[3, :, p].astype(jnp.float32)
            + zl[2, :, p].astype(jnp.float32)
        )
    for copy in started:
        copy.wait_send()
    far_send(f_chip, f_far, 0, 1, finish=True)
    far_send(b_chip, b_far, 6, -1, finish=True)


def all_blocks(tok, grd, info, wall, q, k, v, probe, rate, gain, coef):
    bf16, f32 = jnp.bfloat16, jnp.float32
    vmem = pl.BlockSpec(memory_space=pltpu.VMEM)
    n_copies = 68
    grads = jax.ShapeDtypeStruct((2, BLOCK, 2 * HEAD), bf16)
    states = pltpu.VMEM((2, 2, HEAD, HEAD), f32)
    return pl.pallas_call(
        kernel,
        out_shape=[jax.ShapeDtypeStruct((TOK, D_EXT), f32), grads, grads, grads],
        in_specs=[vmem, vmem, vmem, pl.BlockSpec(memory_space=pl.ANY)]
        + [vmem] * 4
        + [pl.BlockSpec(memory_space=pltpu.SMEM), vmem, vmem],
        out_specs=[vmem] * 4,
        scratch_shapes=[
            pltpu.VMEM((8, W_ROWS, N_ALL), bf16),
            pltpu.VMEM((8, TOK, D), bf16),
            pltpu.VMEM((8, TOK, D), bf16),
            pltpu.VMEM((8, 8, 128), f32),
            pltpu.VMEM((4, CAP, D), bf16),
            pltpu.VMEM((4, CAP, D), bf16),
            pltpu.VMEM((4 * CAP, N_IN), f32),
            pltpu.VMEM((4 * CAP, N_ALL - N_IN), f32),
            pltpu.VMEM((4 * CAP, N_IN), bf16),
            pltpu.VMEM((4, CAP, D_EXT), bf16),
            pltpu.VMEM((CAP, HALF), bf16),
            pltpu.VMEM((CAP, D_EXT - HALF), bf16),
            pltpu.VMEM((CAP, D_EXT), bf16),
            pltpu.VMEM((CAP, D_EXT), bf16),
            pltpu.VMEM((8, TOK, D_EXT), bf16),
            pltpu.VMEM((4, TOK, D_EXT), bf16),
            pltpu.VMEM((3, TOK, D_EXT), bf16),
            pltpu.VMEM((CAP, 128), bf16),
            states, states, pltpu.VMEM((2, HEAD, HEAD), f32),
            states, states, pltpu.VMEM((2, HEAD, HEAD), f32),
            pltpu.VMEM((3, 2, 2, HEAD, HEAD), f32),
            pltpu.VMEM((3, 2, 2, HEAD, HEAD), f32),
            states,
            pltpu.VMEM((2, BLOCK, 2 * HEAD), f32),
            pltpu.VMEM((2, BLOCK, 2 * HEAD), f32),
            pltpu.SemaphoreType.DMA((n_copies,)),
            pltpu.SemaphoreType.DMA((n_copies,)),
            pltpu.SemaphoreType.DMA((1,)),
            pltpu.SemaphoreType.DMA((12,)),
            pltpu.SemaphoreType.DMA((12,)),
        ],
        compiler_params=pltpu.CompilerParams(
            collective_id=0, has_side_effects=True, vmem_limit_bytes=64 * 1024 * 1024 - 65536
        ),
        cost_estimate=pl.CostEstimate(
            flops=12 * 10**9, bytes_accessed=40 * 10**6, transcendentals=200000
        ),
        name="all_blocks",
    )(tok, grd, info, wall, q, k, v, probe, rate, gain, coef)


def on_device(
    queries,
    key_rows,
    value_rows,
    decay_rate,
    norm_gain,
    attn_probe,
    hidden_in,
    moe_probe,
    router_weight,
    routes,
    gate_weight,
    up_weight,
    down_weight,
    rollout_logprob,
    trainer_logprob,
    advantage,
    clip_low,
    clip_high,
):
    rollouts, block_size, feature_width = queries.shape
    importance = jnp.exp(trainer_logprob - rollout_logprob)
    clipped = jnp.minimum(jnp.maximum(importance, clip_low[0]), clip_high[0])
    coeff = -(clipped * advantage) / rollouts
    objective = coeff * trainer_logprob
    positions, model_width = hidden_in.shape[1:]
    experts = router_weight.shape[1]
    z_index = lax.axis_index("z")
    local_coeff = lax.dynamic_slice_in_dim(
        coeff, (4 * z_index + lax.axis_index("y")) * positions, positions, 1
    )
    grad_rows = (local_coeff[:, :, None] * moe_probe.astype(jnp.float32)).astype(jnp.bfloat16)
    onehot = (routes[..., None] == jnp.arange(experts, dtype=jnp.int32)).astype(jnp.float32)
    member = onehot.sum(axis=2)
    rank = jnp.cumsum(member, axis=1) - member
    slot = rank + 5.0 * jnp.arange(rollouts, dtype=jnp.float32)[:, None, None]
    slot = jnp.where(member > 0, slot + 1.0 + (10 * z_index).astype(jnp.float32), 0.0)
    logits = jnp.einsum("rpd,de->rpe", hidden_in, router_weight, preferred_element_type=jnp.float32)
    chosen = jnp.einsum("rpke,rpe->rpk", onehot, logits, precision=highest)
    exponent = jnp.exp(chosen)
    gates = exponent / jnp.sum(exponent, axis=-1, keepdims=True)
    gate_expert = jnp.einsum("rpk,rpke->rpe", gates, onehot, precision=highest)
    both = jnp.concatenate([slot, gate_expert], axis=2).reshape(TOK, 2 * experts).T
    info = lax.dynamic_update_slice(
        jnp.zeros((2 * experts, 128), jnp.float32), both, (0, TOK * z_index)
    )
    gate, up, down = gate_weight[0], up_weight[0], down_weight[0]
    wall = jnp.concatenate(
        [
            gate[:, :H_MAIN], up[:, :H_MAIN], gate[:, H_MAIN:], up[:, H_MAIN:],
            down, jnp.zeros((W_ROWS, H_TAIL), jnp.bfloat16),
        ],
        axis=1,
    )
    coef = jnp.broadcast_to(coeff[:, :, None], (rollouts, block_size, HEAD))
    summed, grad_queries, grad_keys, grad_values = all_blocks(
        hidden_in.reshape(TOK, model_width), grad_rows.reshape(TOK, model_width), info, wall,
        queries, key_rows, value_rows, attn_probe, decay_rate, norm_gain.reshape(1, feature_width),
        coef,
    )
    row_score = summed[:, model_width : model_width + experts].reshape(rollouts, positions, experts)
    score_pick = jnp.einsum("rpke,rpe->rpk", onehot, row_score, precision=highest)
    score_mean = jnp.sum(gates * score_pick, axis=-1, keepdims=True)
    logit_grad = gates * (score_pick - score_mean)
    logit_expert = jnp.einsum("rpk,rpke->rpe", logit_grad, onehot, precision=highest)
    grad_hidden = summed[:, :model_width].reshape(rollouts, positions, model_width)
    grad_hidden = grad_hidden + jnp.einsum(
        "rpe,de->rpd", logit_expert, router_weight.astype(jnp.float32), precision=highest
    )
    return (objective, grad_queries, grad_keys, grad_values, grad_hidden.astype(jnp.bfloat16))


def solution(mesh):
    grid = Mesh(mesh.devices.reshape(4, 2, 8, 4), ("x", "c", "z", "y"))
    seq, exp = AXES_SEQ, AXES_EXPERT
    rows = P(None, seq, exp)
    toks = P(None, seq + exp, None)
    wts = P(exp, seq, None)
    in_specs = (
        rows, rows, rows, P(exp), P(exp), rows, toks, toks, P(), toks, wts, wts, wts,
        P(None, seq), P(None, seq), P(None, seq), P(), P(),
    )
    out_specs = (P(None, seq), rows, rows, rows, toks)
    return jax.shard_map(
        on_device, mesh=grid, in_specs=in_specs, out_specs=out_specs, check_vma=False
    )
```

```python
import jax
import jax.numpy as jnp
from jax import lax
from jax.experimental import pallas as pl
from jax.experimental.pallas import tpu as pltpu
from jax.sharding import Mesh, PartitionSpec as P

norm_epsilon = 1e-06
MESH = pl.DeviceIdType.MESH
AXES_SEQ = ("x", "c")
AXES_EXPERT = ("z", "y")

D = 6144
W_ROWS = 768
H_MAIN = 512
H_TAIL = 64
N_IN = 1152
N_ALL = 1792
TOK = 16
CAP = 80
HALF = 3072
BLOCK, HEAD = 256, 128
D_EXT = D + 128


def kernel(
    tok, moe, router, route, gate_w, up_w, down_w, qr, kr, vr, pr, rate, gain,
    roll_lp, train_lp, adv, low, high,
    obj, gh, gq, gk, gv,
    coef, coef_tok, grd, info, gates, wraw, out,
    wbuf, zx, zg, zi, xa, ga, pre, ugr, ggu, dxs, yha, yhb, yfp, yfm, cz, zr, zl, psel,
    f_own, f_sib, f_chip, b_own, b_sib, b_chip, f_far, b_far, state, dk_part, dv_part,
    ssem, rsem, lsem, xss, xrs,
):
    x, c, z, y = (lax.axis_index(a) for a in ("x", "c", "z", "y"))
    xp, xm = (x + 1) % 4, (x + 3) % 4
    yp, ym, y2 = (y + 1) % 4, (y + 3) % 4, (y + 2) % 4
    zp, zm = (z + 1) % 8, (z + 7) % 8
    right = {"x": {"x": xp}, "y": {"y": yp}, "z": {"z": zp}}
    left = {"x": {"x": xm}, "y": {"y": ym}, "z": {"z": zm}}
    sib = {"c": 1 - c}
    me = 2 * x + c
    started = []

    def send(src, dst, dev):
        at = len(started)
        copy = pltpu.make_async_remote_copy(
            src_ref=src, dst_ref=dst, send_sem=ssem.at[at], recv_sem=rsem.at[at],
            device_id=dev, device_id_type=MESH,
        )
        copy.start()
        started.append(copy)
        return copy

    raw = [
        pltpu.make_async_copy(w.at[0], wraw.at[n], lsem.at[n])
        for n, w in enumerate((gate_w, up_w, down_w))
    ]
    for copy in raw:
        copy.start()
    barrier = pltpu.get_barrier_semaphore()
    peers = [right[a] for a in "xyz"] + [left[a] for a in "xyz"] + [sib]
    peers += [{"x": xp, "c": 1 - c}, {"x": xm, "c": 1 - c}, {"x": (x + 2) % 4}]
    peers += [{"x": (x + 2) % 4, "c": 1 - c}]
    for peer in peers:
        pl.semaphore_signal(barrier, inc=1, device_id=peer, device_id_type=MESH)
    pl.semaphore_wait(barrier, len(peers))

    zx[z] = tok[...]
    zxr = [send(tok, zx.at[z], right["z"])]
    zxl = [send(tok, zx.at[z], left["z"])]

    for copy in raw:
        copy.wait()

    def pack(first):
        @pl.loop(0, W_ROWS // 128)
        def _(i):
            r = pl.ds(pl.multiple_of(first + i * 64, 64), 64)
            wbuf[me, r, 0:512] = wraw[0, r, 0:512]
            wbuf[me, r, 512:1024] = wraw[1, r, 0:512]
            wbuf[me, r, 1024:1152] = jnp.concatenate(
                [wraw[0, r, 512:576], wraw[1, r, 512:576]], axis=1
            )
            wbuf[me, r, 1152:1664] = wraw[2, r, 0:512]
            wbuf[me, r, 1664:1792] = jnp.concatenate(
                [wraw[2, r, 512:576], jnp.zeros((64, 64), jnp.bfloat16)], axis=1
            )

    half_a, half_b = pl.ds(0, W_ROWS // 2), pl.ds(W_ROWS // 2, W_ROWS // 2)
    pack(0)
    wra = send(wbuf.at[me, half_a], wbuf.at[me, half_a], right["x"])
    pack(W_ROWS // 2)
    wlb = send(wbuf.at[me, half_b], wbuf.at[me, half_b], left["x"])
    wrb = send(wbuf.at[me, half_b], wbuf.at[me, half_b], right["x"])
    wla = send(wbuf.at[me, half_a], wbuf.at[me, half_a], left["x"])
    ws = [send(wbuf.at[me], wbuf.at[me], sib)]

    f32, bf16 = jnp.float32, jnp.bfloat16
    nn, nt, tn = (((1,), (0,)), ((), ())), (((1,), (1,)), ((), ())), (((0,), (0,)), ((), ()))

    def mm(a, b, dims):
        return lax.dot_general(a, b, dims, preferred_element_type=f32)

    def parts_of(v):
        high = v.astype(bf16)
        return high, (v - high.astype(f32)).astype(bf16)

    def row_decay(h, sign, shift):
        row = lax.broadcasted_iota(jnp.int32, (BLOCK, HEAD), 0).astype(f32)
        return jnp.exp(-rate[h] * (sign * row + shift))

    def lanes(h):
        return pl.ds(pl.multiple_of(h * HEAD, HEAD), HEAD)

    def block_decay(h, blocks):
        return jnp.exp(jnp.full((HEAD, HEAD), -rate[h] * (BLOCK * blocks), f32))

    def summaries():
        @pl.loop(0, 4)
        def _(i):
            r, h = i // 2, i % 2
            v_high, v_low = parts_of(vr[r, :, lanes(h)].astype(f32) * row_decay(h, -1.0, BLOCK - 1.0))
            key = kr[r, :, lanes(h)]
            f_own[r, h] = mm(key, v_high, tn) + mm(key, v_low, tn)

    def chip_state(own_ref, sib_ref, chip_ref, near_is_own):
        for h in range(2):
            mine, other = own_ref[c, h], sib_ref[c, h]
            near = jnp.where(near_is_own, mine, other)
            far = jnp.where(near_is_own, other, mine)
            chip_ref[h] = near + block_decay(h, 1) * far

    def far_copy(chip_ref, far_ref, base, dx, cc, to):
        return pltpu.make_async_remote_copy(
            src_ref=chip_ref, dst_ref=far_ref.at[dx - 1, c],
            send_sem=xss.at[base + 2 * (dx - 1) + cc], recv_sem=xrs.at[base + 2 * (dx - 1) + c],
            device_id={"x": to, "c": cc}, device_id_type=MESH,
        )

    def far_send(chip_ref, far_ref, base, step, finish=False):
        for dx in (1, 2, 3):
            to = x + step * dx

            @pl.when(jnp.logical_and(to >= 0, to < 4))
            def _():
                for cc in (0, 1):
                    copy = far_copy(chip_ref, far_ref, base, dx, cc, to)
                    if finish:
                        copy.wait_send()
                    else:
                        copy.start()

    def far_state(chip_ref, far_ref, sib_ref, base, step, with_sib):
        for dx in (1, 2, 3):
            at = x - step * dx
            there = jnp.logical_and(at >= 0, at < 4)

            @pl.when(there)
            def _():
                for r in (0, 1):
                    pltpu.make_async_remote_copy(
                        src_ref=chip_ref, dst_ref=far_ref.at[dx - 1, r],
                        send_sem=xss.at[base + 2 * (dx - 1) + r],
                        recv_sem=xrs.at[base + 2 * (dx - 1) + r],
                        device_id={"x": (x + 1) % 4, "c": r}, device_id_type=MESH,
                    ).wait_recv()

            @pl.when(jnp.logical_not(there))
            def _():
                far_ref[dx - 1] = jnp.zeros_like(far_ref[dx - 1])

        for r in range(2):
            for h in range(2):
                two = block_decay(h, 2)
                far = far_ref[0, r, h] + two * (far_ref[1, r, h] + two * far_ref[2, r, h])
                near = sib_ref[r, h] + block_decay(h, 1) * far
                state[r, h] = jnp.where(with_sib, near, far)

    def attention_main():
        @pl.loop(0, 4)
        def _(i):
            r, h = i // 2, i % 2
            query, key, value = qr[r, :, lanes(h)], kr[r, :, lanes(h)], vr[r, :, lanes(h)]
            at_i = lax.broadcasted_iota(jnp.int32, (BLOCK, BLOCK), 0)
            at_j = lax.broadcasted_iota(jnp.int32, (BLOCK, BLOCK), 1)
            apart = jnp.maximum(at_i - at_j, 0).astype(f32)
            within = jnp.where(at_i >= at_j, jnp.exp(-rate[h] * apart), 0.0)
            s_high, s_low = parts_of(mm(query, key, nt) * within)
            t_high, t_low = parts_of(state[r, h])
            lead = row_decay(h, 1.0, 1.0)
            attn = mm(s_high, value, nn) + mm(s_low, value, nn)
            attn = attn + lead * (mm(query, t_high, nn) + mm(query, t_low, nn))
            inverse = lax.rsqrt(jnp.mean(attn * attn, axis=1, keepdims=True) + norm_epsilon)
            scaled = gain[:, lanes(h)] * (coef[r] * pr[r, :, lanes(h)].astype(f32))
            along = jnp.mean(scaled * attn, axis=1, keepdims=True)
            grad = inverse * scaled - attn * (inverse * inverse * inverse * along)
            g_high, g_low = parts_of(grad)
            d_high, d_low = parts_of(grad * row_decay(h, 1.0, 0.0))
            b_own[r, h] = mm(query, d_high, tn) + mm(query, d_low, tn)
            p_high, p_low = parts_of((mm(g_high, value, nt) + mm(g_low, value, nt)) * within)
            dq = mm(p_high, key, nn) + mm(p_low, key, nn)
            dq = dq + lead * (mm(g_high, t_high, nt) + mm(g_low, t_high, nt) + mm(g_high, t_low, nt))
            gq[r, :, lanes(h)] = dq.astype(bf16)
            dk_part[r, :, lanes(h)] = mm(p_high, query, tn) + mm(p_low, query, tn)
            dv_part[r, :, lanes(h)] = (
                mm(s_high, g_high, tn) + mm(s_low, g_high, tn) + mm(s_high, g_low, tn)
            )

    def attention_last():
        @pl.loop(0, 4)
        def _(i):
            r, h = i // 2, i % 2
            key, value = kr[r, :, lanes(h)], vr[r, :, lanes(h)]
            t_high, t_low = parts_of(state[r, h])
            tail = row_decay(h, -1.0, float(BLOCK))
            dk = dk_part[r, :, lanes(h)] + tail * (mm(value, t_high, nt) + mm(value, t_low, nt))
            dv = dv_part[r, :, lanes(h)] + tail * (mm(key, t_high, nn) + mm(key, t_low, nn))
            gk[r, :, lanes(h)] = dk.astype(bf16)
            gv[r, :, lanes(h)] = dv.astype(bf16)

    lane = lax.broadcasted_iota(jnp.int32, (TOK, 128), 1)
    token = lax.broadcasted_iota(jnp.int32, (TOK, 128), 0)
    member = jnp.logical_or(lane == route[:, 0:1], lane == route[:, 1:2])
    t_row = lax.broadcasted_iota(jnp.int32, (TOK, TOK), 0)
    t_col = lax.broadcasted_iota(jnp.int32, (TOK, TOK), 1)
    ahead = jnp.logical_and(t_col < t_row, (t_col >= 8) == (t_row >= 8))
    rank = mm(ahead.astype(f32).astype(bf16), member.astype(f32).astype(bf16), nn)
    slot = rank + jnp.where(token >= 8, 6.0, 1.0) + (10 * z).astype(f32)
    slot = jnp.where(member, slot, 0.0)
    gates[...] = jnp.zeros_like(gates)
    gates[:, 0:4] = mm(tok[...], router[...], nn)
    weight = jnp.where(member, jnp.exp(gates[...]), 0.0)
    gate = weight / jnp.sum(weight, axis=1, keepdims=True)
    gates[...] = gate
    a_high, a_low = parts_of(slot + pltpu.roll(gate, 4, 1))
    place = (lane == token + TOK * z).astype(f32).astype(bf16)
    info[...] = (mm(a_high, place, tn) + mm(a_low, place, tn))[0:8]
    zi[z] = info[...]
    zir = [send(info, zi.at[z], right["z"])]
    zil = [send(info, zi.at[z], left["z"])]

    ratio = jnp.exp(train_lp[...] - roll_lp[...])
    ratio = jnp.minimum(jnp.maximum(ratio, low[0]), high[0])
    coeff = -(ratio * adv[...]) / 2.0
    obj[...] = coeff * train_lp[...]
    eye = lax.broadcasted_iota(jnp.int32, (128, 128), 0) == lax.broadcasted_iota(
        jnp.int32, (128, 128), 1
    )
    for r in range(2):
        for part in range(2):
            row = jnp.broadcast_to(coeff[r : r + 1, 128 * part : 128 * part + 128], (128, 128))
            col = jnp.sum(jnp.where(eye, row, 0.0), axis=1, keepdims=True)
            coef[r, 128 * part : 128 * part + 128, :] = jnp.broadcast_to(col, (128, 128))
    here = pl.ds(pl.multiple_of(8 * (4 * z + y), 8), 8)
    for r in range(2):
        coef_tok[8 * r : 8 * r + 8, :] = coef[r, here, :]

    @pl.loop(0, D // 512)
    def _(i):
        cols = pl.ds(pl.multiple_of(i * 512, 512), 512)
        grad = moe[:, cols].astype(f32) * coef_tok[:, 0:1]
        grd[:, cols] = grad.astype(bf16)
        zg[z, :, cols] = grad.astype(bf16)

    pre[...] = jnp.zeros_like(pre)
    ugr[...] = jnp.zeros_like(ugr)
    summaries()
    fs = send(f_own, f_sib, sib)

    def z_hop(h, buf, rights, lefts):
        rights[h - 1].wait_recv()
        if h < 4:
            at = (z + 8 - h) % 8
            rights.append(send(buf.at[at], buf.at[at], right["z"]))
        if h <= 3:
            lefts[h - 1].wait_recv()
            if h < 3:
                at = (z + h) % 8
                lefts.append(send(buf.at[at], buf.at[at], left["z"]))

    for h in range(1, 5):
        z_hop(h, zx, zxr, zxl)
        z_hop(h, zi, zir, zil)
    zgr = [send(grd, zg.at[z], right["z"])]
    zgl = [send(grd, zg.at[z], left["z"])]

    k = z // 2
    total = zi[0]
    for i in range(1, 8):
        total = total + zi[i]
    kind = lax.broadcasted_iota(jnp.int32, (8, 128), 0)
    slot_row = jnp.sum(jnp.where(kind == k, total, 0.0), axis=0, keepdims=True)
    gate_row = jnp.sum(jnp.where(kind == k + 4, total, 0.0), axis=0, keepdims=True)
    rows = lax.broadcasted_iota(jnp.int32, (CAP, 128), 0).astype(jnp.float32) + 1.0
    hot = (rows == jnp.broadcast_to(slot_row, (CAP, 128))).astype(jnp.float32)
    gate_slot = jnp.sum(hot * jnp.broadcast_to(gate_row, (CAP, 128)), axis=1, keepdims=True)
    psel[...] = hot.astype(jnp.bfloat16)

    def compact(buf, dst):
        @pl.loop(0, D // 512)
        def _(i):
            cols = pl.ds(pl.multiple_of(i * 512, 512), 512)
            block = buf[:, :, cols].reshape(8 * TOK, 512)
            dst[y, :, cols] = jnp.dot(
                psel[...], block, preferred_element_type=jnp.float32
            ).astype(jnp.bfloat16)

    col_a, col_b = pl.ds(0, HALF), pl.ds(HALF, HALF)

    def y_send(buf):
        ra = send(buf.at[y, :, col_a], buf.at[y, :, col_a], right["y"])
        lb = send(buf.at[y, :, col_b], buf.at[y, :, col_b], left["y"])
        rb = send(buf.at[y, :, col_b], buf.at[y, :, col_b], right["y"])
        la = send(buf.at[y, :, col_a], buf.at[y, :, col_a], left["y"])
        return ra, lb, rb, la

    def y_relay(buf, ra, lb):
        ra.wait_recv()
        fa = send(buf.at[ym, :, col_a], buf.at[ym, :, col_a], right["y"])
        lb.wait_recv()
        fb = send(buf.at[yp, :, col_b], buf.at[yp, :, col_b], left["y"])
        return fa, fb

    compact(zx, xa)
    yx = y_send(xa)
    z_hop(1, zg, zgr, zgl)
    s_xm, s_xp, s_x2 = 2 * xm + c, 2 * xp + c, 2 * ((x + 2) % 4) + c
    wra.wait_recv()
    wfa = send(wbuf.at[s_xm, half_a], wbuf.at[s_xm, half_a], right["x"])
    ws.append(send(wbuf.at[s_xm, half_a], wbuf.at[s_xm, half_a], sib))
    wlb.wait_recv()
    wfb = send(wbuf.at[s_xp, half_b], wbuf.at[s_xp, half_b], left["x"])
    ws.append(send(wbuf.at[s_xp, half_b], wbuf.at[s_xp, half_b], sib))
    fs.wait_recv()
    chip_state(f_own, f_sib, f_chip, c == 1)
    far_send(f_chip, f_far, 0, 1)
    z_hop(2, zg, zgr, zgl)
    z_hop(3, zg, zgr, zgl)
    yxf = y_relay(xa, yx[0], yx[1])
    z_hop(4, zg, zgr, zgl)
    compact(zg, ga)
    yg = y_send(ga)
    yx[2].wait_recv()
    yx[3].wait_recv()
    wrb.wait_recv()
    ws.append(send(wbuf.at[s_xm, half_b], wbuf.at[s_xm, half_b], sib))
    wla.wait_recv()
    ws.append(send(wbuf.at[s_xp, half_a], wbuf.at[s_xp, half_a], sib))
    yxf[0].wait_recv()
    yxf[1].wait_recv()

    def add_in(shard):
        cols = pl.ds(pl.multiple_of(shard * W_ROWS, W_ROWS), W_ROWS)
        left_op = xa[:, :, cols].reshape(4 * CAP, W_ROWS)
        for at, wide in ((0, 256), (256, 256), (512, 256), (768, 256), (1024, 128)):
            pre[:, at : at + wide] += jnp.dot(
                left_op, wbuf[shard, :, at : at + wide], preferred_element_type=jnp.float32
            )

    def add_out(shard):
        cols = pl.ds(pl.multiple_of(shard * W_ROWS, W_ROWS), W_ROWS)
        left_op = ga[:, :, cols].reshape(4 * CAP, W_ROWS)
        for at, wide in ((0, 256), (256, 256), (512, 128)):
            ugr[:, at : at + wide] += jnp.dot(
                left_op, wbuf[shard, :, N_IN + at : N_IN + at + wide],
                preferred_element_type=jnp.float32,
            )

    for copy in ws:
        copy.wait_recv()
    ws_done = len(ws)

    @pl.loop(0, 6)
    def _(i):
        add_in((2 * (x + 3) + i) % 8)

    ygf = y_relay(ga, yg[0], yg[1])
    yg[2].wait_recv()
    yg[3].wait_recv()
    ygf[0].wait_recv()
    ygf[1].wait_recv()

    @pl.loop(0, 6)
    def _(i):
        add_out((2 * (x + 3) + i) % 8)

    wfa.wait_recv()
    ws.append(send(wbuf.at[s_x2, half_a], wbuf.at[s_x2, half_a], sib))
    wfb.wait_recv()
    ws.append(send(wbuf.at[s_x2, half_b], wbuf.at[s_x2, half_b], sib))
    add_in(s_x2)
    add_out(s_x2)
    for copy in ws[ws_done:]:
        copy.wait_recv()
    s_x2o = 2 * ((x + 2) % 4) + 1 - c
    add_in(s_x2o)
    add_out(s_x2o)

    def grads(gate, up, unit):
        sig = jax.nn.sigmoid(gate)
        act = gate * sig
        up_grad = unit * act
        gate_grad = unit * up * sig * (1.0 + gate * (1.0 - sig))
        score = jnp.sum(act * up * unit, axis=1, keepdims=True)
        return gate_grad, up_grad, score

    @pl.loop(0, 4)
    def _(b):
        @pl.loop(0, CAP // TOK)
        def _(i):
            at = pl.multiple_of(b * CAP + i * TOK, TOK)
            r = pl.ds(at, TOK)
            gg, ug, s1 = grads(pre[r, 0:512], pre[r, 512:1024], ugr[r, 0:512])
            tail = pre[r, 1024:1152]
            ggt, ugt, s2 = grads(tail, pltpu.roll(tail, 64, 1), ugr[r, 512:640])
            ggu[r, 0:512] = gg.astype(jnp.bfloat16)
            ggu[r, 512:1024] = ug.astype(jnp.bfloat16)
            ggu[r, 1024:1152] = (ggt + pltpu.roll(ugt, 64, 1)).astype(jnp.bfloat16)
            score = jnp.where(lane == k, jnp.broadcast_to(s1 + s2, (TOK, 128)), 0.0)
            dxs[b, pl.ds(pl.multiple_of(i * TOK, TOK), TOK), D:D_EXT] = score.astype(jnp.bfloat16)

    def to_dx(shard):
        for at in (0, 256, 512):
            cols = pl.ds(pl.multiple_of(shard * W_ROWS + at, 256), 256)
            part = lax.dot_general(
                ggu[...], wbuf[shard, at : at + 256, 0:N_IN], (((1,), (1,)), ((), ())),
                preferred_element_type=jnp.float32,
            )
            dxs[:, :, cols] = part.astype(jnp.bfloat16).reshape(4, CAP, 256)

    ext_b = pl.ds(HALF, D_EXT - HALF)

    @pl.loop(0, 4)
    def _(i):
        to_dx(i)

    ha = send(dxs.at[y2, :, col_a], yha, right["y"])
    fma = send(dxs.at[ym, :, col_a], yfp.at[:, col_a], left["y"])

    @pl.loop(4, 8)
    def _(i):
        to_dx(i)

    hb = send(dxs.at[y2, :, ext_b], yhb, left["y"])
    fpb = send(dxs.at[yp, :, ext_b], yfm.at[:, ext_b], right["y"])

    def add_rows(dst, add, lo, n):
        @pl.loop(0, n // 128)
        def _(i):
            to = pl.ds(pl.multiple_of(lo + i * 128, 128), 128)
            fr = pl.ds(pl.multiple_of(i * 128, 128), 128)
            dst[:, to] = (
                dst[:, to].astype(jnp.float32) + add[:, fr].astype(jnp.float32)
            ).astype(jnp.bfloat16)

    ha.wait_recv()
    add_rows(dxs.at[yp], yha, 0, HALF)
    fpa = send(dxs.at[yp, :, col_a], yfm.at[:, col_a], right["y"])
    hb.wait_recv()
    add_rows(dxs.at[ym], yhb, HALF, D_EXT - HALF)
    fmb = send(dxs.at[ym, :, ext_b], yfp.at[:, ext_b], left["y"])
    far_state(f_chip, f_far, f_sib, 0, 1, c == 1)
    attention_main()
    bs = send(b_own, b_sib, sib)
    bs.wait_recv()
    chip_state(b_own, b_sib, b_chip, c == 0)
    far_send(b_chip, b_far, 6, -1)
    for copy in (fma, fpb, fpa, fmb):
        copy.wait_recv()

    def spread(cols, wide, gated):
        part = dxs[y, :, cols].astype(jnp.float32) + yfp[:, cols].astype(jnp.float32)
        part = part + yfm[:, cols].astype(jnp.float32)
        if gated:
            part = part * gate_slot
        back = lax.dot_general(
            psel[...], part.astype(jnp.bfloat16), (((0,), (0,)), ((), ())),
            preferred_element_type=jnp.float32,
        )
        cz[:, :, cols] = back.astype(jnp.bfloat16).reshape(8, TOK, wide)

    @pl.loop(0, D // 512)
    def _(i):
        spread(pl.ds(pl.multiple_of(i * 512, 512), 512), 512, True)

    spread(pl.ds(D, 128), 128, False)

    parts = (col_a, ext_b)

    def z_first(dst, dev, at):
        return [send(cz.at[at, :, p], dst.at[0, :, p], dev) for p in parts]

    zrc = [z_first(zr, right["z"], (z + 4) % 8)]
    zlc = [z_first(zl, left["z"], (z + 5) % 8)]
    far_state(b_chip, b_far, b_sib, 6, -1, c == 0)
    attention_last()
    for h in range(1, 4):
        nr, nl = [], []
        for n, p in enumerate(parts):
            at = (z + 4 - h) % 8
            zrc[h - 1][n].wait_recv()
            cz[at, :, p] = (
                cz[at, :, p].astype(jnp.float32) + zr[h - 1, :, p].astype(jnp.float32)
            ).astype(jnp.bfloat16)
            nr.append(send(cz.at[at, :, p], zr.at[h, :, p], right["z"]))
            if h < 3:
                at = (z + 5 + h) % 8
                zlc[h - 1][n].wait_recv()
                cz[at, :, p] = (
                    cz[at, :, p].astype(jnp.float32) + zl[h - 1, :, p].astype(jnp.float32)
                ).astype(jnp.bfloat16)
                nl.append(send(cz.at[at, :, p], zl.at[h, :, p], left["z"]))
        zrc.append(nr)
        zlc.append(nl)
    for n, p in enumerate(parts):
        zlc[2][n].wait_recv()
        zrc[3][n].wait_recv()
        out[:, p] = (
            cz[z, :, p].astype(jnp.float32)
            + zr[3, :, p].astype(jnp.float32)
            + zl[2, :, p].astype(jnp.float32)
        )

    score = out[:, D:D_EXT]
    gate = gates[...]
    logit = gate * (score - jnp.sum(gate * score, axis=1, keepdims=True))
    l_high, l_low = parts_of(logit[:, 0:4])

    @pl.loop(0, D // 512)
    def _(i):
        cols = pl.ds(pl.multiple_of(i * 512, 512), 512)
        to_hidden = mm(l_high, router[cols, :], nt) + mm(l_low, router[cols, :], nt)
        gh[:, cols] = (out[:, cols] + to_hidden).astype(bf16)

    for copy in started:
        copy.wait_send()
    far_send(f_chip, f_far, 0, 1, finish=True)
    far_send(b_chip, b_far, 6, -1, finish=True)


def copy_out(*refs):
    n = len(refs) // 3
    sem = refs[-1]
    ins, outs, bufs = refs[:n], refs[n : 2 * n], refs[2 * n : 3 * n]
    arrive = [pltpu.make_async_copy(ins[i], bufs[i], sem.at[i]) for i in range(n)]
    leave = [pltpu.make_async_copy(bufs[i], outs[i], sem.at[n + i]) for i in range(n)]
    for copy in arrive:
        copy.start()
    for i in range(n):
        arrive[i].wait()
        leave[i].start()
    for copy in leave:
        copy.wait()


def results(*arrays):
    n = len(arrays)
    where = pl.BlockSpec(memory_space=pl.ANY)
    return pl.pallas_call(
        copy_out,
        out_shape=[jax.ShapeDtypeStruct(a.shape, a.dtype) for a in arrays],
        in_specs=[where] * n,
        out_specs=[where] * n,
        scratch_shapes=[pltpu.VMEM(a.shape, a.dtype) for a in arrays]
        + [pltpu.SemaphoreType.DMA((2 * n,))],
        name="results",
    )(*arrays)


def all_blocks(*operands):
    bf16, f32 = jnp.bfloat16, jnp.float32
    vmem, smem = (pl.BlockSpec(memory_space=m) for m in (pltpu.VMEM, pltpu.SMEM))
    hbm = pl.BlockSpec(memory_space=pl.ANY)
    n_copies = 68
    grads = jax.ShapeDtypeStruct((2, BLOCK, 2 * HEAD), bf16)
    states = pltpu.VMEM((2, 2, HEAD, HEAD), f32)
    return pl.pallas_call(
        kernel,
        out_shape=[
            jax.ShapeDtypeStruct((2, BLOCK), f32), jax.ShapeDtypeStruct((TOK, D), bf16),
            grads, grads, grads,
        ],
        in_specs=[vmem] * 4 + [hbm] * 3 + [vmem] * 4 + [smem] + [vmem] * 4 + [smem] * 2,
        out_specs=[vmem] * 5,
        scratch_shapes=[
            pltpu.VMEM((2, BLOCK, 128), f32),
            pltpu.VMEM((TOK, 128), f32),
            pltpu.VMEM((TOK, D), bf16),
            pltpu.VMEM((8, 128), f32),
            pltpu.VMEM((TOK, 128), f32),
            pltpu.VMEM((3, W_ROWS, H_MAIN + H_TAIL), bf16),
            pltpu.VMEM((TOK, D_EXT), f32),
            pltpu.VMEM((8, W_ROWS, N_ALL), bf16),
            pltpu.VMEM((8, TOK, D), bf16),
            pltpu.VMEM((8, TOK, D), bf16),
            pltpu.VMEM((8, 8, 128), f32),
            pltpu.VMEM((4, CAP, D), bf16),
            pltpu.VMEM((4, CAP, D), bf16),
            pltpu.VMEM((4 * CAP, N_IN), f32),
            pltpu.VMEM((4 * CAP, N_ALL - N_IN), f32),
            pltpu.VMEM((4 * CAP, N_IN), bf16),
            pltpu.VMEM((4, CAP, D_EXT), bf16),
            pltpu.VMEM((CAP, HALF), bf16),
            pltpu.VMEM((CAP, D_EXT - HALF), bf16),
            pltpu.VMEM((CAP, D_EXT), bf16),
            pltpu.VMEM((CAP, D_EXT), bf16),
            pltpu.VMEM((8, TOK, D_EXT), bf16),
            pltpu.VMEM((4, TOK, D_EXT), bf16),
            pltpu.VMEM((3, TOK, D_EXT), bf16),
            pltpu.VMEM((CAP, 128), bf16),
            states, states, pltpu.VMEM((2, HEAD, HEAD), f32),
            states, states, pltpu.VMEM((2, HEAD, HEAD), f32),
            pltpu.VMEM((3, 2, 2, HEAD, HEAD), f32),
            pltpu.VMEM((3, 2, 2, HEAD, HEAD), f32),
            states,
            pltpu.VMEM((2, BLOCK, 2 * HEAD), f32),
            pltpu.VMEM((2, BLOCK, 2 * HEAD), f32),
            pltpu.SemaphoreType.DMA((n_copies,)),
            pltpu.SemaphoreType.DMA((n_copies,)),
            pltpu.SemaphoreType.DMA((3,)),
            pltpu.SemaphoreType.DMA((12,)),
            pltpu.SemaphoreType.DMA((12,)),
        ],
        compiler_params=pltpu.CompilerParams(
            collective_id=0, has_side_effects=True, vmem_limit_bytes=64 * 1024 * 1024 - 65536
        ),
        cost_estimate=pl.CostEstimate(
            flops=12 * 10**9, bytes_accessed=40 * 10**6, transcendentals=200000
        ),
        name="all_blocks",
    )(*operands)


def on_device(
    queries,
    key_rows,
    value_rows,
    decay_rate,
    norm_gain,
    attn_probe,
    hidden_in,
    moe_probe,
    router_weight,
    routes,
    gate_weight,
    up_weight,
    down_weight,
    rollout_logprob,
    trainer_logprob,
    advantage,
    clip_low,
    clip_high,
):
    rollouts, positions, width = hidden_in.shape
    objective, *rest = all_blocks(
        hidden_in.reshape(TOK, width), moe_probe.reshape(TOK, width), router_weight,
        routes.reshape(TOK, 2), gate_weight, up_weight, down_weight,
        queries, key_rows, value_rows, attn_probe, decay_rate, norm_gain.reshape(1, -1),
        rollout_logprob, trainer_logprob, advantage, clip_low, clip_high,
    )
    objective, grad_hidden, *grads = results(objective, *rest)
    return (objective, *grads, grad_hidden.reshape(rollouts, positions, width))


def solution(mesh):
    grid = Mesh(mesh.devices.reshape(4, 2, 8, 4), ("x", "c", "z", "y"))
    seq, exp = AXES_SEQ, AXES_EXPERT
    rows = P(None, seq, exp)
    toks = P(None, seq + exp, None)
    wts = P(exp, seq, None)
    in_specs = (
        rows, rows, rows, P(exp), P(exp), rows, toks, toks, P(), toks, wts, wts, wts,
        P(None, seq), P(None, seq), P(None, seq), P(), P(),
    )
    out_specs = (P(None, seq), rows, rows, rows, toks)
    return jax.shard_map(
        on_device, mesh=grid, in_specs=in_specs, out_specs=out_specs, check_vma=False
    )
```

```python
import jax
import jax.numpy as jnp
from jax import lax
from jax.experimental import pallas as pl
from jax.experimental.pallas import tpu as pltpu
from jax.sharding import Mesh, PartitionSpec as P

norm_epsilon = 1e-06
MESH = pl.DeviceIdType.MESH
AXES_SEQ = ("x", "c")
AXES_EXPERT = ("z", "y")

D = 6144
W_COLS = 768
UNITS = 576
H_MAIN = 512
N_IN = 1152
N_ALL = 1728
U_PAD = 640
TOK = 16
CAP = 80
HALF = 3072
BLOCK, HEAD = 256, 128
D_EXT = D + 128


def kernel(
    tok, moe, router, route, gate_w, up_w, down_w, qr, kr, vr, pr, rate, gain,
    roll_lp, train_lp, adv, low, high,
    obj, gh, gq, gk, gv,
    coef, coef_tok, route_tok, grd, info, gates, out,
    wbuf, zx, zg, zi, xa, ga, pre, ugr, ggu, dxs, yh, yfp, yfm, cz, zr, zl, psel,
    f_own, f_sib, f_chip, b_own, b_sib, b_chip, f_far, b_far, state, dk_part, dv_part,
    ssem, rsem, lsem, xss, xrs,
):
    x, c, z, y = (lax.axis_index(a) for a in ("x", "c", "z", "y"))
    xp, xm = (x + 1) % 4, (x + 3) % 4
    yp, ym, y2 = (y + 1) % 4, (y + 3) % 4, (y + 2) % 4
    zp, zm = (z + 1) % 8, (z + 7) % 8
    right = {"x": {"x": xp}, "y": {"y": yp}, "z": {"z": zp}}
    left = {"x": {"x": xm}, "y": {"y": ym}, "z": {"z": zm}}
    sib = {"c": 1 - c}
    me = 2 * x + c
    started = []

    def send(src, dst, dev):
        at = len(started)
        copy = pltpu.make_async_remote_copy(
            src_ref=src, dst_ref=dst, send_sem=ssem.at[at], recv_sem=rsem.at[at],
            device_id=dev, device_id_type=MESH,
        )
        copy.start()
        started.append(copy)
        return copy

    raw = [
        pltpu.make_async_copy(
            w.at[0, pl.ds(src, n)], wbuf.at[me, pl.ds(dst, n)], lsem.at[i]
        )
        for i, (w, src, dst, n) in enumerate((
            (gate_w, 0, 0, H_MAIN),
            (up_w, 0, H_MAIN, H_MAIN),
            (gate_w, H_MAIN, 2 * H_MAIN, UNITS - H_MAIN),
            (up_w, H_MAIN, H_MAIN + UNITS, UNITS - H_MAIN),
            (down_w, 0, N_IN, UNITS),
        ))
    ]
    for copy in raw:
        copy.start()
    barrier = pltpu.get_barrier_semaphore()
    peers = [right[a] for a in "xyz"] + [left[a] for a in "xyz"] + [sib]
    peers += [{"x": xp, "c": 1 - c}, {"x": xm, "c": 1 - c}, {"x": (x + 2) % 4}]
    peers += [{"x": (x + 2) % 4, "c": 1 - c}]
    for peer in peers:
        pl.semaphore_signal(barrier, inc=1, device_id=peer, device_id_type=MESH)
    pl.semaphore_wait(barrier, len(peers))

    col_a, col_b = pl.ds(0, HALF), pl.ds(HALF, HALF)
    zx[z] = tok[...]

    def z_own(src, dst, dev):
        return [[send(src.at[:, p], dst.at[z, :, p], dev) for p in (col_a, col_b)]]

    zxr = z_own(tok, zx, right["z"])
    zxl = z_own(tok, zx, left["z"])

    half = N_ALL // 2
    half_a, half_b = pl.ds(0, half), pl.ds(half, half)
    quarters_a = pl.ds(0, half // 2), pl.ds(half // 2, half // 2)
    quarters_b = pl.ds(half, half // 2), pl.ds(half + half // 2, half // 2)
    for copy in raw:
        copy.wait()
    wra = send(wbuf.at[me, half_a], wbuf.at[me, half_a], right["x"])
    wlb = send(wbuf.at[me, half_b], wbuf.at[me, half_b], left["x"])
    wrb = send(wbuf.at[me, half_b], wbuf.at[me, half_b], right["x"])
    wla = send(wbuf.at[me, half_a], wbuf.at[me, half_a], left["x"])
    ws = [send(wbuf.at[me], wbuf.at[me], sib)]

    f32, bf16 = jnp.float32, jnp.bfloat16
    nn, nt, tn = (((1,), (0,)), ((), ())), (((1,), (1,)), ((), ())), (((0,), (0,)), ((), ()))

    def mm(a, b, dims):
        return lax.dot_general(a, b, dims, preferred_element_type=f32)

    def parts_of(v):
        high = v.astype(bf16)
        return high, (v - high.astype(f32)).astype(bf16)

    def row_decay(h, sign, shift):
        row = lax.broadcasted_iota(jnp.int32, (BLOCK, HEAD), 0).astype(f32)
        return jnp.exp(-rate[h] * (sign * row + shift))

    def lanes(h):
        return pl.ds(pl.multiple_of(h * HEAD, HEAD), HEAD)

    def block_decay(h, blocks):
        return jnp.exp(jnp.full((HEAD, HEAD), -rate[h] * (BLOCK * blocks), f32))

    def summaries():
        @pl.loop(0, 4)
        def _(i):
            r, h = i // 2, i % 2
            v_high, v_low = parts_of(vr[r, :, lanes(h)].astype(f32) * row_decay(h, -1.0, BLOCK - 1.0))
            key = kr[r, :, lanes(h)]
            f_own[r, h] = mm(key, v_high, tn) + mm(key, v_low, tn)

    def chip_state(own_ref, sib_ref, chip_ref, near_is_own):
        for h in range(2):
            mine, other = own_ref[c, h], sib_ref[c, h]
            near = jnp.where(near_is_own, mine, other)
            far = jnp.where(near_is_own, other, mine)
            chip_ref[h] = near + block_decay(h, 1) * far

    def far_copy(chip_ref, far_ref, base, dx, cc, to):
        return pltpu.make_async_remote_copy(
            src_ref=chip_ref, dst_ref=far_ref.at[dx - 1, c],
            send_sem=xss.at[base + 2 * (dx - 1) + cc], recv_sem=xrs.at[base + 2 * (dx - 1) + c],
            device_id={"x": to, "c": cc}, device_id_type=MESH,
        )

    def far_send(chip_ref, far_ref, base, step, finish=False):
        for dx in (1, 2, 3):
            to = x + step * dx

            @pl.when(jnp.logical_and(to >= 0, to < 4))
            def _():
                for cc in (0, 1):
                    copy = far_copy(chip_ref, far_ref, base, dx, cc, to)
                    if finish:
                        copy.wait_send()
                    else:
                        copy.start()

    def far_state(chip_ref, far_ref, sib_ref, base, step, with_sib):
        for dx in (1, 2, 3):
            at = x - step * dx
            there = jnp.logical_and(at >= 0, at < 4)

            @pl.when(there)
            def _():
                for r in (0, 1):
                    pltpu.make_async_remote_copy(
                        src_ref=chip_ref, dst_ref=far_ref.at[dx - 1, r],
                        send_sem=xss.at[base + 2 * (dx - 1) + r],
                        recv_sem=xrs.at[base + 2 * (dx - 1) + r],
                        device_id={"x": (x + 1) % 4, "c": r}, device_id_type=MESH,
                    ).wait_recv()

            @pl.when(jnp.logical_not(there))
            def _():
                far_ref[dx - 1] = jnp.zeros_like(far_ref[dx - 1])

        for r in range(2):
            for h in range(2):
                two = block_decay(h, 2)
                far = far_ref[0, r, h] + two * (far_ref[1, r, h] + two * far_ref[2, r, h])
                near = sib_ref[r, h] + block_decay(h, 1) * far
                state[r, h] = jnp.where(with_sib, near, far)

    def attention_main(first, end):
        @pl.loop(first, end)
        def _(i):
            r, h = i // 2, i % 2
            query, key, value = qr[r, :, lanes(h)], kr[r, :, lanes(h)], vr[r, :, lanes(h)]
            at_i = lax.broadcasted_iota(jnp.int32, (BLOCK, BLOCK), 0)
            at_j = lax.broadcasted_iota(jnp.int32, (BLOCK, BLOCK), 1)
            apart = jnp.maximum(at_i - at_j, 0).astype(f32)
            within = jnp.where(at_i >= at_j, jnp.exp(-rate[h] * apart), 0.0)
            s_high, s_low = parts_of(mm(query, key, nt) * within)
            t_high, t_low = parts_of(state[r, h])
            lead = row_decay(h, 1.0, 1.0)
            attn = mm(s_high, value, nn) + mm(s_low, value, nn)
            attn = attn + lead * (mm(query, t_high, nn) + mm(query, t_low, nn))
            inverse = lax.rsqrt(jnp.mean(attn * attn, axis=1, keepdims=True) + norm_epsilon)
            scaled = gain[:, lanes(h)] * (coef[r] * pr[r, :, lanes(h)].astype(f32))
            along = jnp.mean(scaled * attn, axis=1, keepdims=True)
            grad = inverse * scaled - attn * (inverse * inverse * inverse * along)
            g_high, g_low = parts_of(grad)
            d_high, d_low = parts_of(grad * row_decay(h, 1.0, 0.0))
            b_own[r, h] = mm(query, d_high, tn) + mm(query, d_low, tn)
            p_high, p_low = parts_of((mm(g_high, value, nt) + mm(g_low, value, nt)) * within)
            dq = mm(p_high, key, nn) + mm(p_low, key, nn)
            dq = dq + lead * (mm(g_high, t_high, nt) + mm(g_low, t_high, nt) + mm(g_high, t_low, nt))
            gq[r, :, lanes(h)] = dq.astype(bf16)
            dk_part[r, :, lanes(h)] = mm(p_high, query, tn) + mm(p_low, query, tn)
            dv_part[r, :, lanes(h)] = (
                mm(s_high, g_high, tn) + mm(s_low, g_high, tn) + mm(s_high, g_low, tn)
            )

    def attention_last():
        @pl.loop(0, 4)
        def _(i):
            r, h = i // 2, i % 2
            key, value = kr[r, :, lanes(h)], vr[r, :, lanes(h)]
            t_high, t_low = parts_of(state[r, h])
            tail = row_decay(h, -1.0, float(BLOCK))
            dk = dk_part[r, :, lanes(h)] + tail * (mm(value, t_high, nt) + mm(value, t_low, nt))
            dv = dv_part[r, :, lanes(h)] + tail * (mm(key, t_high, nn) + mm(key, t_low, nn))
            gk[r, :, lanes(h)] = dk.astype(bf16)
            gv[r, :, lanes(h)] = dv.astype(bf16)

    lane = lax.broadcasted_iota(jnp.int32, (TOK, 128), 1)
    token = lax.broadcasted_iota(jnp.int32, (TOK, 128), 0)
    eye = lax.broadcasted_iota(jnp.int32, (128, 128), 0) == lax.broadcasted_iota(
        jnp.int32, (128, 128), 1
    )
    for r in range(2):
        for j in range(2):
            row = jnp.broadcast_to(route[r, j : j + 1, :].astype(f32), (8, 8))
            col = jnp.sum(jnp.where(eye[0:8, 0:8], row, 0.0), axis=1, keepdims=True)
            route_tok[j, 8 * r : 8 * r + 8, :] = jnp.broadcast_to(col, (8, 128))
    lane_f = lane.astype(f32)
    member = jnp.logical_or(lane_f == route_tok[0], lane_f == route_tok[1])
    t_row = lax.broadcasted_iota(jnp.int32, (TOK, TOK), 0)
    t_col = lax.broadcasted_iota(jnp.int32, (TOK, TOK), 1)
    ahead = jnp.logical_and(t_col < t_row, (t_col >= 8) == (t_row >= 8))
    rank = mm(ahead.astype(f32).astype(bf16), member.astype(f32).astype(bf16), nn)
    slot = rank + jnp.where(token >= 8, 6.0, 1.0) + (10 * z).astype(f32)
    slot = jnp.where(member, slot, 0.0)
    gates[...] = jnp.zeros_like(gates)
    gates[:, 0:4] = mm(tok[...], router[...], nt)
    weight = jnp.where(member, jnp.exp(gates[...]), 0.0)
    gate = weight / jnp.sum(weight, axis=1, keepdims=True)
    gates[...] = gate
    a_high, a_low = parts_of(slot + pltpu.roll(gate, 4, 1))
    place = (lane == token + TOK * z).astype(f32).astype(bf16)
    info[...] = (mm(a_high, place, tn) + mm(a_low, place, tn))[0:8]
    zi[z] = info[...]
    zir = [[send(info, zi.at[z], right["z"])]]
    zil = [[send(info, zi.at[z], left["z"])]]

    ratio = jnp.exp(train_lp[...] - roll_lp[...])
    ratio = jnp.minimum(jnp.maximum(ratio, low[0]), high[0])
    coeff = -(ratio * adv[...]) / 2.0
    obj[...] = coeff * train_lp[...]
    for r in range(2):
        for part in range(2):
            row = jnp.broadcast_to(coeff[r : r + 1, 128 * part : 128 * part + 128], (128, 128))
            col = jnp.sum(jnp.where(eye, row, 0.0), axis=1, keepdims=True)
            coef[r, 128 * part : 128 * part + 128, :] = jnp.broadcast_to(col, (128, 128))
    here = pl.ds(pl.multiple_of(8 * (4 * z + y), 8), 8)
    for r in range(2):
        coef_tok[8 * r : 8 * r + 8, :] = coef[r, here, :]

    @pl.loop(0, D // 512)
    def _(i):
        cols = pl.ds(pl.multiple_of(i * 512, 512), 512)
        grad = moe[:, cols].astype(f32) * coef_tok[:, 0:1]
        grd[:, cols] = grad.astype(bf16)
        zg[z, :, cols] = grad.astype(bf16)

    pre[...] = jnp.zeros_like(pre)
    ugr[...] = jnp.zeros_like(ugr)
    summaries()
    fs = send(f_own, f_sib, sib)

    def z_hop(h, buf, rights, lefts, pieces):
        nr, nl = [], []
        for n, p in enumerate(pieces):
            rights[h - 1][n].wait_recv()
            if h < 4:
                at = (z + 8 - h) % 8
                nr.append(send(buf.at[at, :, p], buf.at[at, :, p], right["z"]))
            if h <= 3:
                lefts[h - 1][n].wait_recv()
                if h < 3:
                    at = (z + h) % 8
                    nl.append(send(buf.at[at, :, p], buf.at[at, :, p], left["z"]))
        rights.append(nr)
        lefts.append(nl)

    halves, whole = (col_a, col_b), (pl.ds(0, 128),)
    for h in range(1, 5):
        z_hop(h, zx, zxr, zxl, halves)
        z_hop(h, zi, zir, zil, whole)
    zgr = z_own(grd, zg, right["z"])
    zgl = z_own(grd, zg, left["z"])

    k = z // 2
    total = zi[0]
    for i in range(1, 8):
        total = total + zi[i]
    kind = lax.broadcasted_iota(jnp.int32, (8, 128), 0)
    slot_row = jnp.sum(jnp.where(kind == k, total, 0.0), axis=0, keepdims=True)
    gate_row = jnp.sum(jnp.where(kind == k + 4, total, 0.0), axis=0, keepdims=True)
    rows = lax.broadcasted_iota(jnp.int32, (CAP, 128), 0).astype(jnp.float32) + 1.0
    hot = (rows == jnp.broadcast_to(slot_row, (CAP, 128))).astype(jnp.float32)
    gate_slot = jnp.sum(hot * jnp.broadcast_to(gate_row, (CAP, 128)), axis=1, keepdims=True)
    psel[...] = hot.astype(jnp.bfloat16)

    def compact(buf, dst):
        @pl.loop(0, D // 512)
        def _(i):
            cols = pl.ds(pl.multiple_of(i * 512, 512), 512)
            block = buf[:, :, cols].reshape(8 * TOK, 512)
            dst[y, :, cols] = jnp.dot(
                psel[...], block, preferred_element_type=jnp.float32
            ).astype(jnp.bfloat16)

    def y_send(buf):
        ra = send(buf.at[y, :, col_a], buf.at[y, :, col_a], right["y"])
        lb = send(buf.at[y, :, col_b], buf.at[y, :, col_b], left["y"])
        rb = send(buf.at[y, :, col_b], buf.at[y, :, col_b], right["y"])
        la = send(buf.at[y, :, col_a], buf.at[y, :, col_a], left["y"])
        return ra, lb, rb, la

    def y_relay(buf, ra, lb):
        ra.wait_recv()
        fa = send(buf.at[ym, :, col_a], buf.at[ym, :, col_a], right["y"])
        lb.wait_recv()
        fb = send(buf.at[yp, :, col_b], buf.at[yp, :, col_b], left["y"])
        return fa, fb

    compact(zx, xa)
    yx = y_send(xa)
    z_hop(1, zg, zgr, zgl, halves)
    s_xm, s_xp, s_x2 = 2 * xm + c, 2 * xp + c, 2 * ((x + 2) % 4) + c
    wra.wait_recv()
    wfa = [send(wbuf.at[s_xm, q], wbuf.at[s_xm, q], right["x"]) for q in quarters_a]
    ws.append(send(wbuf.at[s_xm, half_a], wbuf.at[s_xm, half_a], sib))
    wlb.wait_recv()
    wfb = [send(wbuf.at[s_xp, q], wbuf.at[s_xp, q], left["x"]) for q in quarters_b]
    ws.append(send(wbuf.at[s_xp, half_b], wbuf.at[s_xp, half_b], sib))
    fs.wait_recv()
    chip_state(f_own, f_sib, f_chip, c == 1)
    far_send(f_chip, f_far, 0, 1)
    z_hop(2, zg, zgr, zgl, halves)
    z_hop(3, zg, zgr, zgl, halves)
    yxf = y_relay(xa, yx[0], yx[1])
    z_hop(4, zg, zgr, zgl, halves)
    compact(zg, ga)
    yg = y_send(ga)
    yx[2].wait_recv()
    yx[3].wait_recv()
    wrb.wait_recv()
    ws.append(send(wbuf.at[s_xm, half_b], wbuf.at[s_xm, half_b], sib))
    wla.wait_recv()
    ws.append(send(wbuf.at[s_xp, half_a], wbuf.at[s_xp, half_a], sib))
    yxf[0].wait_recv()
    yxf[1].wait_recv()

    def add_in(shard):
        cols = pl.ds(pl.multiple_of(shard * W_COLS, W_COLS), W_COLS)
        left_op = xa[:, :, cols].reshape(4 * CAP, W_COLS)
        for at, wide in ((0, 256), (256, 256), (512, 256), (768, 256), (1024, 128)):
            pre[:, at : at + wide] += mm(left_op, wbuf[shard, at : at + wide, :], nt)

    def add_out(shard):
        cols = pl.ds(pl.multiple_of(shard * W_COLS, W_COLS), W_COLS)
        left_op = ga[:, :, cols].reshape(4 * CAP, W_COLS)
        for at, wide in ((0, 256), (256, 256), (512, 64)):
            ugr[:, at : at + wide] += mm(left_op, wbuf[shard, N_IN + at : N_IN + at + wide, :], nt)

    for copy in ws:
        copy.wait_recv()
    ws_done = len(ws)

    @pl.loop(0, 6)
    def _(i):
        add_in((2 * (x + 3) + i) % 8)

    ygf = y_relay(ga, yg[0], yg[1])
    yg[2].wait_recv()
    yg[3].wait_recv()
    ygf[0].wait_recv()
    ygf[1].wait_recv()

    @pl.loop(0, 6)
    def _(i):
        add_out((2 * (x + 3) + i) % 8)

    for n in range(2):
        wfa[n].wait_recv()
        ws.append(send(wbuf.at[s_x2, quarters_a[n]], wbuf.at[s_x2, quarters_a[n]], sib))
        wfb[n].wait_recv()
        ws.append(send(wbuf.at[s_x2, quarters_b[n]], wbuf.at[s_x2, quarters_b[n]], sib))
    add_in(s_x2)
    add_out(s_x2)
    for copy in ws[ws_done:]:
        copy.wait_recv()
    s_x2o = 2 * ((x + 2) % 4) + 1 - c
    add_in(s_x2o)
    add_out(s_x2o)

    def grads(gate, up, unit):
        sig = jax.nn.sigmoid(gate)
        act = gate * sig
        up_grad = unit * act
        gate_grad = unit * up * sig * (1.0 + gate * (1.0 - sig))
        score = jnp.sum(act * up * unit, axis=1, keepdims=True)
        return gate_grad, up_grad, score

    @pl.loop(0, 4)
    def _(b):
        @pl.loop(0, CAP // TOK)
        def _(i):
            at = pl.multiple_of(b * CAP + i * TOK, TOK)
            r = pl.ds(at, TOK)
            gg, ug, s1 = grads(pre[r, 0:512], pre[r, 512:1024], ugr[r, 0:512])
            tail = pre[r, 1024:1152]
            ggt, ugt, s2 = grads(tail, pltpu.roll(tail, 64, 1), ugr[r, 512:640])
            ggu[r, 0:512] = gg.astype(jnp.bfloat16)
            ggu[r, 512:1024] = ug.astype(jnp.bfloat16)
            ggu[r, 1024:1152] = (ggt + pltpu.roll(ugt, 64, 1)).astype(jnp.bfloat16)
            score = jnp.where(lane == k, jnp.broadcast_to(s1 + s2, (TOK, 128)), 0.0)
            dxs[b, pl.ds(pl.multiple_of(i * TOK, TOK), TOK), D:D_EXT] = score.astype(jnp.bfloat16)

    def to_dx(shard):
        for at in (0, 256, 512):
            cols = pl.ds(pl.multiple_of(shard * W_COLS + at, 256), 256)
            part = mm(ggu[...], wbuf[shard, 0:N_IN, at : at + 256], nn)
            dxs[:, :, cols] = part.astype(bf16).reshape(4, CAP, 256)

    span = 2 * W_COLS
    group_a = [pl.ds(g * span, W_COLS) for g in range(4)]
    group_b = [pl.ds(g * span + W_COLS, W_COLS + (128 if g == 3 else 0)) for g in range(4)]
    group = [pl.ds(g * span, span + (128 if g == 3 else 0)) for g in range(4)]
    far_a, far_b, to_left, to_right, last_a, last_b = {}, {}, {}, {}, {}, {}

    def dx_group(g):
        @pl.loop(2 * g, 2 * g + 2)
        def _(i):
            to_dx(i)

        a, b = group_a[g], group_b[g]
        far_a[g] = send(dxs.at[y2, :, a], yh.at[:, a], right["y"])
        far_b[g] = send(dxs.at[y2, :, b], yh.at[:, b], left["y"])

    def direct(g):
        a, b = group_a[g], group_b[g]
        to_right[g] = send(dxs.at[yp, :, b], yfm.at[:, b], right["y"])
        to_left[g] = send(dxs.at[ym, :, a], yfp.at[:, a], left["y"])

    def add_cols(dst, cols):
        @pl.loop(0, cols.size // 128)
        def _(i):
            at = pl.ds(pl.multiple_of(cols.start + i * 128, 128), 128)
            dst[:, at] = (dst[:, at].astype(f32) + yh[:, at].astype(f32)).astype(bf16)

    def relayed(g):
        a, b = group_a[g], group_b[g]
        far_a[g].wait_recv()
        add_cols(dxs.at[yp], a)
        last_a[g] = send(dxs.at[yp, :, a], yfm.at[:, a], right["y"])
        far_b[g].wait_recv()
        add_cols(dxs.at[ym], b)
        last_b[g] = send(dxs.at[ym, :, b], yfp.at[:, b], left["y"])

    def spread(cols, wide, gated):
        part = dxs[y, :, cols].astype(f32) + yfp[:, cols].astype(f32) + yfm[:, cols].astype(f32)
        if gated:
            part = part * gate_slot
        cz[:, :, cols] = mm(psel[...], part.astype(bf16), tn).astype(bf16).reshape(8, TOK, wide)

    z_right, z_left = {}, {}

    def y_end(g):
        for copies in (to_left, to_right, last_a, last_b):
            copies[g].wait_recv()

        @pl.loop(0, span // 512)
        def _(i):
            spread(pl.ds(pl.multiple_of(g * span + i * 512, 512), 512), 512, True)

        if g == 3:
            spread(pl.ds(D, 128), 128, False)
        z_right[g] = [send(cz.at[(z + 4) % 8, :, group[g]], zr.at[0, :, group[g]], right["z"])]
        z_left[g] = [send(cz.at[(z + 5) % 8, :, group[g]], zl.at[0, :, group[g]], left["z"])]

    def z_add(at, src, cols):
        cz[at, :, cols] = (cz[at, :, cols].astype(f32) + src[:, cols].astype(f32)).astype(bf16)

    def z_step(g, h):
        cols = group[g]
        at = (z + 4 - h) % 8
        z_right[g][h - 1].wait_recv()
        z_add(at, zr.at[h - 1], cols)
        z_right[g].append(send(cz.at[at, :, cols], zr.at[h, :, cols], right["z"]))
        if h < 3:
            at = (z + 5 + h) % 8
            z_left[g][h - 1].wait_recv()
            z_add(at, zl.at[h - 1], cols)
            z_left[g].append(send(cz.at[at, :, cols], zl.at[h, :, cols], left["z"]))

    def z_end(g):
        cols = group[g]
        z_left[g][2].wait_recv()
        z_right[g][3].wait_recv()
        out[:, cols] = (
            cz[z, :, cols].astype(f32) + zr[3, :, cols].astype(f32) + zl[2, :, cols].astype(f32)
        )

    dx_group(0)
    direct(0)
    dx_group(1)
    relayed(0)
    direct(1)
    dx_group(2)
    relayed(1)
    direct(2)
    dx_group(3)
    relayed(2)
    direct(3)
    far_state(f_chip, f_far, f_sib, 0, 1, c == 1)
    attention_main(0, 2)
    y_end(0)
    relayed(3)
    attention_main(2, 4)
    bs = send(b_own, b_sib, sib)
    z_step(0, 1)
    y_end(1)
    bs.wait_recv()
    chip_state(b_own, b_sib, b_chip, c == 0)
    far_send(b_chip, b_far, 6, -1)
    z_step(0, 2)
    z_step(1, 1)
    z_step(0, 3)
    y_end(2)
    z_step(1, 2)
    z_end(0)
    z_step(2, 1)
    z_step(1, 3)
    y_end(3)
    z_step(2, 2)
    z_end(1)
    z_step(3, 1)
    z_step(2, 3)
    z_step(3, 2)
    far_state(b_chip, b_far, b_sib, 6, -1, c == 0)
    z_end(2)
    z_step(3, 3)
    attention_last()
    z_end(3)

    score = out[:, D:D_EXT]
    gate = gates[...]
    logit = gate * (score - jnp.sum(gate * score, axis=1, keepdims=True))
    l_high, l_low = parts_of(logit[:, 0:4])

    @pl.loop(0, D // 512)
    def _(i):
        cols = pl.ds(pl.multiple_of(i * 512, 512), 512)
        to_hidden = mm(l_high, router[:, cols], nn) + mm(l_low, router[:, cols], nn)
        gh[:, cols] = (out[:, cols] + to_hidden).astype(bf16)

    for copy in started:
        copy.wait_send()
    far_send(f_chip, f_far, 0, 1, finish=True)
    far_send(b_chip, b_far, 6, -1, finish=True)


def copy_out(*refs):
    n = len(refs) // 3
    sem = refs[-1]
    ins, outs, bufs = refs[:n], refs[n : 2 * n], refs[2 * n : 3 * n]
    arrive = [pltpu.make_async_copy(ins[i], bufs[i], sem.at[i]) for i in range(n)]
    leave = [pltpu.make_async_copy(bufs[i], outs[i], sem.at[n + i]) for i in range(n)]
    for copy in arrive:
        copy.start()
    for i in range(n):
        arrive[i].wait()
        leave[i].start()
    for copy in leave:
        copy.wait()


def results(*arrays):
    n = len(arrays)
    where = pl.BlockSpec(memory_space=pl.ANY)
    return pl.pallas_call(
        copy_out,
        out_shape=[jax.ShapeDtypeStruct(a.shape, a.dtype) for a in arrays],
        in_specs=[where] * n,
        out_specs=[where] * n,
        scratch_shapes=[pltpu.VMEM(a.shape, a.dtype) for a in arrays]
        + [pltpu.SemaphoreType.DMA((2 * n,))],
        name="results",
    )(*arrays)


def all_blocks(*operands):
    bf16, f32 = jnp.bfloat16, jnp.float32
    vmem, smem = (pl.BlockSpec(memory_space=m) for m in (pltpu.VMEM, pltpu.SMEM))
    hbm = pl.BlockSpec(memory_space=pl.ANY)
    n_copies = 118
    grads = jax.ShapeDtypeStruct((2, BLOCK, 2 * HEAD), bf16)
    states = pltpu.VMEM((2, 2, HEAD, HEAD), f32)
    return pl.pallas_call(
        kernel,
        out_shape=[
            jax.ShapeDtypeStruct((2, BLOCK), f32), jax.ShapeDtypeStruct((TOK, D), bf16),
            grads, grads, grads,
        ],
        in_specs=[vmem] * 4 + [hbm] * 3 + [vmem] * 4 + [smem] + [vmem] * 4 + [smem] * 2,
        out_specs=[vmem] * 5,
        scratch_shapes=[
            pltpu.VMEM((2, BLOCK, 128), f32),
            pltpu.VMEM((TOK, 128), f32),
            pltpu.VMEM((2, TOK, 128), f32),
            pltpu.VMEM((TOK, D), bf16),
            pltpu.VMEM((8, 128), f32),
            pltpu.VMEM((TOK, 128), f32),
            pltpu.VMEM((TOK, D_EXT), f32),
            pltpu.VMEM((8, N_ALL, W_COLS), bf16),
            pltpu.VMEM((8, TOK, D), bf16),
            pltpu.VMEM((8, TOK, D), bf16),
            pltpu.VMEM((8, 8, 128), f32),
            pltpu.VMEM((4, CAP, D), bf16),
            pltpu.VMEM((4, CAP, D), bf16),
            pltpu.VMEM((4 * CAP, N_IN), f32),
            pltpu.VMEM((4 * CAP, U_PAD), f32),
            pltpu.VMEM((4 * CAP, N_IN), bf16),
            pltpu.VMEM((4, CAP, D_EXT), bf16),
            pltpu.VMEM((CAP, D_EXT), bf16),
            pltpu.VMEM((CAP, D_EXT), bf16),
            pltpu.VMEM((CAP, D_EXT), bf16),
            pltpu.VMEM((8, TOK, D_EXT), bf16),
            pltpu.VMEM((4, TOK, D_EXT), bf16),
            pltpu.VMEM((3, TOK, D_EXT), bf16),
            pltpu.VMEM((CAP, 128), bf16),
            states, states, pltpu.VMEM((2, HEAD, HEAD), f32),
            states, states, pltpu.VMEM((2, HEAD, HEAD), f32),
            pltpu.VMEM((3, 2, 2, HEAD, HEAD), f32),
            pltpu.VMEM((3, 2, 2, HEAD, HEAD), f32),
            states,
            pltpu.VMEM((2, BLOCK, 2 * HEAD), f32),
            pltpu.VMEM((2, BLOCK, 2 * HEAD), f32),
            pltpu.SemaphoreType.DMA((n_copies,)),
            pltpu.SemaphoreType.DMA((n_copies,)),
            pltpu.SemaphoreType.DMA((5,)),
            pltpu.SemaphoreType.DMA((12,)),
            pltpu.SemaphoreType.DMA((12,)),
        ],
        compiler_params=pltpu.CompilerParams(
            collective_id=0, has_side_effects=True, vmem_limit_bytes=64 * 1024 * 1024 - 65536
        ),
        cost_estimate=pl.CostEstimate(
            flops=12 * 10**9, bytes_accessed=40 * 10**6, transcendentals=200000
        ),
        name="all_blocks",
    )(*operands)


def on_device(
    queries,
    key_rows,
    value_rows,
    decay_rate,
    norm_gain,
    attn_probe,
    hidden_in,
    moe_probe,
    router_weight,
    routes,
    gate_weight,
    up_weight,
    down_weight,
    rollout_logprob,
    trainer_logprob,
    advantage,
    clip_low,
    clip_high,
):
    rollouts, positions, width = hidden_in.shape
    objective, *rest = all_blocks(
        hidden_in.reshape(TOK, width), moe_probe.reshape(TOK, width), router_weight.T,
        routes.transpose(0, 2, 1), *(w.transpose(0, 2, 1) for w in (gate_weight, up_weight, down_weight)),
        queries, key_rows, value_rows, attn_probe, decay_rate, norm_gain.reshape(1, -1),
        rollout_logprob, trainer_logprob, advantage, clip_low, clip_high,
    )
    objective, grad_hidden, *grads = results(objective, *rest)
    return (objective, *grads, grad_hidden.reshape(rollouts, positions, width))


def solution(mesh):
    grid = Mesh(mesh.devices.reshape(4, 2, 8, 4), ("x", "c", "z", "y"))
    seq, exp = AXES_SEQ, AXES_EXPERT
    rows = P(None, seq, exp)
    toks = P(None, seq + exp, None)
    wts = P(exp, seq, None)
    in_specs = (
        rows, rows, rows, P(exp), P(exp), rows, toks, toks, P(), toks, wts, wts, wts,
        P(None, seq), P(None, seq), P(None, seq), P(), P(),
    )
    out_specs = (P(None, seq), rows, rows, rows, toks)
    return jax.shard_map(
        on_device, mesh=grid, in_specs=in_specs, out_specs=out_specs, check_vma=False
    )
```

```python
import jax
import jax.numpy as jnp
from jax import lax
from jax.experimental import pallas as pl
from jax.experimental.pallas import tpu as pltpu
from jax.sharding import Mesh, PartitionSpec as P

norm_epsilon = 1e-06
MESH = pl.DeviceIdType.MESH
AXES_SEQ = ("x", "c")
AXES_EXPERT = ("z", "y")

D = 6144
W_COLS = 768
UNITS = 576
H_MAIN = 512
N_IN = 1152
N_ALL = 1728
U_PAD = 640
TOK = 16
CAP = 80
HALF = 3072
BLOCK, HEAD = 256, 128
D_EXT = D + 128


def kernel(
    tok, moe, router, route, gate_w, up_w, down_w, qr, kr, vr, pr, rate, gain,
    roll_lp, train_lp, adv, low, high,
    obj, gh, gq, gk, gv,
    coef, coef_tok, route_tok, grd, info, gates, out,
    wbuf, zx, zg, zi, xa, ga, pre, ugr, ggu, dxs, yh, yfp, yfm, cz, zr, zl, psel,
    f_own, f_sib, f_chip, b_own, b_sib, b_chip, f_far, b_far, state, dk_part, dv_part,
    ssem, rsem, lsem, xss, xrs,
):
    x, c, z, y = (lax.axis_index(a) for a in ("x", "c", "z", "y"))
    xp, xm = (x + 1) % 4, (x + 3) % 4
    yp, ym, y2 = (y + 1) % 4, (y + 3) % 4, (y + 2) % 4
    zp, zm = (z + 1) % 8, (z + 7) % 8
    right = {"x": {"x": xp}, "y": {"y": yp}, "z": {"z": zp}}
    left = {"x": {"x": xm}, "y": {"y": ym}, "z": {"z": zm}}
    sib = {"c": 1 - c}
    me = 2 * x + c
    started = []

    def send(src, dst, dev):
        at = len(started)
        copy = pltpu.make_async_remote_copy(
            src_ref=src, dst_ref=dst, send_sem=ssem.at[at], recv_sem=rsem.at[at],
            device_id=dev, device_id_type=MESH,
        )
        copy.start()
        started.append(copy)
        return copy

    raw = [
        pltpu.make_async_copy(
            w.at[0, pl.ds(src, n)], wbuf.at[me, pl.ds(dst, n)], lsem.at[i]
        )
        for i, (w, src, dst, n) in enumerate((
            (gate_w, 0, 0, H_MAIN),
            (up_w, 0, H_MAIN, H_MAIN),
            (gate_w, H_MAIN, 2 * H_MAIN, UNITS - H_MAIN),
            (up_w, H_MAIN, H_MAIN + UNITS, UNITS - H_MAIN),
            (down_w, 0, N_IN, UNITS),
        ))
    ]
    for copy in raw:
        copy.start()
    barrier = pltpu.get_barrier_semaphore()
    peers = [right[a] for a in "xyz"] + [left[a] for a in "xyz"] + [sib]
    peers += [{"x": xp, "c": 1 - c}, {"x": xm, "c": 1 - c}, {"x": (x + 2) % 4}]
    peers += [{"x": (x + 2) % 4, "c": 1 - c}]
    for peer in peers:
        pl.semaphore_signal(barrier, inc=1, device_id=peer, device_id_type=MESH)
    pl.semaphore_wait(barrier, len(peers))

    col_a, col_b = pl.ds(0, HALF), pl.ds(HALF, HALF)
    zx[z] = tok[...]

    def z_own(src, dst, dev):
        return [[send(src.at[:, p], dst.at[z, :, p], dev) for p in (col_a, col_b)]]

    zxr = z_own(tok, zx, right["z"])
    zxl = z_own(tok, zx, left["z"])

    half = N_ALL // 2
    half_a, half_b = pl.ds(0, half), pl.ds(half, half)
    quarters_a = pl.ds(0, half // 2), pl.ds(half // 2, half // 2)
    quarters_b = pl.ds(half, half // 2), pl.ds(half + half // 2, half // 2)
    for copy in raw:
        copy.wait()
    wra = send(wbuf.at[me, half_a], wbuf.at[me, half_a], right["x"])
    wlb = send(wbuf.at[me, half_b], wbuf.at[me, half_b], left["x"])
    wrb = send(wbuf.at[me, half_b], wbuf.at[me, half_b], right["x"])
    wla = send(wbuf.at[me, half_a], wbuf.at[me, half_a], left["x"])
    ws = [send(wbuf.at[me], wbuf.at[me], sib)]

    f32, bf16 = jnp.float32, jnp.bfloat16
    nn, nt, tn = (((1,), (0,)), ((), ())), (((1,), (1,)), ((), ())), (((0,), (0,)), ((), ()))

    def mm(a, b, dims):
        return lax.dot_general(a, b, dims, preferred_element_type=f32)

    def parts_of(v):
        high = v.astype(bf16)
        return high, (v - high.astype(f32)).astype(bf16)

    def row_decay(h, sign, shift):
        row = lax.broadcasted_iota(jnp.int32, (BLOCK, HEAD), 0).astype(f32)
        return jnp.exp(-rate[h] * (sign * row + shift))

    def lanes(h):
        return pl.ds(pl.multiple_of(h * HEAD, HEAD), HEAD)

    def block_decay(h, blocks):
        return jnp.exp(jnp.full((HEAD, HEAD), -rate[h] * (BLOCK * blocks), f32))

    def summaries():
        @pl.loop(0, 4)
        def _(i):
            r, h = i // 2, i % 2
            v_high, v_low = parts_of(vr[r, :, lanes(h)].astype(f32) * row_decay(h, -1.0, BLOCK - 1.0))
            key = kr[r, :, lanes(h)]
            f_own[r, h] = mm(key, v_high, tn) + mm(key, v_low, tn)

    def chip_state(own_ref, sib_ref, chip_ref, near_is_own):
        for h in range(2):
            mine, other = own_ref[c, h], sib_ref[c, h]
            near = jnp.where(near_is_own, mine, other)
            far = jnp.where(near_is_own, other, mine)
            chip_ref[h] = near + block_decay(h, 1) * far

    def far_copy(chip_ref, far_ref, base, dx, cc, to):
        return pltpu.make_async_remote_copy(
            src_ref=chip_ref, dst_ref=far_ref.at[dx - 1, c],
            send_sem=xss.at[base + 2 * (dx - 1) + cc], recv_sem=xrs.at[base + 2 * (dx - 1) + c],
            device_id={"x": to, "c": cc}, device_id_type=MESH,
        )

    def far_send(chip_ref, far_ref, base, step, finish=False):
        for dx in (1, 2, 3):
            to = x + step * dx

            @pl.when(jnp.logical_and(to >= 0, to < 4))
            def _():
                for cc in (0, 1):
                    copy = far_copy(chip_ref, far_ref, base, dx, cc, to)
                    if finish:
                        copy.wait_send()
                    else:
                        copy.start()

    def far_state(chip_ref, far_ref, sib_ref, base, step, with_sib):
        for dx in (1, 2, 3):
            at = x - step * dx
            there = jnp.logical_and(at >= 0, at < 4)

            @pl.when(there)
            def _():
                for r in (0, 1):
                    pltpu.make_async_remote_copy(
                        src_ref=chip_ref, dst_ref=far_ref.at[dx - 1, r],
                        send_sem=xss.at[base + 2 * (dx - 1) + r],
                        recv_sem=xrs.at[base + 2 * (dx - 1) + r],
                        device_id={"x": (x + 1) % 4, "c": r}, device_id_type=MESH,
                    ).wait_recv()

            @pl.when(jnp.logical_not(there))
            def _():
                far_ref[dx - 1] = jnp.zeros_like(far_ref[dx - 1])

        for r in range(2):
            for h in range(2):
                two = block_decay(h, 2)
                far = far_ref[0, r, h] + two * (far_ref[1, r, h] + two * far_ref[2, r, h])
                near = sib_ref[r, h] + block_decay(h, 1) * far
                state[r, h] = jnp.where(with_sib, near, far)

    def attention_main(first, end):
        @pl.loop(first, end)
        def _(i):
            r, h = i // 2, i % 2
            query, key, value = qr[r, :, lanes(h)], kr[r, :, lanes(h)], vr[r, :, lanes(h)]
            at_i = lax.broadcasted_iota(jnp.int32, (BLOCK, BLOCK), 0)
            at_j = lax.broadcasted_iota(jnp.int32, (BLOCK, BLOCK), 1)
            apart = jnp.maximum(at_i - at_j, 0).astype(f32)
            within = jnp.where(at_i >= at_j, jnp.exp(-rate[h] * apart), 0.0)
            s_high, s_low = parts_of(mm(query, key, nt) * within)
            t_high, t_low = parts_of(state[r, h])
            lead = row_decay(h, 1.0, 1.0)
            attn = mm(s_high, value, nn) + mm(s_low, value, nn)
            attn = attn + lead * (mm(query, t_high, nn) + mm(query, t_low, nn))
            inverse = lax.rsqrt(jnp.mean(attn * attn, axis=1, keepdims=True) + norm_epsilon)
            scaled = gain[:, lanes(h)] * (coef[r] * pr[r, :, lanes(h)].astype(f32))
            along = jnp.mean(scaled * attn, axis=1, keepdims=True)
            grad = inverse * scaled - attn * (inverse * inverse * inverse * along)
            g_high, g_low = parts_of(grad)
            d_high, d_low = parts_of(grad * row_decay(h, 1.0, 0.0))
            b_own[r, h] = mm(query, d_high, tn) + mm(query, d_low, tn)
            p_high, p_low = parts_of((mm(g_high, value, nt) + mm(g_low, value, nt)) * within)
            dq = mm(p_high, key, nn) + mm(p_low, key, nn)
            dq = dq + lead * (mm(g_high, t_high, nt) + mm(g_low, t_high, nt) + mm(g_high, t_low, nt))
            gq[r, :, lanes(h)] = dq.astype(bf16)
            dk_part[r, :, lanes(h)] = mm(p_high, query, tn) + mm(p_low, query, tn)
            dv_part[r, :, lanes(h)] = (
                mm(s_high, g_high, tn) + mm(s_low, g_high, tn) + mm(s_high, g_low, tn)
            )

    def attention_last():
        @pl.loop(0, 4)
        def _(i):
            r, h = i // 2, i % 2
            key, value = kr[r, :, lanes(h)], vr[r, :, lanes(h)]
            t_high, t_low = parts_of(state[r, h])
            tail = row_decay(h, -1.0, float(BLOCK))
            dk = dk_part[r, :, lanes(h)] + tail * (mm(value, t_high, nt) + mm(value, t_low, nt))
            dv = dv_part[r, :, lanes(h)] + tail * (mm(key, t_high, nn) + mm(key, t_low, nn))
            gk[r, :, lanes(h)] = dk.astype(bf16)
            gv[r, :, lanes(h)] = dv.astype(bf16)

    lane = lax.broadcasted_iota(jnp.int32, (TOK, 128), 1)
    token = lax.broadcasted_iota(jnp.int32, (TOK, 128), 0)
    eye = lax.broadcasted_iota(jnp.int32, (128, 128), 0) == lax.broadcasted_iota(
        jnp.int32, (128, 128), 1
    )
    for r in range(2):
        for j in range(2):
            row = jnp.broadcast_to(route[r, j : j + 1, :].astype(f32), (8, 8))
            col = jnp.sum(jnp.where(eye[0:8, 0:8], row, 0.0), axis=1, keepdims=True)
            route_tok[j, 8 * r : 8 * r + 8, :] = jnp.broadcast_to(col, (8, 128))
    lane_f = lane.astype(f32)
    member = jnp.logical_or(lane_f == route_tok[0], lane_f == route_tok[1])
    t_row = lax.broadcasted_iota(jnp.int32, (TOK, TOK), 0)
    t_col = lax.broadcasted_iota(jnp.int32, (TOK, TOK), 1)
    ahead = jnp.logical_and(t_col < t_row, (t_col >= 8) == (t_row >= 8))
    rank = mm(ahead.astype(f32).astype(bf16), member.astype(f32).astype(bf16), nn)
    slot = rank + jnp.where(token >= 8, 6.0, 1.0) + (10 * z).astype(f32)
    slot = jnp.where(member, slot, 0.0)
    gates[...] = jnp.zeros_like(gates)
    gates[:, 0:4] = mm(tok[...], router[...], nt)
    weight = jnp.where(member, jnp.exp(gates[...]), 0.0)
    gate = weight / jnp.sum(weight, axis=1, keepdims=True)
    gates[...] = gate
    a_high, a_low = parts_of(slot + pltpu.roll(gate, 4, 1))
    place = (lane == token + TOK * z).astype(f32).astype(bf16)
    info[...] = (mm(a_high, place, tn) + mm(a_low, place, tn))[0:8]
    zi[z] = info[...]
    zir = [[send(info, zi.at[z], right["z"])]]
    zil = [[send(info, zi.at[z], left["z"])]]

    def z_hop(h, buf, rights, lefts, pieces):
        nr, nl = [], []
        for n, p in enumerate(pieces):
            rights[h - 1][n].wait_recv()
            if h < 4:
                at = (z + 8 - h) % 8
                nr.append(send(buf.at[at, :, p], buf.at[at, :, p], right["z"]))
            if h <= 3:
                lefts[h - 1][n].wait_recv()
                if h < 3:
                    at = (z + h) % 8
                    nl.append(send(buf.at[at, :, p], buf.at[at, :, p], left["z"]))
        rights.append(nr)
        lefts.append(nl)

    halves, whole = (col_a, col_b), (pl.ds(0, 128),)
    for h in range(1, 5):
        z_hop(h, zx, zxr, zxl, halves)
        z_hop(h, zi, zir, zil, whole)

    k = z // 2
    total = zi[0]
    for i in range(1, 8):
        total = total + zi[i]
    kind = lax.broadcasted_iota(jnp.int32, (8, 128), 0)
    slot_row = jnp.sum(jnp.where(kind == k, total, 0.0), axis=0, keepdims=True)
    gate_row = jnp.sum(jnp.where(kind == k + 4, total, 0.0), axis=0, keepdims=True)
    rows = lax.broadcasted_iota(jnp.int32, (CAP, 128), 0).astype(jnp.float32) + 1.0
    hot = (rows == jnp.broadcast_to(slot_row, (CAP, 128))).astype(jnp.float32)
    gate_slot = jnp.sum(hot * jnp.broadcast_to(gate_row, (CAP, 128)), axis=1, keepdims=True)
    psel[...] = hot.astype(jnp.bfloat16)

    def compact(buf, dst):
        @pl.loop(0, D // 512)
        def _(i):
            cols = pl.ds(pl.multiple_of(i * 512, 512), 512)
            block = buf[:, :, cols].reshape(8 * TOK, 512)
            dst[y, :, cols] = jnp.dot(
                psel[...], block, preferred_element_type=jnp.float32
            ).astype(jnp.bfloat16)

    def y_send(buf):
        ra = send(buf.at[y, :, col_a], buf.at[y, :, col_a], right["y"])
        lb = send(buf.at[y, :, col_b], buf.at[y, :, col_b], left["y"])
        rb = send(buf.at[y, :, col_b], buf.at[y, :, col_b], right["y"])
        la = send(buf.at[y, :, col_a], buf.at[y, :, col_a], left["y"])
        return ra, lb, rb, la

    def y_relay(buf, ra, lb):
        ra.wait_recv()
        fa = send(buf.at[ym, :, col_a], buf.at[ym, :, col_a], right["y"])
        lb.wait_recv()
        fb = send(buf.at[yp, :, col_b], buf.at[yp, :, col_b], left["y"])
        return fa, fb

    compact(zx, xa)
    yx = y_send(xa)

    ratio = jnp.exp(train_lp[...] - roll_lp[...])
    ratio = jnp.minimum(jnp.maximum(ratio, low[0]), high[0])
    coeff = -(ratio * adv[...]) / 2.0
    obj[...] = coeff * train_lp[...]
    for r in range(2):
        for part in range(2):
            row = jnp.broadcast_to(coeff[r : r + 1, 128 * part : 128 * part + 128], (128, 128))
            col = jnp.sum(jnp.where(eye, row, 0.0), axis=1, keepdims=True)
            coef[r, 128 * part : 128 * part + 128, :] = jnp.broadcast_to(col, (128, 128))
    here = pl.ds(pl.multiple_of(8 * (4 * z + y), 8), 8)
    for r in range(2):
        coef_tok[8 * r : 8 * r + 8, :] = coef[r, here, :]

    @pl.loop(0, D // 512)
    def _(i):
        cols = pl.ds(pl.multiple_of(i * 512, 512), 512)
        grad = moe[:, cols].astype(f32) * coef_tok[:, 0:1]
        grd[:, cols] = grad.astype(bf16)
        zg[z, :, cols] = grad.astype(bf16)

    zgr = z_own(grd, zg, right["z"])
    zgl = z_own(grd, zg, left["z"])
    pre[...] = jnp.zeros_like(pre)
    ugr[...] = jnp.zeros_like(ugr)
    summaries()
    fs = send(f_own, f_sib, sib)
    z_hop(1, zg, zgr, zgl, halves)
    s_xm, s_xp, s_x2 = 2 * xm + c, 2 * xp + c, 2 * ((x + 2) % 4) + c
    wra.wait_recv()
    wfa = [send(wbuf.at[s_xm, q], wbuf.at[s_xm, q], right["x"]) for q in quarters_a]
    ws.append(send(wbuf.at[s_xm, half_a], wbuf.at[s_xm, half_a], sib))
    wlb.wait_recv()
    wfb = [send(wbuf.at[s_xp, q], wbuf.at[s_xp, q], left["x"]) for q in quarters_b]
    ws.append(send(wbuf.at[s_xp, half_b], wbuf.at[s_xp, half_b], sib))
    fs.wait_recv()
    chip_state(f_own, f_sib, f_chip, c == 1)
    far_send(f_chip, f_far, 0, 1)
    z_hop(2, zg, zgr, zgl, halves)
    z_hop(3, zg, zgr, zgl, halves)
    yxf = y_relay(xa, yx[0], yx[1])
    z_hop(4, zg, zgr, zgl, halves)
    compact(zg, ga)
    yg = y_send(ga)
    yx[2].wait_recv()
    yx[3].wait_recv()
    wrb.wait_recv()
    ws.append(send(wbuf.at[s_xm, half_b], wbuf.at[s_xm, half_b], sib))
    wla.wait_recv()
    ws.append(send(wbuf.at[s_xp, half_a], wbuf.at[s_xp, half_a], sib))
    yxf[0].wait_recv()
    yxf[1].wait_recv()

    def add_in(shard):
        cols = pl.ds(pl.multiple_of(shard * W_COLS, W_COLS), W_COLS)
        left_op = xa[:, :, cols].reshape(4 * CAP, W_COLS)
        for at, wide in ((0, 256), (256, 256), (512, 256), (768, 256), (1024, 128)):
            pre[:, at : at + wide] += mm(left_op, wbuf[shard, at : at + wide, :], nt)

    def add_out(shard):
        cols = pl.ds(pl.multiple_of(shard * W_COLS, W_COLS), W_COLS)
        left_op = ga[:, :, cols].reshape(4 * CAP, W_COLS)
        for at, wide in ((0, 256), (256, 256), (512, 64)):
            ugr[:, at : at + wide] += mm(left_op, wbuf[shard, N_IN + at : N_IN + at + wide, :], nt)

    for copy in ws:
        copy.wait_recv()
    ws_done = len(ws)

    @pl.loop(0, 6)
    def _(i):
        add_in((2 * (x + 3) + i) % 8)

    ygf = y_relay(ga, yg[0], yg[1])
    yg[2].wait_recv()
    yg[3].wait_recv()
    ygf[0].wait_recv()
    ygf[1].wait_recv()

    @pl.loop(0, 6)
    def _(i):
        add_out((2 * (x + 3) + i) % 8)

    for n in range(2):
        wfa[n].wait_recv()
        ws.append(send(wbuf.at[s_x2, quarters_a[n]], wbuf.at[s_x2, quarters_a[n]], sib))
        wfb[n].wait_recv()
        ws.append(send(wbuf.at[s_x2, quarters_b[n]], wbuf.at[s_x2, quarters_b[n]], sib))
    add_in(s_x2)
    add_out(s_x2)
    for copy in ws[ws_done:]:
        copy.wait_recv()
    s_x2o = 2 * ((x + 2) % 4) + 1 - c
    add_in(s_x2o)
    add_out(s_x2o)

    def grads(gate, up, unit):
        sig = jax.nn.sigmoid(gate)
        act = gate * sig
        up_grad = unit * act
        gate_grad = unit * up * sig * (1.0 + gate * (1.0 - sig))
        score = jnp.sum(act * up * unit, axis=1, keepdims=True)
        return gate_grad, up_grad, score

    @pl.loop(0, 4)
    def _(b):
        @pl.loop(0, CAP // TOK)
        def _(i):
            at = pl.multiple_of(b * CAP + i * TOK, TOK)
            r = pl.ds(at, TOK)
            gg, ug, s1 = grads(pre[r, 0:512], pre[r, 512:1024], ugr[r, 0:512])
            tail = pre[r, 1024:1152]
            ggt, ugt, s2 = grads(tail, pltpu.roll(tail, 64, 1), ugr[r, 512:640])
            ggu[r, 0:512] = gg.astype(jnp.bfloat16)
            ggu[r, 512:1024] = ug.astype(jnp.bfloat16)
            ggu[r, 1024:1152] = (ggt + pltpu.roll(ugt, 64, 1)).astype(jnp.bfloat16)
            score = jnp.where(lane == k, jnp.broadcast_to(s1 + s2, (TOK, 128)), 0.0)
            dxs[b, pl.ds(pl.multiple_of(i * TOK, TOK), TOK), D:D_EXT] = score.astype(jnp.bfloat16)

    def to_dx(shard):
        for at in (0, 256, 512):
            cols = pl.ds(pl.multiple_of(shard * W_COLS + at, 256), 256)
            part = mm(ggu[...], wbuf[shard, 0:N_IN, at : at + 256], nn)
            dxs[:, :, cols] = part.astype(bf16).reshape(4, CAP, 256)

    span = 2 * W_COLS
    group_a = [pl.ds(g * span, W_COLS) for g in range(4)]
    group_b = [pl.ds(g * span + W_COLS, W_COLS + (128 if g == 3 else 0)) for g in range(4)]
    group = [pl.ds(g * span, span + (128 if g == 3 else 0)) for g in range(4)]
    far_a, far_b, to_left, to_right, last_a, last_b = {}, {}, {}, {}, {}, {}

    def dx_group(g):
        @pl.loop(2 * g, 2 * g + 2)
        def _(i):
            to_dx(i)

        a, b = group_a[g], group_b[g]
        far_a[g] = send(dxs.at[y2, :, a], yh.at[:, a], right["y"])
        far_b[g] = send(dxs.at[y2, :, b], yh.at[:, b], left["y"])

    def direct(g):
        a, b = group_a[g], group_b[g]
        to_right[g] = send(dxs.at[yp, :, b], yfm.at[:, b], right["y"])
        to_left[g] = send(dxs.at[ym, :, a], yfp.at[:, a], left["y"])

    def add_cols(dst, cols):
        @pl.loop(0, cols.size // 128)
        def _(i):
            at = pl.ds(pl.multiple_of(cols.start + i * 128, 128), 128)
            dst[:, at] = (dst[:, at].astype(f32) + yh[:, at].astype(f32)).astype(bf16)

    def relayed(g):
        a, b = group_a[g], group_b[g]
        far_a[g].wait_recv()
        add_cols(dxs.at[yp], a)
        last_a[g] = send(dxs.at[yp, :, a], yfm.at[:, a], right["y"])
        far_b[g].wait_recv()
        add_cols(dxs.at[ym], b)
        last_b[g] = send(dxs.at[ym, :, b], yfp.at[:, b], left["y"])

    def spread(cols, wide, gated):
        part = dxs[y, :, cols].astype(f32) + yfp[:, cols].astype(f32) + yfm[:, cols].astype(f32)
        if gated:
            part = part * gate_slot
        cz[:, :, cols] = mm(psel[...], part.astype(bf16), tn).astype(bf16).reshape(8, TOK, wide)

    z_right, z_left = {}, {}

    def y_end(g):
        for copies in (to_left, to_right, last_a, last_b):
            copies[g].wait_recv()

        @pl.loop(0, span // 512)
        def _(i):
            spread(pl.ds(pl.multiple_of(g * span + i * 512, 512), 512), 512, True)

        if g == 3:
            spread(pl.ds(D, 128), 128, False)
        z_right[g] = [send(cz.at[(z + 4) % 8, :, group[g]], zr.at[0, :, group[g]], right["z"])]
        z_left[g] = [send(cz.at[(z + 5) % 8, :, group[g]], zl.at[0, :, group[g]], left["z"])]

    def z_add(at, src, cols):
        cz[at, :, cols] = (cz[at, :, cols].astype(f32) + src[:, cols].astype(f32)).astype(bf16)

    def z_step(g, h):
        cols = group[g]
        at = (z + 4 - h) % 8
        z_right[g][h - 1].wait_recv()
        z_add(at, zr.at[h - 1], cols)
        z_right[g].append(send(cz.at[at, :, cols], zr.at[h, :, cols], right["z"]))
        if h < 3:
            at = (z + 5 + h) % 8
            z_left[g][h - 1].wait_recv()
            z_add(at, zl.at[h - 1], cols)
            z_left[g].append(send(cz.at[at, :, cols], zl.at[h, :, cols], left["z"]))

    def z_end(g):
        cols = group[g]
        z_left[g][2].wait_recv()
        z_right[g][3].wait_recv()
        out[:, cols] = (
            cz[z, :, cols].astype(f32) + zr[3, :, cols].astype(f32) + zl[2, :, cols].astype(f32)
        )

    dx_group(0)
    direct(0)
    dx_group(1)
    relayed(0)
    direct(1)
    dx_group(2)
    relayed(1)
    direct(2)
    dx_group(3)
    far_state(f_chip, f_far, f_sib, 0, 1, c == 1)
    attention_main(0, 1)
    y_end(0)
    attention_main(1, 2)
    z_step(0, 1)
    relayed(2)
    direct(3)
    attention_main(2, 3)
    z_step(0, 2)
    y_end(1)
    attention_main(3, 4)
    bs = send(b_own, b_sib, sib)
    z_step(0, 3)
    z_step(1, 1)
    relayed(3)
    bs.wait_recv()
    chip_state(b_own, b_sib, b_chip, c == 0)
    far_send(b_chip, b_far, 6, -1)
    z_end(0)
    z_step(1, 2)
    y_end(2)
    z_step(1, 3)
    z_step(2, 1)
    z_end(1)
    z_step(2, 2)
    y_end(3)
    z_step(2, 3)
    z_step(3, 1)
    z_end(2)
    z_step(3, 2)
    z_step(3, 3)
    far_state(b_chip, b_far, b_sib, 6, -1, c == 0)
    attention_last()
    z_end(3)

    score = out[:, D:D_EXT]
    gate = gates[...]
    logit = gate * (score - jnp.sum(gate * score, axis=1, keepdims=True))
    l_high, l_low = parts_of(logit[:, 0:4])

    @pl.loop(0, D // 512)
    def _(i):
        cols = pl.ds(pl.multiple_of(i * 512, 512), 512)
        to_hidden = mm(l_high, router[:, cols], nn) + mm(l_low, router[:, cols], nn)
        gh[:, cols] = (out[:, cols] + to_hidden).astype(bf16)

    for copy in started:
        copy.wait_send()
    far_send(f_chip, f_far, 0, 1, finish=True)
    far_send(b_chip, b_far, 6, -1, finish=True)


def copy_out(*refs):
    n = len(refs) // 3
    sem = refs[-1]
    ins, outs, bufs = refs[:n], refs[n : 2 * n], refs[2 * n : 3 * n]
    arrive = [pltpu.make_async_copy(ins[i], bufs[i], sem.at[i]) for i in range(n)]
    leave = [pltpu.make_async_copy(bufs[i], outs[i], sem.at[n + i]) for i in range(n)]
    for copy in arrive:
        copy.start()
    for i in range(n):
        arrive[i].wait()
        leave[i].start()
    for copy in leave:
        copy.wait()


def results(*arrays):
    n = len(arrays)
    where = pl.BlockSpec(memory_space=pl.ANY)
    return pl.pallas_call(
        copy_out,
        out_shape=[jax.ShapeDtypeStruct(a.shape, a.dtype) for a in arrays],
        in_specs=[where] * n,
        out_specs=[where] * n,
        scratch_shapes=[pltpu.VMEM(a.shape, a.dtype) for a in arrays]
        + [pltpu.SemaphoreType.DMA((2 * n,))],
        name="results",
    )(*arrays)


def all_blocks(*operands):
    bf16, f32 = jnp.bfloat16, jnp.float32
    vmem, smem = (pl.BlockSpec(memory_space=m) for m in (pltpu.VMEM, pltpu.SMEM))
    hbm = pl.BlockSpec(memory_space=pl.ANY)
    n_copies = 118
    grads = jax.ShapeDtypeStruct((2, BLOCK, 2 * HEAD), bf16)
    states = pltpu.VMEM((2, 2, HEAD, HEAD), f32)
    return pl.pallas_call(
        kernel,
        out_shape=[
            jax.ShapeDtypeStruct((2, BLOCK), f32), jax.ShapeDtypeStruct((TOK, D), bf16),
            grads, grads, grads,
        ],
        in_specs=[vmem] * 4 + [hbm] * 3 + [vmem] * 4 + [smem] + [vmem] * 4 + [smem] * 2,
        out_specs=[vmem] * 5,
        scratch_shapes=[
            pltpu.VMEM((2, BLOCK, 128), f32),
            pltpu.VMEM((TOK, 128), f32),
            pltpu.VMEM((2, TOK, 128), f32),
            pltpu.VMEM((TOK, D), bf16),
            pltpu.VMEM((8, 128), f32),
            pltpu.VMEM((TOK, 128), f32),
            pltpu.VMEM((TOK, D_EXT), f32),
            pltpu.VMEM((8, N_ALL, W_COLS), bf16),
            pltpu.VMEM((8, TOK, D), bf16),
            pltpu.VMEM((8, TOK, D), bf16),
            pltpu.VMEM((8, 8, 128), f32),
            pltpu.VMEM((4, CAP, D), bf16),
            pltpu.VMEM((4, CAP, D), bf16),
            pltpu.VMEM((4 * CAP, N_IN), f32),
            pltpu.VMEM((4 * CAP, U_PAD), f32),
            pltpu.VMEM((4 * CAP, N_IN), bf16),
            pltpu.VMEM((4, CAP, D_EXT), bf16),
            pltpu.VMEM((CAP, D_EXT), bf16),
            pltpu.VMEM((CAP, D_EXT), bf16),
            pltpu.VMEM((CAP, D_EXT), bf16),
            pltpu.VMEM((8, TOK, D_EXT), bf16),
            pltpu.VMEM((4, TOK, D_EXT), bf16),
            pltpu.VMEM((3, TOK, D_EXT), bf16),
            pltpu.VMEM((CAP, 128), bf16),
            states, states, pltpu.VMEM((2, HEAD, HEAD), f32),
            states, states, pltpu.VMEM((2, HEAD, HEAD), f32),
            pltpu.VMEM((3, 2, 2, HEAD, HEAD), f32),
            pltpu.VMEM((3, 2, 2, HEAD, HEAD), f32),
            states,
            pltpu.VMEM((2, BLOCK, 2 * HEAD), f32),
            pltpu.VMEM((2, BLOCK, 2 * HEAD), f32),
            pltpu.SemaphoreType.DMA((n_copies,)),
            pltpu.SemaphoreType.DMA((n_copies,)),
            pltpu.SemaphoreType.DMA((5,)),
            pltpu.SemaphoreType.DMA((12,)),
            pltpu.SemaphoreType.DMA((12,)),
        ],
        compiler_params=pltpu.CompilerParams(
            collective_id=0, has_side_effects=True, vmem_limit_bytes=64 * 1024 * 1024 - 65536
        ),
        cost_estimate=pl.CostEstimate(
            flops=12 * 10**9, bytes_accessed=40 * 10**6, transcendentals=200000
        ),
        name="all_blocks",
    )(*operands)


def on_device(
    queries,
    key_rows,
    value_rows,
    decay_rate,
    norm_gain,
    attn_probe,
    hidden_in,
    moe_probe,
    router_weight,
    routes,
    gate_weight,
    up_weight,
    down_weight,
    rollout_logprob,
    trainer_logprob,
    advantage,
    clip_low,
    clip_high,
):
    rollouts, positions, width = hidden_in.shape
    objective, *rest = all_blocks(
        hidden_in.reshape(TOK, width), moe_probe.reshape(TOK, width), router_weight.T,
        routes.transpose(0, 2, 1), *(w.transpose(0, 2, 1) for w in (gate_weight, up_weight, down_weight)),
        queries, key_rows, value_rows, attn_probe, decay_rate, norm_gain.reshape(1, -1),
        rollout_logprob, trainer_logprob, advantage, clip_low, clip_high,
    )
    objective, grad_hidden, *grads = results(objective, *rest)
    return (objective, *grads, grad_hidden.reshape(rollouts, positions, width))


def solution(mesh):
    grid = Mesh(mesh.devices.reshape(4, 2, 8, 4), ("x", "c", "z", "y"))
    seq, exp = AXES_SEQ, AXES_EXPERT
    rows = P(None, seq, exp)
    toks = P(None, seq + exp, None)
    wts = P(exp, seq, None)
    in_specs = (
        rows, rows, rows, P(exp), P(exp), rows, toks, toks, P(), toks, wts, wts, wts,
        P(None, seq), P(None, seq), P(None, seq), P(), P(),
    )
    out_specs = (P(None, seq), rows, rows, rows, toks)
    return jax.shard_map(
        on_device, mesh=grid, in_specs=in_specs, out_specs=out_specs, check_vma=False
    )
```

```python
import jax
import jax.numpy as jnp
from jax import lax
from jax.experimental import pallas as pl
from jax.experimental.pallas import tpu as pltpu
from jax.sharding import Mesh, PartitionSpec as P

norm_epsilon = 1e-06
MESH = pl.DeviceIdType.MESH
AXES_SEQ = ("x", "c")
AXES_EXPERT = ("z", "y")

D = 6144
W_COLS = 768
UNITS = 576
H_MAIN = 512
N_IN = 1152
N_ALL = 1728
U_PAD = 640
TOK = 16
CAP = 80
HALF = 3072
BLOCK, HEAD = 256, 128
D_EXT = D + 128


def kernel(
    tok, moe, router, route, gate_w, up_w, down_w, qr, kr, vr, pr, rate, gain,
    roll_lp, train_lp, adv, low, high,
    obj, gh, gq, gk, gv,
    coef, coef_tok, route_tok, grd, info, gates, logit,
    wbuf, zx, zg, zi, xa, ga, pre, ugr, ggu, dxs, yh, yfp, yfm, cz, zr, zl, psel,
    f_own, f_sib, f_chip, b_own, b_sib, b_chip, f_far, b_far, state, dk_part, dv_part,
    ssem, rsem, lsem, xss, xrs,
):
    x, c, z, y = (lax.axis_index(a) for a in ("x", "c", "z", "y"))
    xp, xm = (x + 1) % 4, (x + 3) % 4
    yp, ym, y2 = (y + 1) % 4, (y + 3) % 4, (y + 2) % 4
    zp, zm = (z + 1) % 8, (z + 7) % 8
    right = {"x": {"x": xp}, "y": {"y": yp}, "z": {"z": zp}}
    left = {"x": {"x": xm}, "y": {"y": ym}, "z": {"z": zm}}
    sib = {"c": 1 - c}
    me = 2 * x + c
    started = []

    def send(src, dst, dev):
        at = len(started)
        copy = pltpu.make_async_remote_copy(
            src_ref=src, dst_ref=dst, send_sem=ssem.at[at], recv_sem=rsem.at[at],
            device_id=dev, device_id_type=MESH,
        )
        copy.start()
        started.append(copy)
        return copy

    raw = [
        pltpu.make_async_copy(
            w.at[0, pl.ds(src, n)], wbuf.at[me, pl.ds(dst, n)], lsem.at[i]
        )
        for i, (w, src, dst, n) in enumerate((
            (gate_w, 0, 0, H_MAIN),
            (up_w, 0, H_MAIN, H_MAIN),
            (gate_w, H_MAIN, 2 * H_MAIN, UNITS - H_MAIN),
            (up_w, H_MAIN, H_MAIN + UNITS, UNITS - H_MAIN),
            (down_w, 0, N_IN, UNITS),
        ))
    ]
    for copy in raw:
        copy.start()
    barrier = pltpu.get_barrier_semaphore()
    peers = [right[a] for a in "xyz"] + [left[a] for a in "xyz"] + [sib]
    peers += [{"x": xp, "c": 1 - c}, {"x": xm, "c": 1 - c}, {"x": (x + 2) % 4}]
    peers += [{"x": (x + 2) % 4, "c": 1 - c}]
    for peer in peers:
        pl.semaphore_signal(barrier, inc=1, device_id=peer, device_id_type=MESH)
    pl.semaphore_wait(barrier, len(peers))

    col_a, col_b = pl.ds(0, HALF), pl.ds(HALF, HALF)
    zx[z] = tok[...]

    def z_own(src, dst, dev):
        return [[send(src.at[:, p], dst.at[z, :, p], dev) for p in (col_a, col_b)]]

    zxr = z_own(tok, zx, right["z"])
    zxl = z_own(tok, zx, left["z"])

    half = N_ALL // 2
    half_a, half_b = pl.ds(0, half), pl.ds(half, half)
    quarters_a = pl.ds(0, half // 2), pl.ds(half // 2, half // 2)
    quarters_b = pl.ds(half, half // 2), pl.ds(half + half // 2, half // 2)
    for copy in raw:
        copy.wait()
    wra = send(wbuf.at[me, half_a], wbuf.at[me, half_a], right["x"])
    wlb = send(wbuf.at[me, half_b], wbuf.at[me, half_b], left["x"])
    wrb = send(wbuf.at[me, half_b], wbuf.at[me, half_b], right["x"])
    wla = send(wbuf.at[me, half_a], wbuf.at[me, half_a], left["x"])
    ws = [send(wbuf.at[me], wbuf.at[me], sib)]

    f32, bf16 = jnp.float32, jnp.bfloat16
    nn, nt, tn = (((1,), (0,)), ((), ())), (((1,), (1,)), ((), ())), (((0,), (0,)), ((), ()))

    def mm(a, b, dims):
        return lax.dot_general(a, b, dims, preferred_element_type=f32)

    def parts_of(v):
        high = v.astype(bf16)
        return high, (v - high.astype(f32)).astype(bf16)

    def row_decay(h, sign, shift):
        row = lax.broadcasted_iota(jnp.int32, (BLOCK, HEAD), 0).astype(f32)
        return jnp.exp(-rate[h] * (sign * row + shift))

    def lanes(h):
        return pl.ds(pl.multiple_of(h * HEAD, HEAD), HEAD)

    def block_decay(h, blocks):
        return jnp.exp(jnp.full((HEAD, HEAD), -rate[h] * (BLOCK * blocks), f32))

    def summaries():
        @pl.loop(0, 4)
        def _(i):
            r, h = i // 2, i % 2
            v_high, v_low = parts_of(vr[r, :, lanes(h)].astype(f32) * row_decay(h, -1.0, BLOCK - 1.0))
            key = kr[r, :, lanes(h)]
            f_own[r, h] = mm(key, v_high, tn) + mm(key, v_low, tn)

    def chip_state(own_ref, sib_ref, chip_ref, near_is_own):
        for h in range(2):
            mine, other = own_ref[c, h], sib_ref[c, h]
            near = jnp.where(near_is_own, mine, other)
            far = jnp.where(near_is_own, other, mine)
            chip_ref[h] = near + block_decay(h, 1) * far

    def far_copy(chip_ref, far_ref, base, dx, cc, to):
        return pltpu.make_async_remote_copy(
            src_ref=chip_ref, dst_ref=far_ref.at[dx - 1, c],
            send_sem=xss.at[base + 2 * (dx - 1) + cc], recv_sem=xrs.at[base + 2 * (dx - 1) + c],
            device_id={"x": to, "c": cc}, device_id_type=MESH,
        )

    def far_send(chip_ref, far_ref, base, step, finish=False):
        for dx in (1, 2, 3):
            to = x + step * dx

            @pl.when(jnp.logical_and(to >= 0, to < 4))
            def _():
                for cc in (0, 1):
                    copy = far_copy(chip_ref, far_ref, base, dx, cc, to)
                    if finish:
                        copy.wait_send()
                    else:
                        copy.start()

    def far_state(chip_ref, far_ref, sib_ref, base, step, with_sib):
        for dx in (1, 2, 3):
            at = x - step * dx
            there = jnp.logical_and(at >= 0, at < 4)

            @pl.when(there)
            def _():
                for r in (0, 1):
                    pltpu.make_async_remote_copy(
                        src_ref=chip_ref, dst_ref=far_ref.at[dx - 1, r],
                        send_sem=xss.at[base + 2 * (dx - 1) + r],
                        recv_sem=xrs.at[base + 2 * (dx - 1) + r],
                        device_id={"x": (x + 1) % 4, "c": r}, device_id_type=MESH,
                    ).wait_recv()

            @pl.when(jnp.logical_not(there))
            def _():
                far_ref[dx - 1] = jnp.zeros_like(far_ref[dx - 1])

        for r in range(2):
            for h in range(2):
                two = block_decay(h, 2)
                far = far_ref[0, r, h] + two * (far_ref[1, r, h] + two * far_ref[2, r, h])
                near = sib_ref[r, h] + block_decay(h, 1) * far
                state[r, h] = jnp.where(with_sib, near, far)

    def attention_main(first, end):
        @pl.loop(first, end)
        def _(i):
            r, h = i // 2, i % 2
            query, key, value = qr[r, :, lanes(h)], kr[r, :, lanes(h)], vr[r, :, lanes(h)]
            at_i = lax.broadcasted_iota(jnp.int32, (BLOCK, BLOCK), 0)
            at_j = lax.broadcasted_iota(jnp.int32, (BLOCK, BLOCK), 1)
            apart = jnp.maximum(at_i - at_j, 0).astype(f32)
            within = jnp.where(at_i >= at_j, jnp.exp(-rate[h] * apart), 0.0)
            s_high, s_low = parts_of(mm(query, key, nt) * within)
            t_high, t_low = parts_of(state[r, h])
            lead = row_decay(h, 1.0, 1.0)
            attn = mm(s_high, value, nn) + mm(s_low, value, nn)
            attn = attn + lead * (mm(query, t_high, nn) + mm(query, t_low, nn))
            inverse = lax.rsqrt(jnp.mean(attn * attn, axis=1, keepdims=True) + norm_epsilon)
            scaled = gain[:, lanes(h)] * (coef[r] * pr[r, :, lanes(h)].astype(f32))
            along = jnp.mean(scaled * attn, axis=1, keepdims=True)
            grad = inverse * scaled - attn * (inverse * inverse * inverse * along)
            g_high, g_low = parts_of(grad)
            d_high, d_low = parts_of(grad * row_decay(h, 1.0, 0.0))
            b_own[r, h] = mm(query, d_high, tn) + mm(query, d_low, tn)
            p_high, p_low = parts_of((mm(g_high, value, nt) + mm(g_low, value, nt)) * within)
            dq = mm(p_high, key, nn) + mm(p_low, key, nn)
            dq = dq + lead * (mm(g_high, t_high, nt) + mm(g_low, t_high, nt) + mm(g_high, t_low, nt))
            gq[r, :, lanes(h)] = dq.astype(bf16)
            dk_part[r, :, lanes(h)] = mm(p_high, query, tn) + mm(p_low, query, tn)
            dv_part[r, :, lanes(h)] = (
                mm(s_high, g_high, tn) + mm(s_low, g_high, tn) + mm(s_high, g_low, tn)
            )

    def attention_last():
        @pl.loop(0, 4)
        def _(i):
            r, h = i // 2, i % 2
            key, value = kr[r, :, lanes(h)], vr[r, :, lanes(h)]
            t_high, t_low = parts_of(state[r, h])
            tail = row_decay(h, -1.0, float(BLOCK))
            dk = dk_part[r, :, lanes(h)] + tail * (mm(value, t_high, nt) + mm(value, t_low, nt))
            dv = dv_part[r, :, lanes(h)] + tail * (mm(key, t_high, nn) + mm(key, t_low, nn))
            gk[r, :, lanes(h)] = dk.astype(bf16)
            gv[r, :, lanes(h)] = dv.astype(bf16)

    lane = lax.broadcasted_iota(jnp.int32, (TOK, 128), 1)
    token = lax.broadcasted_iota(jnp.int32, (TOK, 128), 0)
    eye = lax.broadcasted_iota(jnp.int32, (128, 128), 0) == lax.broadcasted_iota(
        jnp.int32, (128, 128), 1
    )
    for r in range(2):
        for j in range(2):
            row = jnp.broadcast_to(route[r, j : j + 1, :].astype(f32), (8, 8))
            col = jnp.sum(jnp.where(eye[0:8, 0:8], row, 0.0), axis=1, keepdims=True)
            route_tok[j, 8 * r : 8 * r + 8, :] = jnp.broadcast_to(col, (8, 128))
    lane_f = lane.astype(f32)
    member = jnp.logical_or(lane_f == route_tok[0], lane_f == route_tok[1])
    t_row = lax.broadcasted_iota(jnp.int32, (TOK, TOK), 0)
    t_col = lax.broadcasted_iota(jnp.int32, (TOK, TOK), 1)
    ahead = jnp.logical_and(t_col < t_row, (t_col >= 8) == (t_row >= 8))
    rank = mm(ahead.astype(f32).astype(bf16), member.astype(f32).astype(bf16), nn)
    slot = rank + jnp.where(token >= 8, 6.0, 1.0) + (10 * z).astype(f32)
    slot = jnp.where(member, slot, 0.0)
    gates[...] = jnp.zeros_like(gates)
    gates[:, 0:4] = mm(tok[...], router[...], nt)
    weight = jnp.where(member, jnp.exp(gates[...]), 0.0)
    gate = weight / jnp.sum(weight, axis=1, keepdims=True)
    gates[...] = gate
    a_high, a_low = parts_of(slot + pltpu.roll(gate, 4, 1))
    place = (lane == token + TOK * z).astype(f32).astype(bf16)
    info[...] = (mm(a_high, place, tn) + mm(a_low, place, tn))[0:8]
    zi[z] = info[...]
    zir = [[send(info, zi.at[z], right["z"])]]
    zil = [[send(info, zi.at[z], left["z"])]]

    def z_hop(h, buf, rights, lefts, pieces):
        nr, nl = [], []
        for n, p in enumerate(pieces):
            rights[h - 1][n].wait_recv()
            if h < 4:
                at = (z + 8 - h) % 8
                nr.append(send(buf.at[at, :, p], buf.at[at, :, p], right["z"]))
            if h <= 3:
                lefts[h - 1][n].wait_recv()
                if h < 3:
                    at = (z + h) % 8
                    nl.append(send(buf.at[at, :, p], buf.at[at, :, p], left["z"]))
        rights.append(nr)
        lefts.append(nl)

    halves, whole = (col_a, col_b), (pl.ds(0, 128),)
    for h in range(1, 5):
        z_hop(h, zx, zxr, zxl, halves)
        z_hop(h, zi, zir, zil, whole)

    k = z // 2
    total = zi[0]
    for i in range(1, 8):
        total = total + zi[i]
    kind = lax.broadcasted_iota(jnp.int32, (8, 128), 0)
    slot_row = jnp.sum(jnp.where(kind == k, total, 0.0), axis=0, keepdims=True)
    gate_row = jnp.sum(jnp.where(kind == k + 4, total, 0.0), axis=0, keepdims=True)
    rows = lax.broadcasted_iota(jnp.int32, (CAP, 128), 0).astype(jnp.float32) + 1.0
    hot = (rows == jnp.broadcast_to(slot_row, (CAP, 128))).astype(jnp.float32)
    gate_slot = jnp.sum(hot * jnp.broadcast_to(gate_row, (CAP, 128)), axis=1, keepdims=True)
    psel[...] = hot.astype(jnp.bfloat16)

    def compact(buf, dst):
        @pl.loop(0, D // 512)
        def _(i):
            cols = pl.ds(pl.multiple_of(i * 512, 512), 512)
            block = buf[:, :, cols].reshape(8 * TOK, 512)
            dst[y, :, cols] = jnp.dot(
                psel[...], block, preferred_element_type=jnp.float32
            ).astype(jnp.bfloat16)

    def y_send(buf):
        ra = send(buf.at[y, :, col_a], buf.at[y, :, col_a], right["y"])
        lb = send(buf.at[y, :, col_b], buf.at[y, :, col_b], left["y"])
        rb = send(buf.at[y, :, col_b], buf.at[y, :, col_b], right["y"])
        la = send(buf.at[y, :, col_a], buf.at[y, :, col_a], left["y"])
        return ra, lb, rb, la

    def y_relay(buf, ra, lb):
        ra.wait_recv()
        fa = send(buf.at[ym, :, col_a], buf.at[ym, :, col_a], right["y"])
        lb.wait_recv()
        fb = send(buf.at[yp, :, col_b], buf.at[yp, :, col_b], left["y"])
        return fa, fb

    compact(zx, xa)
    yx = y_send(xa)

    ratio = jnp.exp(train_lp[...] - roll_lp[...])
    ratio = jnp.minimum(jnp.maximum(ratio, low[0]), high[0])
    coeff = -(ratio * adv[...]) / 2.0
    obj[...] = coeff * train_lp[...]
    for r in range(2):
        for part in range(2):
            row = jnp.broadcast_to(coeff[r : r + 1, 128 * part : 128 * part + 128], (128, 128))
            col = jnp.sum(jnp.where(eye, row, 0.0), axis=1, keepdims=True)
            coef[r, 128 * part : 128 * part + 128, :] = jnp.broadcast_to(col, (128, 128))
    here = pl.ds(pl.multiple_of(8 * (4 * z + y), 8), 8)
    for r in range(2):
        coef_tok[8 * r : 8 * r + 8, :] = coef[r, here, :]

    @pl.loop(0, D // 512)
    def _(i):
        cols = pl.ds(pl.multiple_of(i * 512, 512), 512)
        grad = moe[:, cols].astype(f32) * coef_tok[:, 0:1]
        grd[:, cols] = grad.astype(bf16)
        zg[z, :, cols] = grad.astype(bf16)

    zgr = z_own(grd, zg, right["z"])
    zgl = z_own(grd, zg, left["z"])
    pre[...] = jnp.zeros_like(pre)
    ugr[...] = jnp.zeros_like(ugr)
    summaries()
    fs = send(f_own, f_sib, sib)
    z_hop(1, zg, zgr, zgl, halves)
    s_xm, s_xp, s_x2 = 2 * xm + c, 2 * xp + c, 2 * ((x + 2) % 4) + c
    wra.wait_recv()
    wfa = [send(wbuf.at[s_xm, q], wbuf.at[s_xm, q], right["x"]) for q in quarters_a]
    ws.append(send(wbuf.at[s_xm, half_a], wbuf.at[s_xm, half_a], sib))
    wlb.wait_recv()
    wfb = [send(wbuf.at[s_xp, q], wbuf.at[s_xp, q], left["x"]) for q in quarters_b]
    ws.append(send(wbuf.at[s_xp, half_b], wbuf.at[s_xp, half_b], sib))
    fs.wait_recv()
    chip_state(f_own, f_sib, f_chip, c == 1)
    far_send(f_chip, f_far, 0, 1)
    z_hop(2, zg, zgr, zgl, halves)
    z_hop(3, zg, zgr, zgl, halves)
    yxf = y_relay(xa, yx[0], yx[1])
    z_hop(4, zg, zgr, zgl, halves)
    compact(zg, ga)
    yg = y_send(ga)
    yx[2].wait_recv()
    yx[3].wait_recv()
    wrb.wait_recv()
    ws.append(send(wbuf.at[s_xm, half_b], wbuf.at[s_xm, half_b], sib))
    wla.wait_recv()
    ws.append(send(wbuf.at[s_xp, half_a], wbuf.at[s_xp, half_a], sib))
    yxf[0].wait_recv()
    yxf[1].wait_recv()

    def add_in(shard):
        cols = pl.ds(pl.multiple_of(shard * W_COLS, W_COLS), W_COLS)
        left_op = xa[:, :, cols].reshape(4 * CAP, W_COLS)
        for at, wide in ((0, 256), (256, 256), (512, 256), (768, 256), (1024, 128)):
            pre[:, at : at + wide] += mm(left_op, wbuf[shard, at : at + wide, :], nt)

    def add_out(shard):
        cols = pl.ds(pl.multiple_of(shard * W_COLS, W_COLS), W_COLS)
        left_op = ga[:, :, cols].reshape(4 * CAP, W_COLS)
        for at, wide in ((0, 256), (256, 256), (512, 64)):
            ugr[:, at : at + wide] += mm(left_op, wbuf[shard, N_IN + at : N_IN + at + wide, :], nt)

    for copy in ws:
        copy.wait_recv()
    ws_done = len(ws)

    @pl.loop(0, 6)
    def _(i):
        add_in((2 * (x + 3) + i) % 8)

    ygf = y_relay(ga, yg[0], yg[1])
    yg[2].wait_recv()
    yg[3].wait_recv()
    ygf[0].wait_recv()
    ygf[1].wait_recv()

    @pl.loop(0, 6)
    def _(i):
        add_out((2 * (x + 3) + i) % 8)

    for n in range(2):
        wfa[n].wait_recv()
        ws.append(send(wbuf.at[s_x2, quarters_a[n]], wbuf.at[s_x2, quarters_a[n]], sib))
        wfb[n].wait_recv()
        ws.append(send(wbuf.at[s_x2, quarters_b[n]], wbuf.at[s_x2, quarters_b[n]], sib))
    add_in(s_x2)
    add_out(s_x2)
    for copy in ws[ws_done:]:
        copy.wait_recv()
    s_x2o = 2 * ((x + 2) % 4) + 1 - c
    add_in(s_x2o)
    add_out(s_x2o)

    def grads(gate, up, unit):
        sig = jax.nn.sigmoid(gate)
        act = gate * sig
        up_grad = unit * act
        gate_grad = unit * up * sig * (1.0 + gate * (1.0 - sig))
        score = jnp.sum(act * up * unit, axis=1, keepdims=True)
        return gate_grad, up_grad, score

    @pl.loop(0, 4)
    def _(b):
        @pl.loop(0, CAP // TOK)
        def _(i):
            at = pl.multiple_of(b * CAP + i * TOK, TOK)
            r = pl.ds(at, TOK)
            gg, ug, s1 = grads(pre[r, 0:512], pre[r, 512:1024], ugr[r, 0:512])
            tail = pre[r, 1024:1152]
            ggt, ugt, s2 = grads(tail, pltpu.roll(tail, 64, 1), ugr[r, 512:640])
            ggu[r, 0:512] = gg.astype(jnp.bfloat16)
            ggu[r, 512:1024] = ug.astype(jnp.bfloat16)
            ggu[r, 1024:1152] = (ggt + pltpu.roll(ugt, 64, 1)).astype(jnp.bfloat16)
            score = jnp.where(lane == k, jnp.broadcast_to(s1 + s2, (TOK, 128)), 0.0)
            dxs[b, pl.ds(pl.multiple_of(i * TOK, TOK), TOK), D:D_EXT] = score.astype(jnp.bfloat16)

    def to_dx(shard):
        for at in (0, 256, 512):
            cols = pl.ds(pl.multiple_of(shard * W_COLS + at, 256), 256)
            part = mm(ggu[...], wbuf[shard, 0:N_IN, at : at + 256], nn)
            dxs[:, :, cols] = part.astype(bf16).reshape(4, CAP, 256)

    shards = [(6, 8), (4, 6), (2, 4), (0, 2)]
    group_a, group_b, group = [], [], []
    for lo, hi in shards:
        first, end = lo * W_COLS, D_EXT if hi == 8 else hi * W_COLS
        middle = (lo + hi) * W_COLS // 2
        group_a.append(pl.ds(first, middle - first))
        group_b.append(pl.ds(middle, end - middle))
        group.append(pl.ds(first, end - first))
    far_a, far_b, to_left, to_right, last_a, last_b = {}, {}, {}, {}, {}, {}

    def dx_group(g):
        @pl.loop(*shards[g])
        def _(i):
            to_dx(i)

        a, b = group_a[g], group_b[g]
        far_a[g] = send(dxs.at[y2, :, a], yh.at[:, a], right["y"])
        far_b[g] = send(dxs.at[y2, :, b], yh.at[:, b], left["y"])

    def direct(g):
        a, b = group_a[g], group_b[g]
        to_right[g] = send(dxs.at[yp, :, b], yfm.at[:, b], right["y"])
        to_left[g] = send(dxs.at[ym, :, a], yfp.at[:, a], left["y"])

    def add_cols(dst, cols):
        @pl.loop(0, cols.size // 128)
        def _(i):
            at = pl.ds(pl.multiple_of(cols.start + i * 128, 128), 128)
            dst[:, at] = (dst[:, at].astype(f32) + yh[:, at].astype(f32)).astype(bf16)

    def relayed(g):
        a, b = group_a[g], group_b[g]
        far_a[g].wait_recv()
        add_cols(dxs.at[yp], a)
        last_a[g] = send(dxs.at[yp, :, a], yfm.at[:, a], right["y"])
        far_b[g].wait_recv()
        add_cols(dxs.at[ym], b)
        last_b[g] = send(dxs.at[ym, :, b], yfp.at[:, b], left["y"])

    def spread(cols, wide, gated):
        part = dxs[y, :, cols].astype(f32) + yfp[:, cols].astype(f32) + yfm[:, cols].astype(f32)
        if gated:
            part = part * gate_slot
        cz[:, :, cols] = mm(psel[...], part.astype(bf16), tn).astype(bf16).reshape(8, TOK, wide)

    z_right, z_left = {}, {}

    def y_end(g):
        for copies in (to_left, to_right, last_a, last_b):
            copies[g].wait_recv()

        @pl.loop(2 * shards[g][0], 2 * shards[g][1])
        def _(i):
            spread(pl.ds(pl.multiple_of(i * 384, 128), 384), 384, True)

        if g == 0:
            spread(pl.ds(D, 128), 128, False)
        z_right[g] = [send(cz.at[(z + 4) % 8, :, group[g]], zr.at[0, :, group[g]], right["z"])]
        z_left[g] = [send(cz.at[(z + 5) % 8, :, group[g]], zl.at[0, :, group[g]], left["z"])]

    def z_add(at, src, cols):
        cz[at, :, cols] = (cz[at, :, cols].astype(f32) + src[:, cols].astype(f32)).astype(bf16)

    def z_step(g, h):
        cols = group[g]
        at = (z + 4 - h) % 8
        z_right[g][h - 1].wait_recv()
        z_add(at, zr.at[h - 1], cols)
        z_right[g].append(send(cz.at[at, :, cols], zr.at[h, :, cols], right["z"]))
        if h < 3:
            at = (z + 5 + h) % 8
            z_left[g][h - 1].wait_recv()
            z_add(at, zl.at[h - 1], cols)
            z_left[g].append(send(cz.at[at, :, cols], zl.at[h, :, cols], left["z"]))

    def span_of(g):
        return (shards[g][1] - shards[g][0]) * W_COLS

    def z_end(g):
        cols = group[g]
        z_left[g][2].wait_recv()
        z_right[g][3].wait_recv()
        whole_sum = (
            cz[z, :, cols].astype(f32) + zr[3, :, cols].astype(f32) + zl[2, :, cols].astype(f32)
        )
        if g == 0:
            score, share = whole_sum[:, span_of(g) :], gates[...]
            logit[...] = share * (score - jnp.sum(share * score, axis=1, keepdims=True))
        l_high, l_low = parts_of(logit[:, 0:4])
        cols = pl.ds(cols.start, span_of(g))
        to_hidden = mm(l_high, router[:, cols], nn) + mm(l_low, router[:, cols], nn)
        gh[:, cols] = (whole_sum[:, : span_of(g)] + to_hidden).astype(bf16)

    dx_group(0)
    direct(0)
    dx_group(1)
    relayed(0)
    direct(1)
    dx_group(2)
    relayed(1)
    direct(2)
    dx_group(3)
    far_state(f_chip, f_far, f_sib, 0, 1, c == 1)
    attention_main(0, 1)
    y_end(0)
    attention_main(1, 2)
    z_step(0, 1)
    relayed(2)
    direct(3)
    attention_main(2, 3)
    z_step(0, 2)
    y_end(1)
    attention_main(3, 4)
    bs = send(b_own, b_sib, sib)
    z_step(0, 3)
    z_step(1, 1)
    relayed(3)
    bs.wait_recv()
    chip_state(b_own, b_sib, b_chip, c == 0)
    far_send(b_chip, b_far, 6, -1)
    z_end(0)
    z_step(1, 2)
    y_end(2)
    z_step(1, 3)
    z_step(2, 1)
    z_end(1)
    z_step(2, 2)
    y_end(3)
    z_step(2, 3)
    z_step(3, 1)
    z_end(2)
    z_step(3, 2)
    z_step(3, 3)
    far_state(b_chip, b_far, b_sib, 6, -1, c == 0)
    attention_last()
    z_end(3)

    for copy in started:
        copy.wait_send()
    far_send(f_chip, f_far, 0, 1, finish=True)
    far_send(b_chip, b_far, 6, -1, finish=True)


def copy_out(*refs):
    n = len(refs) // 3
    sem = refs[-1]
    ins, outs, bufs = refs[:n], refs[n : 2 * n], refs[2 * n : 3 * n]
    arrive = [pltpu.make_async_copy(ins[i], bufs[i], sem.at[i]) for i in range(n)]
    leave = [pltpu.make_async_copy(bufs[i], outs[i], sem.at[n + i]) for i in range(n)]
    for copy in arrive:
        copy.start()
    for i in range(n):
        arrive[i].wait()
        leave[i].start()
    for copy in leave:
        copy.wait()


def results(*arrays):
    n = len(arrays)
    where = pl.BlockSpec(memory_space=pl.ANY)
    return pl.pallas_call(
        copy_out,
        out_shape=[jax.ShapeDtypeStruct(a.shape, a.dtype) for a in arrays],
        in_specs=[where] * n,
        out_specs=[where] * n,
        scratch_shapes=[pltpu.VMEM(a.shape, a.dtype) for a in arrays]
        + [pltpu.SemaphoreType.DMA((2 * n,))],
        name="results",
    )(*arrays)


def all_blocks(*operands):
    bf16, f32 = jnp.bfloat16, jnp.float32
    vmem, smem = (pl.BlockSpec(memory_space=m) for m in (pltpu.VMEM, pltpu.SMEM))
    hbm = pl.BlockSpec(memory_space=pl.ANY)
    n_copies = 118
    grads = jax.ShapeDtypeStruct((2, BLOCK, 2 * HEAD), bf16)
    states = pltpu.VMEM((2, 2, HEAD, HEAD), f32)
    return pl.pallas_call(
        kernel,
        out_shape=[
            jax.ShapeDtypeStruct((2, BLOCK), f32), jax.ShapeDtypeStruct((TOK, D), bf16),
            grads, grads, grads,
        ],
        in_specs=[vmem] * 4 + [hbm] * 3 + [vmem] * 4 + [smem] + [vmem] * 4 + [smem] * 2,
        out_specs=[vmem] * 5,
        scratch_shapes=[
            pltpu.VMEM((2, BLOCK, 128), f32),
            pltpu.VMEM((TOK, 128), f32),
            pltpu.VMEM((2, TOK, 128), f32),
            pltpu.VMEM((TOK, D), bf16),
            pltpu.VMEM((8, 128), f32),
            pltpu.VMEM((TOK, 128), f32),
            pltpu.VMEM((TOK, 128), f32),
            pltpu.VMEM((8, N_ALL, W_COLS), bf16),
            pltpu.VMEM((8, TOK, D), bf16),
            pltpu.VMEM((8, TOK, D), bf16),
            pltpu.VMEM((8, 8, 128), f32),
            pltpu.VMEM((4, CAP, D), bf16),
            pltpu.VMEM((4, CAP, D), bf16),
            pltpu.VMEM((4 * CAP, N_IN), f32),
            pltpu.VMEM((4 * CAP, U_PAD), f32),
            pltpu.VMEM((4 * CAP, N_IN), bf16),
            pltpu.VMEM((4, CAP, D_EXT), bf16),
            pltpu.VMEM((CAP, D_EXT), bf16),
            pltpu.VMEM((CAP, D_EXT), bf16),
            pltpu.VMEM((CAP, D_EXT), bf16),
            pltpu.VMEM((8, TOK, D_EXT), bf16),
            pltpu.VMEM((4, TOK, D_EXT), bf16),
            pltpu.VMEM((3, TOK, D_EXT), bf16),
            pltpu.VMEM((CAP, 128), bf16),
            states, states, pltpu.VMEM((2, HEAD, HEAD), f32),
            states, states, pltpu.VMEM((2, HEAD, HEAD), f32),
            pltpu.VMEM((3, 2, 2, HEAD, HEAD), f32),
            pltpu.VMEM((3, 2, 2, HEAD, HEAD), f32),
            states,
            pltpu.VMEM((2, BLOCK, 2 * HEAD), f32),
            pltpu.VMEM((2, BLOCK, 2 * HEAD), f32),
            pltpu.SemaphoreType.DMA((n_copies,)),
            pltpu.SemaphoreType.DMA((n_copies,)),
            pltpu.SemaphoreType.DMA((5,)),
            pltpu.SemaphoreType.DMA((12,)),
            pltpu.SemaphoreType.DMA((12,)),
        ],
        compiler_params=pltpu.CompilerParams(
            collective_id=0, has_side_effects=True, vmem_limit_bytes=64 * 1024 * 1024 - 65536
        ),
        cost_estimate=pl.CostEstimate(
            flops=12 * 10**9, bytes_accessed=40 * 10**6, transcendentals=200000
        ),
        name="all_blocks",
    )(*operands)


def on_device(
    queries,
    key_rows,
    value_rows,
    decay_rate,
    norm_gain,
    attn_probe,
    hidden_in,
    moe_probe,
    router_weight,
    routes,
    gate_weight,
    up_weight,
    down_weight,
    rollout_logprob,
    trainer_logprob,
    advantage,
    clip_low,
    clip_high,
):
    rollouts, positions, width = hidden_in.shape
    objective, *rest = all_blocks(
        hidden_in.reshape(TOK, width), moe_probe.reshape(TOK, width), router_weight.T,
        routes.transpose(0, 2, 1), *(w.transpose(0, 2, 1) for w in (gate_weight, up_weight, down_weight)),
        queries, key_rows, value_rows, attn_probe, decay_rate, norm_gain.reshape(1, -1),
        rollout_logprob, trainer_logprob, advantage, clip_low, clip_high,
    )
    objective, grad_hidden, *grads = results(objective, *rest)
    return (objective, *grads, grad_hidden.reshape(rollouts, positions, width))


def solution(mesh):
    grid = Mesh(mesh.devices.reshape(4, 2, 8, 4), ("x", "c", "z", "y"))
    seq, exp = AXES_SEQ, AXES_EXPERT
    rows = P(None, seq, exp)
    toks = P(None, seq + exp, None)
    wts = P(exp, seq, None)
    in_specs = (
        rows, rows, rows, P(exp), P(exp), rows, toks, toks, P(), toks, wts, wts, wts,
        P(None, seq), P(None, seq), P(None, seq), P(), P(),
    )
    out_specs = (P(None, seq), rows, rows, rows, toks)
    return jax.shard_map(
        on_device, mesh=grid, in_specs=in_specs, out_specs=out_specs, check_vma=False
    )
```
